32 devices in a mesh: east: 8 (over z, core), north: 4 (over y, x).
Axes of the slice: x: 2, y: 2, z: 4, core: 2. Of those that a mesh axis runs over, the one named last changes fastest.
Arguments:
- increment: float32 [16, 512, 512], P(None, 'east', 'north'), may hold values from -6 to 6
- widths_fine: int32 [512, 512], P('east', 'north'), may hold values from 1 to 8
- widths_half: int32 [256, 256], P('east', 'north'), may hold values from 1 to 8
- widths_quarter: int32 [128, 128], P('east', 'north'), may hold values from 1 to 8
- widths_eighth: int32 [64, 64], P('east', 'north'), may hold values from 1 to 8
- amplitude_fine: float32 [512, 512], P('east', 'north'), may hold values from 0.5 to 2
- amplitude_half: float32 [256, 256], P('east', 'north'), may hold values from 0.5 to 2
- amplitude_quarter: float32 [128, 128], P('east', 'north'), may hold values from 0.5 to 2
- amplitude_eighth: float32 [64, 64], P('east', 'north'), may hold values from 0.5 to 2
- vertical: float32 [4, 16, 16], replicated, may hold values from -1.5 to 1.5
Outputs:
- filtered: float32 [16, 512, 512], P(None, 'east', 'north')
The draws below stay inside these ranges and needn't reach their ends.
Inputs may be any that keep to these rules, and one draw needn't show every extreme that they name: `widths_fine`: half-widths in cells. `widths_half`: half-widths in cells. `widths_quarter`: half-widths in cells. `widths_eighth`: half-widths in cells.
All inputs are finite; a program needn't handle non-finite values.
Results may differ from the reference program's by a relative error of at most 0.00011.
Values sent between devices are 32-bit elements; how exact they have to be, the bound alone decides.
No kernel may reach another device: no remote copies, remote signals or barrier semaphores. Data moves between devices by JAX's collectives and lax.ppermute only.
A program may use at most 64 MiB of HBM per device.

```python
import math
import jax
import jax.numpy as jnp
from jax import lax

NZ = 16
HMAX = 8
LEVELS = 4
NE = 512
NN = 512


def with_ends(drawn, key, low, largest):
    longest = drawn.shape.index(max(drawn.shape))
    spots = []
    for shift in (0, 1):
        where = [jax.random.randint(jax.random.fold_in(key, axis), (), 0, length) for axis, length in enumerate(drawn.shape)]
        where[longest] = (where[longest] + shift) % drawn.shape[longest]
        spots.append(tuple(where))
    return drawn.at[spots[0]].set(low).at[spots[1]].set(largest)


def block_levels(rng, dims, split, least, top_value):
    def one(axis_at, blocks):
        draws = jax.random.uniform(jax.random.fold_in(jax.random.fold_in(rng, 6), axis_at), (blocks,), jnp.float32, least / len(split), top_value / len(split))
        return jnp.repeat(jnp.exp(draws), dims[axis_at] // blocks).reshape((-1,) + (1,) * (len(dims) - axis_at - 1))

    loudness = one(*split[0])
    for cut in split[1:]:
        loudness = loudness * one(*cut)
    return loudness


def centred(key, dims, scale, bound, split=(), held_as=jnp.bfloat16):
    array = scale * jax.random.normal(key, dims, jnp.float32)
    if split:
        array = array * block_levels(key, dims, split, -0.22, 0.18)
    return jnp.clip(array, -bound, bound).astype(held_as)


def setup_inputs(seed: int = 0) -> dict:
    key_of = jax.random.split(jax.random.key(seed), 11)
    increment = centred(key_of[0], (NZ, NE, NN), 1.0, 6.0, ((1, 8), (2, 4)), jnp.float32)
    widths_fine = with_ends(jax.random.randint(key_of[1], (NE, NN), 1, HMAX + 1), jax.random.fold_in(key_of[1], 1), 1, HMAX).astype(jnp.int32)
    widths_half = with_ends(jax.random.randint(key_of[2], (NE // 2, NN // 2), 1, HMAX + 1), jax.random.fold_in(key_of[2], 1), 1, HMAX).astype(jnp.int32)
    widths_quarter = with_ends(jax.random.randint(key_of[3], (NE // 4, NN // 4), 1, HMAX + 1), jax.random.fold_in(key_of[3], 1), 1, HMAX).astype(jnp.int32)
    widths_eighth = with_ends(jax.random.randint(key_of[4], (NE // 8, NN // 8), 1, HMAX + 1), jax.random.fold_in(key_of[4], 1), 1, HMAX).astype(jnp.int32)
    amplitude_fine = jnp.clip(jnp.exp(math.log(2.0) - 1.3862944 * jax.random.uniform(key_of[5], (NE, NN), jnp.float32) ** block_levels(key_of[5], (NE, NN), ((0, 8), (1, 4)), -0.2, 0.2)), 0.5, 2.0)
    amplitude_half = jnp.clip(jnp.exp(math.log(2.0) - 1.3862944 * jax.random.uniform(key_of[6], (NE // 2, NN // 2), jnp.float32) ** block_levels(key_of[6], (NE // 2, NN // 2), ((0, 8), (1, 4)), -0.2, 0.2)), 0.5, 2.0)
    amplitude_quarter = jnp.clip(jnp.exp(math.log(2.0) - 1.3862944 * jax.random.uniform(key_of[7], (NE // 4, NN // 4), jnp.float32) ** block_levels(key_of[7], (NE // 4, NN // 4), ((0, 8), (1, 4)), -0.2, 0.2)), 0.5, 2.0)
    amplitude_eighth = jnp.clip(jnp.exp(math.log(2.0) - 1.3862944 * jax.random.uniform(key_of[8], (NE // 8, NN // 8), jnp.float32) ** block_levels(key_of[8], (NE // 8, NN // 8), ((0, 8), (1, 4)), -0.2, 0.2)), 0.5, 2.0)
    vertical = centred(key_of[9], (LEVELS, NZ, NZ), NZ ** -0.5, 1.5, (), jnp.float32)
    return dict(increment=increment, widths_fine=widths_fine, widths_half=widths_half, widths_quarter=widths_quarter, widths_eighth=widths_eighth, amplitude_fine=amplitude_fine, amplitude_half=amplitude_half, amplitude_quarter=amplitude_quarter, amplitude_eighth=amplitude_eighth, vertical=vertical)


def beta_taps(widths):
    grown = widths.astype(jnp.float32) + 1.0
    offsets = jnp.arange(-HMAX, HMAX + 1).astype(jnp.float32)
    ratios = offsets[:, None, None] / grown[None]
    profile = jnp.square(jnp.maximum(1.0 - ratios * ratios, 0.0))
    return profile / jnp.sum(profile, axis=0, keepdims=True)


def east_pass(padded, factors):
    row_count = factors.shape[1]
    running = factors[0][None] * padded[:, 0:row_count, :]
    for offset in range(1, factors.shape[0]):
        running = running + factors[offset][None] * padded[:, offset:offset + row_count, :]
    return running


def north_pass(padded, factors):
    col_count = factors.shape[2]
    running = factors[0][None] * padded[:, :, 0:col_count]
    for offset in range(1, factors.shape[0]):
        running = running + factors[offset][None] * padded[:, :, offset:offset + col_count]
    return running


def restrict(padded):
    row_count = padded.shape[1] - 2
    half_done = 0.375 * (padded[:, 1:row_count + 1:2, :] + padded[:, 2:row_count + 2:2, :]) + 0.125 * (padded[:, 0:row_count:2, :] + padded[:, 3:row_count + 2:2, :])
    col_count = padded.shape[2] - 2
    return 0.375 * (half_done[:, :, 1:col_count + 1:2] + half_done[:, :, 2:col_count + 2:2]) + 0.125 * (half_done[:, :, 0:col_count:2] + half_done[:, :, 3:col_count + 2:2])


def prolong(padded):
    layers = padded.shape[0]
    coarse_rows = padded.shape[1] - 2
    coarse_cols = padded.shape[2] - 2
    middle = padded[:, 1:coarse_rows + 1, :]
    even_rows = 0.75 * middle + 0.25 * padded[:, 0:coarse_rows, :]
    odd_rows = 0.75 * middle + 0.25 * padded[:, 2:coarse_rows + 2, :]
    stacked = jnp.stack([even_rows, odd_rows], axis=2).reshape(layers, 2 * coarse_rows, coarse_cols + 2)
    centre = stacked[:, :, 1:coarse_cols + 1]
    even_cols = 0.75 * centre + 0.25 * stacked[:, :, 0:coarse_cols]
    odd_cols = 0.75 * centre + 0.25 * stacked[:, :, 2:coarse_cols + 2]
    return jnp.stack([even_cols, odd_cols], axis=3).reshape(layers, 2 * coarse_rows, 2 * coarse_cols)


def pad_one(source):
    return jnp.pad(source, ((0, 0), (1, 1), (1, 1)))


def filter_level(source, widths, amplitude, mixing, generation):
    factors = beta_taps(widths)
    padded = jnp.pad(source, ((0, 0), (HMAX, HMAX), (0, 0)))
    eastward = east_pass(padded, factors)
    widened = jnp.pad(eastward, ((0, 0), (0, 0), (HMAX, HMAX)))
    northward = north_pass(widened, factors)
    mixed = jnp.einsum("ab,bxy->axy", mixing, northward, precision=lax.Precision.HIGHEST)
    return (4.0 ** generation) * amplitude[None] * mixed


def reference(increment, widths_fine, widths_half, widths_quarter, widths_eighth, amplitude_fine, amplitude_half, amplitude_quarter, amplitude_eighth, vertical):
    sources = [increment]
    for generation in range(3):
        sources.append(restrict(pad_one(sources[-1])))
    width_list = [widths_fine, widths_half, widths_quarter, widths_eighth]
    gain_list = [amplitude_fine, amplitude_half, amplitude_quarter, amplitude_eighth]
    result = filter_level(sources[3], width_list[3], gain_list[3], vertical[3], 3)
    for generation in (2, 1, 0):
        result = filter_level(sources[generation], width_list[generation], gain_list[generation], vertical[generation], generation) + prolong(pad_one(result))
    return result
```

```python
import functools

import jax
import jax.numpy as jnp
import numpy as np
from jax import lax
from jax.experimental import pallas as pl
from jax.experimental.pallas import tpu as pltpu
from jax.sharding import PartitionSpec as P

H = 8
LANES = 128
LEVELS = 3
F32 = jnp.float32
BF16 = jnp.bfloat16
SLOT = H + 2
PER_TILE = LANES // SLOT


def tables(rows, cols):
    bases, at = [], H
    for l in range(1, LEVELS + 1):
        bases.append(at)
        at += (cols >> l) + 2
    assert at <= LANES and cols == LANES
    down = np.zeros((4, cols, LANES), np.float32)
    for variant in range(4):
        current = np.eye(cols)
        low = 0
        for l in range(1, LEVELS + 1):
            m = cols >> l
            step = np.zeros((current.shape[1], m + 2))
            for j in range(-1, m + 1):
                for f, w in ((2 * j, 0.375), (2 * j + 1, 0.375), (2 * j - 1, 0.125), (2 * j + 2, 0.125)):
                    if 0 <= f - low < current.shape[1]:
                        step[f - low, j + 1] += w
            current = current @ step
            if variant & 1:
                current[:, 0] = 0
            if variant & 2:
                current[:, -1] = 0
            low = -1
            down[variant, :, bases[l - 1] : bases[l - 1] + m + 2] = current
    up = np.zeros((LEVELS + 1, LANES, LANES), np.float32)
    for l in range(LEVELS):
        m = cols >> l
        for f in range(-1, m + 1) if l else range(m):
            j = f // 2
            out = f + H + 1 if l else f
            up[l, j + H + 1, out] += 0.75
            up[l, j + (1 if f % 2 else -1) + H + 1, out] += 0.25
    for z in range(16):
        for i in range(8):
            j = i // 2 + 1
            up[LEVELS, z * 8 + i, j * 16 + z] += 0.75
            up[LEVELS, z * 8 + i, (j + (1 if i % 2 else -1)) * 16 + z] += 0.25
    for t in (down, up):
        assert (t == t.astype(jnp.bfloat16).astype(np.float32)).all()
    return bases, down.astype(jnp.bfloat16), up.astype(jnp.bfloat16)


def split(x):
    high = x.astype(BF16)
    return high, (x - high.astype(F32)).astype(BF16)


def mm(a, b):
    return jnp.dot(a, b, preferred_element_type=F32)


def dot_exact(x, weights):
    high, low = split(x)
    return mm(high, weights) + mm(low, weights)


def lanes_of(rows):
    return lax.broadcasted_iota(jnp.int32, (rows, LANES), 1)


def roll(x, shift):
    shift %= LANES
    return pltpu.roll(x, shift, 1) if shift else x


def taps(widths):
    grown = widths + 1.0
    inverse = 1.0 / (grown * grown)
    profile = [jnp.square(jnp.maximum(1.0 - float(k * k) * inverse, 0.0)) for k in range(1, H + 1)]
    total = profile[0]
    for p in profile[1:]:
        total = total + p
    scale = 1.0 / (1.0 + 2.0 * total)
    return [scale] + [p * scale for p in profile]


def prepare(geo, inc, *refs):
    widths, gains = refs[:LEVELS], refs[LEVELS : 2 * LEVELS]
    table, field, *rest = refs[2 * LEVELS :]
    coarse, (send_a, send_b, send_c, send_d, half) = rest[:LEVELS], rest[LEVELS:]
    Z, R, M, bases = geo["Z"], geo["R"], geo["M"], geo["bases"]
    e, n = lax.axis_index("east"), lax.axis_index("north")
    has_low, has_high = e > 0, e < geo["E"] - 1
    even = e % 2 == 0
    flat = field.reshape(R * Z, M)
    for z in range(Z):
        flat[pl.ds(z, R, stride=Z), :] = inc[z]
    variant = (n == 0).astype(jnp.int32) + 2 * (n == geo["N"] - 1).astype(jnp.int32)
    weights = table[variant]
    half_flat = half.reshape(R * Z, M)
    chunk = R * Z // 4
    for c in range(4):
        half_flat[pl.ds(c * chunk, chunk), :] = dot_exact(flat[pl.ds(c * chunk, chunk), :], weights)
    source, low, top = half, 0, R
    for l in range(1, LEVELS + 1):
        r, out = R >> l, coarse[l - 1]

        def get(i, source=source, low=low, top=top):
            return source[i - low] if low <= i < top else None

        for j in range(-1, r + 1):
            total = None
            for pair, w in (((2 * j, 2 * j + 1), 0.375), ((2 * j - 1, 2 * j + 2), 0.125)):
                terms = [t for t in (get(i) for i in pair) if t is not None]
                if terms:
                    part = w * functools.reduce(jnp.add, terms)
                    total = part if total is None else total + part
            if j == -1:
                total = jnp.where(has_low, total, 0.0)
            if j == r:
                total = jnp.where(has_high, total, 0.0)
            out[j + 1] = total
        source, low, top = out, -1, r + 1
    start = R - H
    send_a[0:H] = field[pl.ds(jnp.where(even, start, 0), H)]
    send_b[0:H] = field[pl.ds(jnp.where(even, 0, start), H)]
    lane = lanes_of(Z)
    for i in range(SLOT):
        def merged(picks):
            out = coarse[LEVELS - 1][picks[LEVELS - 1]]
            for l in range(LEVELS - 1, 0, -1):
                out = jnp.where(lane < bases[l], coarse[l - 1][picks[l - 1]], out)
            return out

        lower = merged([i] * LEVELS)
        upper = merged([(R >> l) - H + i for l in range(1, LEVELS + 1)])
        send_a[H + i] = jnp.where(even, upper, lower)
        send_b[H + i] = jnp.where(even, lower, upper)
    last = H + SLOT
    send_a[last] = jnp.zeros((Z, LANES), F32)
    send_b[last] = jnp.zeros((Z, LANES), F32)
    for j, ref in enumerate((*widths, *gains)):
        r, m = ref.shape
        lower = ref[pl.ds(0, 1), :].astype(F32)
        upper = ref[pl.ds(r - 1, 1), :].astype(F32)
        send_a[last, pl.ds(j, 1), pl.ds(0, m)] = jnp.where(even, upper, lower)
        send_b[last, pl.ds(j, 1), pl.ds(0, m)] = jnp.where(even, lower, upper)
    r = R >> LEVELS
    forward = (e // 2) % 2 == 0
    for i in range(2):
        lower, upper = coarse[LEVELS - 1][i], coarse[LEVELS - 1][r + i]
        send_c[i] = jnp.where(forward, upper, lower)
        send_d[i] = jnp.where(forward, lower, upper)


def east_rows(source, factors, out, count, block, factor_at=0):
    def step(b, carry):
        x0 = b * block
        rows = [source[x0 + i] for i in range(block + 2 * H)]
        for i in range(block):
            def factor(k):
                return factors[k, pl.ds(x0 + i + factor_at, 1), :]

            total = factor(0) * rows[i + H]
            for k in range(1, H + 1):
                total = total + factor(k) * (rows[i + H + k] + rows[i + H - k])
            out[x0 + i] = total
        return carry

    lax.fori_loop(0, count // block, step, 0)


def middle(geo, *refs):
    Z, R, M, bases = geo["Z"], geo["R"], geo["M"], geo["bases"]
    it = iter(refs)
    take = lambda count: [next(it) for _ in range(count)]
    (field,) = take(1)
    coarse = take(LEVELS)
    got_a, got_b, got_c, got_d, widths0 = take(5)
    widths, gains = take(LEVELS), take(LEVELS)
    eastward, factors = take(2)
    joined = take(LEVELS)
    send_x, send_y = take(2)
    wide, gain = take(LEVELS), take(LEVELS)
    (full,) = take(1)
    e, n = lax.axis_index("east"), lax.axis_index("north")
    even = e % 2 == 0
    forward = (e // 2) % 2 == 0
    for k, a in enumerate(taps(widths0[...].astype(F32))):
        factors[k] = a
    full[pl.ds(H, R)] = field[...]
    full[0:H] = jnp.where(even, got_b[0:H], got_a[0:H])
    full[H + R : R + 2 * H] = jnp.where(even, got_a[0:H], got_b[0:H])
    east_rows(full, factors, eastward, R, 2)
    for l in range(1, LEVELS + 1):
        r, out, own = R >> l, joined[l - 1], coarse[l - 1]
        out[H : H + r + 2] = own[...]
        out[0:H] = jnp.zeros((H, Z, LANES), F32)
        out[H + r + 2 : 2 * H + r + 2] = jnp.zeros((H, Z, LANES), F32)
    for i in range(SLOT):
        a, b = got_a[H + i], got_b[H + i]
        lower, upper = jnp.where(even, b, a), jnp.where(even, a, b)
        for l in range(1, LEVELS + 1):
            r, out = R >> l, joined[l - 1]
            out[i] = out[i] + lower
            out[r + H + i] = out[r + H + i] + upper
    r, out = R >> LEVELS, joined[LEVELS - 1]
    for i in range(2):
        c, d = got_c[i], got_d[i]
        out[i] = out[i] + jnp.where(forward, d, c)
        out[r + 2 * H + i] = out[r + 2 * H + i] + jnp.where(forward, c, d)
    last = H + SLOT
    rows_a, rows_b = got_a[last], got_b[last]
    lower, upper = jnp.where(even, rows_b, rows_a), jnp.where(even, rows_a, rows_b)
    for j, (own, out) in enumerate(zip((*widths, *gains), (*wide, *gain))):
        r, m = own.shape
        out[...] = jnp.zeros(out.shape, F32)
        out[pl.ds(H, r), pl.ds(H + 1, m)] = own[...].astype(F32)
        out[pl.ds(H - 1, 1), pl.ds(H + 1, m)] = lower[j : j + 1, 0:m]
        out[pl.ds(H + r, 1), pl.ds(H + 1, m)] = upper[j : j + 1, 0:m]
    north_even = n % 2 == 0
    lane = lanes_of(Z)

    def send(t, low_side, high_side):
        send_x[t] = jnp.where(north_even, high_side, low_side)
        send_y[t] = jnp.where(north_even, low_side, high_side)

    zero = jnp.zeros((Z, LANES), F32)
    todo = [(l, i) for l in range(LEVELS) for i in range(joined[l].shape[0])]
    for t in range(geo["coarse_tiles"]):
        low_side, high_side = zero, zero
        for s, (l, i) in enumerate(todo[t * PER_TILE : (t + 1) * PER_TILE]):
            row, m = joined[l][i], M >> (l + 1)
            here = (lane >= SLOT * s) & (lane < SLOT * (s + 1))
            low_side = jnp.where(here, roll(row, SLOT * s - bases[l]), low_side)
            high_side = jnp.where(here, roll(row, SLOT * s - bases[l] - m + H), high_side)
        send(t, low_side, high_side)
    per = LANES // H
    for t in range(R // per):
        low_side, high_side = zero, zero
        for s in range(per):
            row = eastward[t * per + s]
            here = (lane >= H * s) & (lane < H * (s + 1))
            low_side = jnp.where(here, roll(row, H * s), low_side)
            high_side = jnp.where(here, roll(row, H * s - M + H), high_side)
        send(geo["coarse_tiles"] + t, low_side, high_side)
    base = geo["coarse_tiles"] + R // per
    for t in range(wide[0].shape[0] // Z):
        low_side, high_side = zero, zero
        for j, ref in enumerate((*wide, *gain)):
            rows, m = ref.shape[0], M >> (j % LEVELS + 1)
            have = min(max(rows - t * Z, 0), Z)
            if not have:
                continue
            part = ref[pl.ds(t * Z, have), :]
            if have < Z:
                part = jnp.concatenate([part, jnp.zeros((Z - have, LANES), F32)], axis=0)
            here = (lane >= 16 * j) & (lane < 16 * j + H + 1)
            low_side = jnp.where(here, roll(part, 16 * j - H - 1), low_side)
            high_side = jnp.where(here, roll(part, 16 * j - m), high_side)
        send(base + t, low_side, high_side)


def kron(vertical, transposed):
    Z = 16
    i = lax.broadcasted_iota(jnp.int32, (LANES, Z), 0)
    a = lax.broadcasted_iota(jnp.int32, (LANES, Z), 1)
    left = ((i // 8 if transposed else i % Z) == a).astype(F32).astype(BF16)
    b = lax.broadcasted_iota(jnp.int32, (Z, LANES), 0)
    o = lax.broadcasted_iota(jnp.int32, (Z, LANES), 1)
    right = (o % Z == b).astype(F32).astype(BF16)
    p = lax.broadcasted_iota(jnp.int32, (LANES, LANES), 0)
    q = lax.broadcasted_iota(jnp.int32, (LANES, LANES), 1)
    mask = (p % 8 if transposed else p // Z) == q // Z
    return [jnp.where(mask, mm(mm(left, part).astype(BF16), right), 0.0).astype(BF16) for part in split(vertical)]


def mix(matrix, data):
    high, low = split(data)
    return mm(matrix[0], high) + mm(matrix[0], low) + mm(matrix[1], high)


def finish(geo, *refs):
    Z, R, M, bases = geo["Z"], geo["R"], geo["M"], geo["bases"]
    it = iter(refs)
    take = lambda count: [next(it) for _ in range(count)]
    eastward, factors = take(2)
    joined = take(LEVELS)
    wide, gain = take(LEVELS), take(LEVELS)
    got_x, got_y, gain0, vertical, table = take(5)
    (out,) = take(1)
    got_low, got_high, ext, coarse_factors, passed, north, result, spread, wf, gf = take(10)
    e, n = lax.axis_index("east"), lax.axis_index("north")
    has_low, has_high = e > 0, e < geo["E"] - 1
    north_even = n % 2 == 0
    got_low[...] = jnp.where(north_even, got_y[...], got_x[...])
    got_high[...] = jnp.where(north_even, got_x[...], got_y[...])
    lane = lanes_of(Z)
    per = LANES // H
    base = geo["coarse_tiles"] + R // per
    first = 0
    starts = []
    for l in range(LEVELS):
        starts.append(first)
        first += joined[l].shape[0]
    previous = None
    for l in range(LEVELS - 1, -1, -1):
        r, m = R >> (l + 1), M >> (l + 1)
        rows = r + 2 * H + 2
        count = wide[l].shape[0]
        for source, target, j in ((wide[l], wf, l), (gain[l], gf, LEVELS + l)):
            for c in range(0, count, 8):
                t, at = base + c // Z, c % Z
                lane8 = lanes_of(8)
                low_side = roll(got_low[t, at : at + 8, :], -16 * j)
                high_side = roll(got_high[t, at : at + 8, :], m + H + 1 - 16 * j)
                own = source[pl.ds(c, 8), :]
                target[pl.ds(c, 8), :] = jnp.where(
                    lane8 < H + 1, low_side, jnp.where(lane8 < m + H + 1, own, jnp.where(lane8 < m + 2 * H + 2, high_side, 0.0))
                )
        for k, a in enumerate(taps(wf[pl.ds(0, count), :])):
            coarse_factors[k, pl.ds(0, count), :] = a
        for i in range(rows):
            t, s = divmod(starts[l] + i, PER_TILE)
            own = roll(joined[l][i], H - bases[l])
            low_side = roll(got_low[t], -SLOT * s)
            high_side = roll(got_high[t], m + H - SLOT * s)
            ext[i] = (
                jnp.where((lane >= H) & (lane < m + H + 2), own, 0.0)
                + jnp.where(lane < SLOT, low_side, 0.0)
                + jnp.where((lane >= m + H) & (lane < m + H + SLOT), high_side, 0.0)
            )
        east_rows(ext, coarse_factors, passed, r + 2, 2, H - 1)

        def step(b, carry):
            for i in range(2):
                x = 2 * b + i
                value = passed[x]
                total = coarse_factors[0, pl.ds(x + H - 1, 1), :] * value
                for k in range(1, H + 1):
                    total = total + coarse_factors[k, pl.ds(x + H - 1, 1), :] * (roll(value, -k) + roll(value, k))
                north[x] = total
            return carry

        lax.fori_loop(0, (r + 2) // 2, step, 0)
        groups = (r + 2 + 7) // 8
        north[r + 2 : groups * 8] = jnp.zeros((groups * 8 - r - 2, Z, LANES), F32)
        matrix = kron(vertical[l + 1] * 4.0 ** (l + 1), False)
        for g in range(groups):
            mixed = mix(matrix, north[8 * g : 8 * g + 8].reshape(8 * Z, LANES))
            for i in range(8):
                row = 8 * g + i
                if row < r + 2:
                    result[row] = gf[pl.ds(row + H - 1, 1), :] * mixed[i * Z : (i + 1) * Z]
        if previous is not None:
            inside = ((lane > H) | (n > 0)) & ((lane < m + H + 1) | (n < geo["N"] - 1))
            for row in range(-1, r + 1):
                j = row // 2
                other = j + (1 if row % 2 else -1)
                total = result[row + 1] + 0.75 * spread[j + 1] + 0.25 * spread[other + 1]
                keep = inside
                if row == -1:
                    keep = keep & has_low
                if row == r:
                    keep = keep & has_high
                result[row + 1] = jnp.where(keep, total, 0.0)
        flat = result.reshape(result.shape[0] * Z, LANES)
        spread_flat = spread.reshape(spread.shape[0] * Z, LANES)
        weights = table[l]
        spread_flat[pl.ds(0, (r + 2) * Z), :] = dot_exact(flat[pl.ds(0, (r + 2) * Z), :], weights)
        previous = True
    matrix = kron(vertical[0], True)
    widen = table[LEVELS][:, 0 : 6 * Z]

    def block(b, carry):
        t = geo["coarse_tiles"] + b // 2
        for i in range(8):
            x = 8 * b + i
            value = eastward[x]
            s = (b % 2) * 8 + i
            low_side = pltpu.roll(got_low[t], (2 * LANES - H - H * s) % LANES, 1)
            high_side = pltpu.roll(got_high[t], (2 * LANES - H * s) % LANES, 1)
            halo = jnp.where(lane < LANES // 2, high_side, low_side)
            total = factors[0, pl.ds(x, 1), :] * value
            for k in range(1, H + 1):
                ahead = roll(jnp.where(lane < k, halo, value), -k)
                behind = roll(jnp.where(lane >= LANES - k, halo, value), k)
                total = total + factors[k, pl.ds(x, 1), :] * (ahead + behind)
            north[i] = total
        mixed = mix(matrix, north[0:8].reshape(8 * Z, LANES))
        coarse = spread[pl.ds(4 * b, 6)].reshape(6 * Z, LANES)
        high, low = split(coarse)
        added = mm(widen, high) + mm(widen, low)
        weight = gain0[pl.ds(pl.multiple_of(8 * b, 8), 8), :]
        for z in range(Z):
            out[z, pl.ds(pl.multiple_of(8 * b, 8), 8), :] = weight * mixed[z * 8 : z * 8 + 8] + added[z * 8 : z * 8 + 8]
        return carry

    lax.fori_loop(0, R // 8, block, 0)


def swap(x, axis, first, by=1):
    count = lax.axis_size(axis)
    route = []
    for i in range(count - by):
        if (i // by) % 2 == first:
            route += [(i, i + by), (i + by, i)]
    return lax.ppermute(x, axis, route)


def body(inc, w0, w1, w2, w3, g0, g1, g2, g3, vertical):
    Z, R, M = inc.shape
    bases, down, up = tables(R, M)
    total_rows = sum((R >> l) + 2 * H + 2 for l in range(1, LEVELS + 1))
    geo = dict(
        Z=Z, R=R, M=M, bases=bases, E=lax.axis_size("east"), N=lax.axis_size("north"),
        coarse_tiles=-(-total_rows // PER_TILE),
    )
    shape = lambda *dims: jax.ShapeDtypeStruct(dims, F32)
    levels = range(1, LEVELS + 1)
    params = pltpu.CompilerParams(vmem_limit_bytes=48 * 1024 * 1024)
    east_tiles = H + SLOT + 1
    outs = pl.pallas_call(
        functools.partial(prepare, geo),
        out_shape=[shape(R, Z, M)] + [shape((R >> l) + 2, Z, M) for l in levels]
        + [shape(east_tiles, Z, M)] * 2 + [shape(2, Z, M)] * 2,
        scratch_shapes=[pltpu.VMEM((R, Z, M), F32)],
        compiler_params=params,
    )(inc, w1, w2, w3, g1, g2, g3, jnp.asarray(down))
    field, coarse, sends = outs[0], outs[1 : 1 + LEVELS], outs[1 + LEVELS :]
    got_b = swap(sends[1], "east", 1)
    got_a = swap(sends[0], "east", 0)
    got_c = swap(sends[2], "east", 0, 2)
    got_d = swap(sends[3], "east", 1, 2)
    wide_shapes = [shape((R >> l) + 2 * H, M) for l in levels]
    north_tiles = geo["coarse_tiles"] + R * H // LANES + wide_shapes[0].shape[0] // Z
    outs = pl.pallas_call(
        functools.partial(middle, geo),
        out_shape=[shape(R, Z, M), shape(H + 1, R, M)]
        + [shape((R >> l) + 2 * H + 2, Z, M) for l in levels]
        + [shape(north_tiles, Z, M)] * 2 + wide_shapes * 2,
        scratch_shapes=[pltpu.VMEM((R + 2 * H, Z, M), F32)],
        compiler_params=params,
    )(field, *coarse, got_a, got_b, got_c, got_d, w0, w1, w2, w3, g1, g2, g3)
    eastward, factors = outs[0], outs[1]
    joined, (send_x, send_y) = outs[2 : 2 + LEVELS], outs[2 + LEVELS : 4 + LEVELS]
    wide, gain = outs[4 + LEVELS : 4 + 2 * LEVELS], outs[4 + 2 * LEVELS :]
    got_x = swap(send_x, "north", 0)
    got_y = swap(send_y, "north", 1)
    rows1 = (R >> 1) + 2
    padded = -(-rows1 // 8) * 8
    return pl.pallas_call(
        functools.partial(finish, geo),
        out_shape=shape(Z, R, M),
        scratch_shapes=[
            pltpu.VMEM((north_tiles, Z, M), F32),
            pltpu.VMEM((north_tiles, Z, M), F32),
            pltpu.VMEM((rows1 + 2 * H, Z, M), F32),
            pltpu.VMEM((H + 1, wide_shapes[0].shape[0], M), F32),
            pltpu.VMEM((rows1, Z, M), F32),
            pltpu.VMEM((padded, Z, M), F32),
            pltpu.VMEM((rows1, Z, M), F32),
            pltpu.VMEM((rows1, Z, M), F32),
            pltpu.VMEM(wide_shapes[0].shape, F32),
            pltpu.VMEM(wide_shapes[0].shape, F32),
        ],
        compiler_params=params,
    )(eastward, factors, *joined, *wide, *gain, got_x, got_y, g0, vertical, jnp.asarray(up))


def solution(mesh):
    tile = P("east", "north")
    return jax.shard_map(
        body,
        mesh=mesh,
        in_specs=(P(None, "east", "north"), *([tile] * 8), P()),
        out_specs=P(None, "east", "north"),
        check_vma=False,
    )
```

```python
import functools

import jax
import jax.numpy as jnp
import numpy as np
from jax import lax
from jax.experimental import pallas as pl
from jax.experimental.pallas import tpu as pltpu
from jax.sharding import PartitionSpec as P

H = 8
LANES = 128
LEVELS = 3
F32 = jnp.float32
BF16 = jnp.bfloat16
SLOT = H + 2
PER_TILE = LANES // SLOT


def tables(rows, cols):
    bases, at = [], H
    for l in range(1, LEVELS + 1):
        bases.append(at)
        at += (cols >> l) + 2
    assert at <= LANES and cols == LANES
    down = np.zeros((4, cols, LANES), np.float32)
    for variant in range(4):
        current = np.eye(cols)
        low = 0
        for l in range(1, LEVELS + 1):
            m = cols >> l
            step = np.zeros((current.shape[1], m + 2))
            for j in range(-1, m + 1):
                for f, w in ((2 * j, 0.375), (2 * j + 1, 0.375), (2 * j - 1, 0.125), (2 * j + 2, 0.125)):
                    if 0 <= f - low < current.shape[1]:
                        step[f - low, j + 1] += w
            current = current @ step
            if variant & 1:
                current[:, 0] = 0
            if variant & 2:
                current[:, -1] = 0
            low = -1
            down[variant, :, bases[l - 1] : bases[l - 1] + m + 2] = current
    frames = [0]
    for l in range(1, LEVELS + 1):
        own = bases[l - 1] + 1
        frames.append(own if own + (cols >> l) + H < LANES else H + 1)
    up = np.zeros((LEVELS + 1, LANES, LANES), np.float32)
    for l in range(LEVELS):
        m = cols >> l
        for f in range(-1, m + 1) if l else range(m):
            j = f // 2
            out, at = f + frames[l], frames[l + 1]
            up[l, j + at, out] += 0.75
            up[l, j + (1 if f % 2 else -1) + at, out] += 0.25
    for z in range(16):
        for i in range(8):
            j = i // 2 + 1
            up[LEVELS, z * 8 + i, j * 16 + z] += 0.75
            up[LEVELS, z * 8 + i, (j + (1 if i % 2 else -1)) * 16 + z] += 0.25
    for t in (down, up):
        assert (t == t.astype(jnp.bfloat16).astype(np.float32)).all()
    shifts = np.concatenate([np.eye(LANES, k=k) + np.eye(LANES, k=-k) for k in range(1, H + 1)], axis=1)
    shifts = np.concatenate([shifts, shifts], axis=0)
    return bases, frames, down.astype(jnp.bfloat16), up.astype(jnp.bfloat16), shifts.astype(jnp.bfloat16)


def split(x):
    high = x.astype(BF16)
    return high, (x - high.astype(F32)).astype(BF16)


def mm(a, b):
    return jnp.dot(a, b, preferred_element_type=F32)


def dot_exact(x, weights):
    high, low = split(x)
    return mm(high, weights) + mm(low, weights)


def lanes_of(rows):
    return lax.broadcasted_iota(jnp.int32, (rows, LANES), 1)


def roll(x, shift):
    shift %= LANES
    return pltpu.roll(x, shift, 1) if shift else x


def taps(widths):
    grown = widths + 1.0
    inverse = 1.0 / (grown * grown)
    profile = [jnp.square(jnp.maximum(1.0 - float(k * k) * inverse, 0.0)) for k in range(1, H + 1)]
    total = profile[0]
    for p in profile[1:]:
        total = total + p
    scale = 1.0 / (1.0 + 2.0 * total)
    return [scale] + [p * scale for p in profile]


def prepare(geo, *refs):
    count = 2 * LEVELS + 2
    outside, (field, *rest) = refs[:count], refs[count:]
    coarse, (send_a, send_b, send_c, send_d, half, *inside) = rest[:LEVELS], rest[LEVELS:]
    sems = inside.pop()
    copies = [pltpu.make_async_copy(a, b, sems.at[i]) for i, (a, b) in enumerate(zip(outside, inside))]
    for copy in copies:
        copy.start()
    inc, table, *small = inside
    widths, gains = small[:LEVELS], small[LEVELS:]
    Z, R, M, bases = geo["Z"], geo["R"], geo["M"], geo["bases"]
    e, n = lax.axis_index("east"), lax.axis_index("north")
    has_low, has_high = e > 0, e < geo["E"] - 1
    even = e % 2 == 0
    flat = field.reshape(R * Z, M)
    for copy in copies:
        copy.wait()
    for z in range(Z):
        flat[pl.ds(z, R, stride=Z), :] = inc[z]
    variant = (n == 0).astype(jnp.int32) + 2 * (n == geo["N"] - 1).astype(jnp.int32)
    weights = table[variant]
    half_flat = half.reshape(R * Z, M)
    chunk = R * Z // 4
    for c in range(4):
        half_flat[pl.ds(c * chunk, chunk), :] = dot_exact(flat[pl.ds(c * chunk, chunk), :], weights)
    source, low, top = half, 0, R
    for l in range(1, LEVELS + 1):
        r, out = R >> l, coarse[l - 1]

        def get(i, source=source, low=low, top=top):
            return source[i - low] if low <= i < top else None

        for j in range(-1, r + 1):
            total = None
            for pair, w in (((2 * j, 2 * j + 1), 0.375), ((2 * j - 1, 2 * j + 2), 0.125)):
                terms = [t for t in (get(i) for i in pair) if t is not None]
                if terms:
                    part = w * functools.reduce(jnp.add, terms)
                    total = part if total is None else total + part
            if j == -1:
                total = jnp.where(has_low, total, 0.0)
            if j == r:
                total = jnp.where(has_high, total, 0.0)
            out[j + 1] = total
        source, low, top = out, -1, r + 1
    start = R - H
    send_a[0:H] = field[pl.ds(jnp.where(even, start, 0), H)]
    send_b[0:H] = field[pl.ds(jnp.where(even, 0, start), H)]
    lane = lanes_of(Z)
    for i in range(SLOT):
        def merged(picks):
            out = coarse[LEVELS - 1][picks[LEVELS - 1]]
            for l in range(LEVELS - 1, 0, -1):
                out = jnp.where(lane < bases[l], coarse[l - 1][picks[l - 1]], out)
            return out

        lower = merged([i] * LEVELS)
        upper = merged([(R >> l) - H + i for l in range(1, LEVELS + 1)])
        send_a[H + i] = jnp.where(even, upper, lower)
        send_b[H + i] = jnp.where(even, lower, upper)
    last = H + SLOT
    send_a[last] = jnp.zeros((Z, LANES), F32)
    send_b[last] = jnp.zeros((Z, LANES), F32)
    for j, ref in enumerate((*widths, *gains)):
        r, m = ref.shape
        lower = ref[pl.ds(0, 1), :].astype(F32)
        upper = ref[pl.ds(r - 1, 1), :].astype(F32)
        send_a[last, pl.ds(j, 1), pl.ds(0, m)] = jnp.where(even, upper, lower)
        send_b[last, pl.ds(j, 1), pl.ds(0, m)] = jnp.where(even, lower, upper)
    r = R >> LEVELS
    forward = (e // 2) % 2 == 0
    for i in range(2):
        lower, upper = coarse[LEVELS - 1][i], coarse[LEVELS - 1][r + i]
        send_c[i] = jnp.where(forward, upper, lower)
        send_d[i] = jnp.where(forward, lower, upper)


def east_rows(source, factors, out, count, block, factor_at=0, source_at=0, out_at=0):
    def step(b, carry):
        x0 = b * block
        rows = [source[x0 + i + source_at] for i in range(block + 2 * H)]
        for i in range(block):
            def factor(k):
                return factors[k, pl.ds(x0 + i + factor_at, 1), :]

            total = factor(0) * rows[i + H]
            for k in range(1, H + 1):
                total = total + factor(k) * (rows[i + H + k] + rows[i + H - k])
            out[x0 + i + out_at] = total
        return carry

    lax.fori_loop(0, count // block, step, 0)


def middle(geo, *refs):
    Z, R, M, bases = geo["Z"], geo["R"], geo["M"], geo["bases"]
    it = iter(refs)
    take = lambda count: [next(it) for _ in range(count)]
    (field,) = take(1)
    coarse = take(LEVELS)
    got_a, got_b, got_c, got_d, widths0 = take(5)
    widths, gains = take(LEVELS), take(LEVELS)
    eastward, factors = take(2)
    joined = take(LEVELS)
    send_x, send_y = take(2)
    wide, gain = take(LEVELS), take(LEVELS)
    (full,) = take(1)
    e, n = lax.axis_index("east"), lax.axis_index("north")
    even = e % 2 == 0
    forward = (e // 2) % 2 == 0
    for k, a in enumerate(taps(widths0[...].astype(F32))):
        factors[k] = a
    full[pl.ds(H, R)] = field[...]
    full[0:H] = jnp.where(even, got_b[0:H], got_a[0:H])
    full[H + R : R + 2 * H] = jnp.where(even, got_a[0:H], got_b[0:H])
    east_rows(full, factors, eastward, R, 4)
    for l in range(1, LEVELS + 1):
        r, out, own = R >> l, joined[l - 1], coarse[l - 1]
        out[H : H + r + 2] = own[...]
        out[0:H] = jnp.zeros((H, Z, LANES), F32)
        out[H + r + 2 : 2 * H + r + 2] = jnp.zeros((H, Z, LANES), F32)
    for i in range(SLOT):
        a, b = got_a[H + i], got_b[H + i]
        lower, upper = jnp.where(even, b, a), jnp.where(even, a, b)
        for l in range(1, LEVELS + 1):
            r, out = R >> l, joined[l - 1]
            out[i] = out[i] + lower
            out[r + H + i] = out[r + H + i] + upper
    r, out = R >> LEVELS, joined[LEVELS - 1]
    for i in range(2):
        c, d = got_c[i], got_d[i]
        out[i] = out[i] + jnp.where(forward, d, c)
        out[r + 2 * H + i] = out[r + 2 * H + i] + jnp.where(forward, c, d)
    last = H + SLOT
    rows_a, rows_b = got_a[last], got_b[last]
    lower, upper = jnp.where(even, rows_b, rows_a), jnp.where(even, rows_a, rows_b)
    for j, (own, out) in enumerate(zip((*widths, *gains), (*wide, *gain))):
        r, m = own.shape
        out[...] = jnp.zeros(out.shape, F32)
        at = geo["frames"][j % LEVELS + 1]
        out[pl.ds(H, r), pl.ds(at, m)] = own[...].astype(F32)
        out[pl.ds(H - 1, 1), pl.ds(at, m)] = lower[j : j + 1, 0:m]
        out[pl.ds(H + r, 1), pl.ds(at, m)] = upper[j : j + 1, 0:m]
    north_even = n % 2 == 0
    lane = lanes_of(Z)

    def send(t, low_side, high_side):
        send_x[t] = jnp.where(north_even, high_side, low_side)
        send_y[t] = jnp.where(north_even, low_side, high_side)

    zero = jnp.zeros((Z, LANES), F32)
    todo = [(l, i) for l in range(LEVELS) for i in range(joined[l].shape[0])]
    for t in range(geo["coarse_tiles"]):
        low_side, high_side = zero, zero
        for s, (l, i) in enumerate(todo[t * PER_TILE : (t + 1) * PER_TILE]):
            row, m = joined[l][i], M >> (l + 1)
            here = (lane >= SLOT * s) & (lane < SLOT * (s + 1))
            low_side = jnp.where(here, roll(row, SLOT * s - bases[l]), low_side)
            high_side = jnp.where(here, roll(row, SLOT * s - bases[l] - m + H), high_side)
        send(t, low_side, high_side)
    per = LANES // H
    for t in range(R // per):
        low_side, high_side = zero, zero
        for s in range(per):
            row, at = eastward[t * per + s], 2 * H * (s % H) + H * (s // H)
            here = (lane >= at) & (lane < at + H)
            low_side = jnp.where(here, roll(row, at), low_side)
            high_side = jnp.where(here, roll(row, at - M + H), high_side)
        send(geo["coarse_tiles"] + t, low_side, high_side)
    base = geo["coarse_tiles"] + R // per
    for t in range(wide[0].shape[0] // Z):
        low_side, high_side = zero, zero
        for j, ref in enumerate((*wide, *gain)):
            rows, m = ref.shape[0], M >> (j % LEVELS + 1)
            have = min(max(rows - t * Z, 0), Z)
            if not have:
                continue
            part = ref[pl.ds(t * Z, have), :]
            if have < Z:
                part = jnp.concatenate([part, jnp.zeros((Z - have, LANES), F32)], axis=0)
            here = (lane >= 16 * j) & (lane < 16 * j + H + 1)
            at = geo["frames"][j % LEVELS + 1]
            low_side = jnp.where(here, roll(part, 16 * j - at), low_side)
            high_side = jnp.where(here, roll(part, 16 * j - at - m + H + 1), high_side)
        send(base + t, low_side, high_side)


def kron(vertical, transposed):
    Z = 16
    i = lax.broadcasted_iota(jnp.int32, (LANES, Z), 0)
    a = lax.broadcasted_iota(jnp.int32, (LANES, Z), 1)
    left = ((i // 8 if transposed else i % Z) == a).astype(F32).astype(BF16)
    b = lax.broadcasted_iota(jnp.int32, (Z, LANES), 0)
    o = lax.broadcasted_iota(jnp.int32, (Z, LANES), 1)
    right = (o % Z == b).astype(F32).astype(BF16)
    p = lax.broadcasted_iota(jnp.int32, (LANES, LANES), 0)
    q = lax.broadcasted_iota(jnp.int32, (LANES, LANES), 1)
    mask = (p % 8 if transposed else p // Z) == q // Z
    return [jnp.where(mask, mm(mm(left, part).astype(BF16), right), 0.0).astype(BF16) for part in split(vertical)]


def mix(matrix, data):
    high, low = split(data)
    return mm(matrix[0], high) + mm(matrix[0], low) + mm(matrix[1], high)


def finish(geo, *refs):
    Z, R, M, bases, frames = geo["Z"], geo["R"], geo["M"], geo["bases"], geo["frames"]
    it = iter(refs)
    take = lambda count: [next(it) for _ in range(count)]
    eastward, factors = take(2)
    joined = take(LEVELS)
    wide, gain = take(LEVELS), take(LEVELS)
    got_x, got_y, gain0, widths0, vertical, table, shifts = take(7)
    (out,) = take(1)
    got_low, got_high, ext, passed, north, result, spread, wf, gf, cf, north0, edge = take(12)
    e, n = lax.axis_index("east"), lax.axis_index("north")
    has_low, has_high = e > 0, e < geo["E"] - 1
    north_even = n % 2 == 0
    got_low[...] = jnp.where(north_even, got_y[...], got_x[...])
    got_high[...] = jnp.where(north_even, got_x[...], got_y[...])
    lane = lanes_of(Z)
    lane8 = lanes_of(8)
    per = LANES // H
    base = geo["coarse_tiles"] + R // per
    levels = range(1, LEVELS + 1)
    rows_of = [R >> l for l in levels]
    starts = lambda more: [sum(rows_of[:l]) + l * more for l in range(LEVELS + 1)]
    ext_at = starts(2 * H + 2)
    out_at = starts(2)
    width_at = starts(2 * H)
    for l in range(LEVELS):
        r, m, at = R >> (l + 1), M >> (l + 1), frames[l + 1]
        for source, target, j in ((wide[l], wf, l), (gain[l], gf, LEVELS + l)):
            for c in range(0, r + 2 * H, 8):
                t, row = base + c // Z, c % Z
                low_side = roll(got_low[t, row : row + 8, :], at - H - 1 - 16 * j)
                high_side = roll(got_high[t, row : row + 8, :], at + m - 16 * j)
                joint = jnp.where(lane8 < at, low_side, jnp.where(lane8 < at + m, source[pl.ds(c, 8), :], high_side))
                target[pl.ds(width_at[l] + c, 8), :] = jnp.where((lane8 >= at - H - 1) & (lane8 < at + m + H + 1), joint, 0.0)
        for i in range(r + 2 * H + 2):
            t, s = divmod(ext_at[l] + i, PER_TILE)
            own = roll(joined[l][i], at - 1 - bases[l])
            low_side = roll(got_low[t], at - H - 1 - SLOT * s)
            high_side = roll(got_high[t], at + m - 1 - SLOT * s)
            ext[ext_at[l] + i] = (
                jnp.where((lane >= at - 1) & (lane < at + m + 1), own, 0.0)
                + jnp.where((lane >= at - H - 1) & (lane < at + 1), low_side, 0.0)
                + jnp.where((lane >= at + m - 1) & (lane < at + m + H + 1), high_side, 0.0)
            )
    for k, a in enumerate(taps(wf[...])):
        cf[k] = a
    for l in range(LEVELS):
        r = R >> (l + 1)
        east_rows(ext, cf, passed, r + 2, 2, width_at[l] + H - 1, ext_at[l], out_at[l])

    def north_rows(source, target, rows, factor):
        data = source[pl.ds(rows[0], len(rows))].reshape(len(rows) * Z, LANES)
        pair = jnp.concatenate(split(data), axis=1)
        for k in range(1, H + 1, 2):
            moved = mm(pair, shifts[:, (k - 1) * LANES : (k + 1) * LANES])
            for i, x in enumerate(rows):
                here = moved[i * Z : (i + 1) * Z]
                before = factor(0, x) * source[x] if k == 1 else target[x]
                target[x] = before + factor(k, x) * here[:, :LANES] + factor(k + 1, x) * here[:, LANES:]

    total = out_at[-1]

    def coarse_factor(k, x):
        l = max(i for i in range(LEVELS) if out_at[i] <= x)
        return cf[k, pl.ds(width_at[l] + H - 1 + x - out_at[l], 1), :]

    half = -(-total // 2)
    north_rows(passed, north, range(0, half), coarse_factor)
    north_rows(passed, north, range(half, total), coarse_factor)
    for l in range(LEVELS - 1, -1, -1):
        r, m, at = R >> (l + 1), M >> (l + 1), frames[l + 1]
        groups = (r + 2 + 7) // 8
        matrix = kron(vertical[l + 1] * 4.0 ** (l + 1), False)
        for g in range(groups):
            have = min(8, r + 2 - 8 * g)
            data = north[out_at[l] + 8 * g : out_at[l] + 8 * g + have].reshape(have * Z, LANES)
            if have < 8:
                data = jnp.concatenate([data, jnp.zeros(((8 - have) * Z, LANES), F32)], axis=0)
            mixed = mix(matrix, data)
            for i in range(have):
                row = 8 * g + i
                result[row] = gf[pl.ds(width_at[l] + row + H - 1, 1), :] * mixed[i * Z : (i + 1) * Z]
        if l < LEVELS - 1:
            inside = ((lane >= at) | (n > 0)) & ((lane < at + m) | (n < geo["N"] - 1))
            for row in range(-1, r + 1):
                j = row // 2
                other = j + (1 if row % 2 else -1)
                summed = result[row + 1] + 0.75 * spread[j + 1] + 0.25 * spread[other + 1]
                keep = inside
                if row == -1:
                    keep = keep & has_low
                if row == r:
                    keep = keep & has_high
                result[row + 1] = jnp.where(keep, summed, 0.0)
        flat = result.reshape(result.shape[0] * Z, LANES)
        spread_flat = spread.reshape(spread.shape[0] * Z, LANES)
        spread_flat[pl.ds(0, (r + 2) * Z), :] = dot_exact(flat[pl.ds(0, (r + 2) * Z), :], table[l])
    slot = lane8 % (2 * H)
    width = jnp.zeros((H, LANES), F32)
    for s in range(H):
        rows = widths0[pl.ds(s, R // H, stride=H), :].astype(F32)
        width = jnp.where(lane8 // (2 * H) == s, roll(rows, 2 * H * s + H), width)
    edge_taps = [jnp.where((slot >= H - k) & (slot < H + k), a, 0.0) for k, a in enumerate(taps(width))]
    low_half = lane % (2 * H) < H
    for t in range(R // H):
        tile = geo["coarse_tiles"] + t // 2
        low_side, high_side = got_low[tile], got_high[tile]
        if t % 2:
            low_side = roll(low_side, -H)
        else:
            high_side = roll(high_side, H)
        halo = jnp.where(low_half, low_side, high_side)
        summed = jnp.zeros((Z, LANES), F32)
        for k in range(1, H + 1):
            summed = summed + edge_taps[k][t : t + 1] * jnp.where(low_half, roll(halo, -k), roll(halo, k))
        edge[t] = summed
    matrix = kron(vertical[0], True)
    widen = table[LEVELS][:, 0 : 6 * Z]
    factor0 = lambda k, x: factors[k, pl.ds(x, 1), :]
    for x0 in range(0, R, R // 2):
        north_rows(eastward, north0, range(x0, x0 + R // 2), factor0)
    at_edge = (lane < H) | (lane >= M - H)
    for b in range(R // 8):
        for i in range(8):
            x = 8 * b + i
            north0[x] = north0[x] + jnp.where(at_edge, roll(edge[b], M - H - 2 * H * i), 0.0)
        mixed = mix(matrix, north0[8 * b : 8 * b + 8].reshape(8 * Z, LANES))
        high, low = split(spread[4 * b : 4 * b + 6].reshape(6 * Z, LANES))
        added = mm(widen, high) + mm(widen, low)
        weight = gain0[pl.ds(8 * b, 8), :]
        for z in range(Z):
            out[z, pl.ds(8 * b, 8), :] = weight * mixed[z * 8 : z * 8 + 8] + added[z * 8 : z * 8 + 8]


def swap(x, axis, first, by=1):
    count = lax.axis_size(axis)
    route = []
    for i in range(count - by):
        if (i // by) % 2 == first:
            route += [(i, i + by), (i + by, i)]
    return lax.ppermute(x, axis, route)


def body(inc, w0, w1, w2, w3, g0, g1, g2, g3, vertical):
    Z, R, M = inc.shape
    bases, frames, down, up, shifts = tables(R, M)
    total_rows = sum((R >> l) + 2 * H + 2 for l in range(1, LEVELS + 1))
    geo = dict(
        Z=Z, R=R, M=M, bases=bases, frames=frames, E=lax.axis_size("east"), N=lax.axis_size("north"),
        coarse_tiles=-(-total_rows // PER_TILE),
    )
    shape = lambda *dims: jax.ShapeDtypeStruct(dims, F32)
    levels = range(1, LEVELS + 1)
    params = pltpu.CompilerParams(vmem_limit_bytes=48 * 1024 * 1024)
    east_tiles = H + SLOT + 1
    given = (inc, jnp.asarray(down), w1, w2, w3, g1, g2, g3)
    outs = pl.pallas_call(
        functools.partial(prepare, geo),
        out_shape=[shape(R, Z, M)] + [shape((R >> l) + 2, Z, M) for l in levels]
        + [shape(east_tiles, Z, M)] * 2 + [shape(2, Z, M)] * 2,
        in_specs=[pl.BlockSpec(memory_space=pl.ANY)] * len(given),
        scratch_shapes=[pltpu.VMEM((R, Z, M), F32)] + [pltpu.VMEM(x.shape, x.dtype) for x in given]
        + [pltpu.SemaphoreType.DMA((len(given),))],
        compiler_params=params,
    )(*given)
    field, coarse, sends = outs[0], outs[1 : 1 + LEVELS], outs[1 + LEVELS :]
    got_b = swap(sends[1], "east", 1)
    got_a = swap(sends[0], "east", 0)
    got_c = swap(sends[2], "east", 0, 2)
    got_d = swap(sends[3], "east", 1, 2)
    wide_shapes = [shape((R >> l) + 2 * H, M) for l in levels]
    north_tiles = geo["coarse_tiles"] + R * H // LANES + wide_shapes[0].shape[0] // Z
    outs = pl.pallas_call(
        functools.partial(middle, geo),
        out_shape=[shape(R, Z, M), shape(H + 1, R, M)]
        + [shape((R >> l) + 2 * H + 2, Z, M) for l in levels]
        + [shape(north_tiles, Z, M)] * 2 + wide_shapes * 2,
        scratch_shapes=[pltpu.VMEM((R + 2 * H, Z, M), F32)],
        compiler_params=params,
    )(field, *coarse, got_a, got_b, got_c, got_d, w0, w1, w2, w3, g1, g2, g3)
    eastward, factors = outs[0], outs[1]
    joined, (send_x, send_y) = outs[2 : 2 + LEVELS], outs[2 + LEVELS : 4 + LEVELS]
    wide, gain = outs[4 + LEVELS : 4 + 2 * LEVELS], outs[4 + 2 * LEVELS :]
    got_x = swap(send_x, "north", 0)
    got_y = swap(send_y, "north", 1)
    rows1 = (R >> 1) + 2
    out_rows = sum((R >> l) + 2 for l in levels)
    width_rows = out_rows + LEVELS * (2 * H - 2)
    return pl.pallas_call(
        functools.partial(finish, geo),
        out_shape=shape(Z, R, M),
        scratch_shapes=[
            pltpu.VMEM(dims, F32)
            for dims in (
                (north_tiles, Z, M), (north_tiles, Z, M), (total_rows, Z, M), (out_rows, Z, M), (out_rows, Z, M),
                (rows1, Z, M), (rows1, Z, M), (width_rows, M), (width_rows, M), (H + 1, width_rows, M),
                (R, Z, M), (R // H, Z, M),
            )
        ],
        compiler_params=params,
    )(eastward, factors, *joined, *wide, *gain, got_x, got_y, g0, w0, vertical, jnp.asarray(up), jnp.asarray(shifts))


def solution(mesh):
    tile = P("east", "north")
    return jax.shard_map(
        body,
        mesh=mesh,
        in_specs=(P(None, "east", "north"), *([tile] * 8), P()),
        out_specs=P(None, "east", "north"),
        check_vma=False,
    )
```

```python
import functools

import jax
import jax.numpy as jnp
import numpy as np
from jax import lax
from jax.experimental import pallas as pl
from jax.experimental.pallas import tpu as pltpu
from jax.sharding import PartitionSpec as P

H = 8
LANES = 128
LEVELS = 3
F32 = jnp.float32
BF16 = jnp.bfloat16
SLOT = H + 2
PER_TILE = LANES // SLOT


def tables(rows, cols):
    bases, at = [], H
    for l in range(1, LEVELS + 1):
        bases.append(at)
        at += (cols >> l) + 2
    assert at <= LANES and cols == LANES
    down = np.zeros((4, cols, LANES), np.float32)
    for variant in range(4):
        current = np.eye(cols)
        low = 0
        for l in range(1, LEVELS + 1):
            m = cols >> l
            step = np.zeros((current.shape[1], m + 2))
            for j in range(-1, m + 1):
                for f, w in ((2 * j, 0.375), (2 * j + 1, 0.375), (2 * j - 1, 0.125), (2 * j + 2, 0.125)):
                    if 0 <= f - low < current.shape[1]:
                        step[f - low, j + 1] += w
            current = current @ step
            if variant & 1:
                current[:, 0] = 0
            if variant & 2:
                current[:, -1] = 0
            low = -1
            down[variant, :, bases[l - 1] : bases[l - 1] + m + 2] = current
    frames = [0]
    for l in range(1, LEVELS + 1):
        own = bases[l - 1] + 1
        frames.append(own if own + (cols >> l) + H < LANES else H + 1)
    up = np.zeros((LEVELS + 1, LANES, LANES), np.float32)
    for l in range(LEVELS):
        m = cols >> l
        for f in range(-1, m + 1) if l else range(m):
            j = f // 2
            out, at = f + frames[l], frames[l + 1]
            up[l, j + at, out] += 0.75
            up[l, j + (1 if f % 2 else -1) + at, out] += 0.25
    for z in range(16):
        for i in range(8):
            j = i // 2 + 1
            up[LEVELS, z * 8 + i, j * 16 + z] += 0.75
            up[LEVELS, z * 8 + i, (j + (1 if i % 2 else -1)) * 16 + z] += 0.25
    for t in (down, up):
        assert (t == t.astype(jnp.bfloat16).astype(np.float32)).all()
    shifts = np.concatenate([np.eye(LANES, k=k) + np.eye(LANES, k=-k) for k in range(1, H + 1)], axis=1)
    shifts = np.concatenate([shifts, shifts], axis=0)
    return bases, frames, down.astype(jnp.bfloat16), up.astype(jnp.bfloat16), shifts.astype(jnp.bfloat16)


def split(x):
    high = x.astype(BF16)
    return high, (x - high.astype(F32)).astype(BF16)


def mm(a, b):
    return jnp.dot(a, b, preferred_element_type=F32)


def dot_exact(x, weights):
    high, low = split(x)
    return mm(high, weights) + mm(low, weights)


def lanes_of(rows):
    return lax.broadcasted_iota(jnp.int32, (rows, LANES), 1)


def roll(x, shift):
    shift %= LANES
    return pltpu.roll(x, shift, 1) if shift else x


def taps(widths):
    grown = widths + 1.0
    inverse = 1.0 / (grown * grown)
    profile = [jnp.square(jnp.maximum(1.0 - float(k * k) * inverse, 0.0)) for k in range(1, H + 1)]
    total = profile[0]
    for p in profile[1:]:
        total = total + p
    scale = 1.0 / (1.0 + 2.0 * total)
    return [scale] + [p * scale for p in profile]


def prepare(geo, *refs):
    count = 2 * LEVELS + 2
    outside, (field, *rest) = refs[:count], refs[count:]
    coarse, (send_a, send_b, send_c, send_d, half, *inside) = rest[:LEVELS], rest[LEVELS:]
    sems = inside.pop()
    copies = [pltpu.make_async_copy(a, b, sems.at[i]) for i, (a, b) in enumerate(zip(outside, inside))]
    for copy in copies:
        copy.start()
    inc, table, *small = inside
    widths, gains = small[:LEVELS], small[LEVELS:]
    Z, R, M, bases = geo["Z"], geo["R"], geo["M"], geo["bases"]
    e, n = lax.axis_index("east"), lax.axis_index("north")
    has_low, has_high = e > 0, e < geo["E"] - 1
    even = e % 2 == 0
    flat = field.reshape(R * Z, M)
    for copy in copies:
        copy.wait()
    for z in range(Z):
        flat[pl.ds(z, R, stride=Z), :] = inc[z]
    variant = (n == 0).astype(jnp.int32) + 2 * (n == geo["N"] - 1).astype(jnp.int32)
    weights = table[variant]
    half_flat = half.reshape(R * Z, M)
    chunk = R * Z // 4
    for c in range(4):
        half_flat[pl.ds(c * chunk, chunk), :] = dot_exact(flat[pl.ds(c * chunk, chunk), :], weights)
    source, low, top = half, 0, R
    for l in range(1, LEVELS + 1):
        r, out = R >> l, coarse[l - 1]

        def get(i, source=source, low=low, top=top):
            return source[i - low] if low <= i < top else None

        for j in range(-1, r + 1):
            total = None
            for pair, w in (((2 * j, 2 * j + 1), 0.375), ((2 * j - 1, 2 * j + 2), 0.125)):
                terms = [t for t in (get(i) for i in pair) if t is not None]
                if terms:
                    part = w * functools.reduce(jnp.add, terms)
                    total = part if total is None else total + part
            if j == -1:
                total = jnp.where(has_low, total, 0.0)
            if j == r:
                total = jnp.where(has_high, total, 0.0)
            out[j + 1] = total
        source, low, top = out, -1, r + 1
    start = R - H
    send_a[0:H] = field[pl.ds(jnp.where(even, start, 0), H)]
    send_b[0:H] = field[pl.ds(jnp.where(even, 0, start), H)]
    lane = lanes_of(Z)
    for i in range(SLOT):
        def merged(picks):
            out = coarse[LEVELS - 1][picks[LEVELS - 1]]
            for l in range(LEVELS - 1, 0, -1):
                out = jnp.where(lane < bases[l], coarse[l - 1][picks[l - 1]], out)
            return out

        lower = merged([i] * LEVELS)
        upper = merged([(R >> l) - H + i for l in range(1, LEVELS + 1)])
        send_a[H + i] = jnp.where(even, upper, lower)
        send_b[H + i] = jnp.where(even, lower, upper)
    last = H + SLOT
    send_a[last] = jnp.zeros((Z, LANES), F32)
    send_b[last] = jnp.zeros((Z, LANES), F32)
    for j, ref in enumerate((*widths, *gains)):
        r, m = ref.shape
        lower = ref[pl.ds(0, 1), :].astype(F32)
        upper = ref[pl.ds(r - 1, 1), :].astype(F32)
        send_a[last, pl.ds(j, 1), pl.ds(0, m)] = jnp.where(even, upper, lower)
        send_b[last, pl.ds(j, 1), pl.ds(0, m)] = jnp.where(even, lower, upper)
    r = R >> LEVELS
    forward = (e // 2) % 2 == 0
    for i in range(2):
        lower, upper = coarse[LEVELS - 1][i], coarse[LEVELS - 1][r + i]
        send_c[i] = jnp.where(forward, upper, lower)
        send_d[i] = jnp.where(forward, lower, upper)


def east_rows(source, factors, out, count, block, factor_at=0, source_at=0, out_at=0):
    def step(b, carry):
        x0 = b * block
        rows = [source[x0 + i + source_at] for i in range(block + 2 * H)]
        for i in range(block):
            def factor(k):
                return factors[k, pl.ds(x0 + i + factor_at, 1), :]

            total = factor(0) * rows[i + H]
            for k in range(1, H + 1):
                total = total + factor(k) * (rows[i + H + k] + rows[i + H - k])
            out[x0 + i + out_at] = total
        return carry

    lax.fori_loop(0, count // block, step, 0)


def middle(geo, *refs):
    Z, R, M, bases = geo["Z"], geo["R"], geo["M"], geo["bases"]
    it = iter(refs)
    take = lambda count: [next(it) for _ in range(count)]
    (field,) = take(1)
    coarse = take(LEVELS)
    got_a, got_b, got_c, got_d, widths0 = take(5)
    widths, gains = take(LEVELS), take(LEVELS)
    eastward, factors = take(2)
    joined = take(LEVELS)
    send_x, send_y = take(2)
    wide, gain = take(LEVELS), take(LEVELS)
    (full,) = take(1)
    e, n = lax.axis_index("east"), lax.axis_index("north")
    even = e % 2 == 0
    forward = (e // 2) % 2 == 0
    for k, a in enumerate(taps(widths0[...].astype(F32))):
        factors[k] = a
    full[pl.ds(H, R)] = field[...]
    full[0:H] = jnp.where(even, got_b[0:H], got_a[0:H])
    full[H + R : R + 2 * H] = jnp.where(even, got_a[0:H], got_b[0:H])
    east_rows(full, factors, eastward, R, 4)
    for l in range(1, LEVELS + 1):
        r, out, own = R >> l, joined[l - 1], coarse[l - 1]
        out[H : H + r + 2] = own[...]
        out[0:H] = jnp.zeros((H, Z, LANES), F32)
        out[H + r + 2 : 2 * H + r + 2] = jnp.zeros((H, Z, LANES), F32)
    for i in range(SLOT):
        a, b = got_a[H + i], got_b[H + i]
        lower, upper = jnp.where(even, b, a), jnp.where(even, a, b)
        for l in range(1, LEVELS + 1):
            r, out = R >> l, joined[l - 1]
            out[i] = out[i] + lower
            out[r + H + i] = out[r + H + i] + upper
    r, out = R >> LEVELS, joined[LEVELS - 1]
    for i in range(2):
        c, d = got_c[i], got_d[i]
        out[i] = out[i] + jnp.where(forward, d, c)
        out[r + 2 * H + i] = out[r + 2 * H + i] + jnp.where(forward, c, d)
    last = H + SLOT
    rows_a, rows_b = got_a[last], got_b[last]
    lower, upper = jnp.where(even, rows_b, rows_a), jnp.where(even, rows_a, rows_b)
    for j, (own, out) in enumerate(zip((*widths, *gains), (*wide, *gain))):
        r, m = own.shape
        out[...] = jnp.zeros(out.shape, F32)
        at = geo["frames"][j % LEVELS + 1]
        out[pl.ds(H, r), pl.ds(at, m)] = own[...].astype(F32)
        out[pl.ds(H - 1, 1), pl.ds(at, m)] = lower[j : j + 1, 0:m]
        out[pl.ds(H + r, 1), pl.ds(at, m)] = upper[j : j + 1, 0:m]
    north_even = n % 2 == 0
    lane = lanes_of(Z)

    def send(t, low_side, high_side):
        send_x[t] = jnp.where(north_even, high_side, low_side)
        send_y[t] = jnp.where(north_even, low_side, high_side)

    zero = jnp.zeros((Z, LANES), F32)
    todo = [(l, i) for l in range(LEVELS) for i in range(joined[l].shape[0])]
    for t in range(geo["coarse_tiles"]):
        low_side, high_side = zero, zero
        for s, (l, i) in enumerate(todo[t * PER_TILE : (t + 1) * PER_TILE]):
            row, m = joined[l][i], M >> (l + 1)
            here = (lane >= SLOT * s) & (lane < SLOT * (s + 1))
            low_side = jnp.where(here, roll(row, SLOT * s - bases[l]), low_side)
            high_side = jnp.where(here, roll(row, SLOT * s - bases[l] - m + H), high_side)
        send(t, low_side, high_side)
    per = LANES // H
    for t in range(R // per):
        low_side, high_side = zero, zero
        for s in range(per):
            row, at = eastward[t * per + s], 2 * H * (s % H) + H * (s // H)
            here = (lane >= at) & (lane < at + H)
            low_side = jnp.where(here, roll(row, at), low_side)
            high_side = jnp.where(here, roll(row, at - M + H), high_side)
        send(geo["coarse_tiles"] + t, low_side, high_side)
    base = geo["coarse_tiles"] + R // per
    for t in range(wide[0].shape[0] // Z):
        low_side, high_side = zero, zero
        for j, ref in enumerate((*wide, *gain)):
            rows, m = ref.shape[0], M >> (j % LEVELS + 1)
            have = min(max(rows - t * Z, 0), Z)
            if not have:
                continue
            part = ref[pl.ds(t * Z, have), :]
            if have < Z:
                part = jnp.concatenate([part, jnp.zeros((Z - have, LANES), F32)], axis=0)
            here = (lane >= 16 * j) & (lane < 16 * j + H + 1)
            at = geo["frames"][j % LEVELS + 1]
            low_side = jnp.where(here, roll(part, 16 * j - at), low_side)
            high_side = jnp.where(here, roll(part, 16 * j - at - m + H + 1), high_side)
        send(base + t, low_side, high_side)


def kron(vertical, transposed):
    Z = 16
    i = lax.broadcasted_iota(jnp.int32, (LANES, Z), 0)
    a = lax.broadcasted_iota(jnp.int32, (LANES, Z), 1)
    left = ((i // 8 if transposed else i % Z) == a).astype(F32).astype(BF16)
    b = lax.broadcasted_iota(jnp.int32, (Z, LANES), 0)
    o = lax.broadcasted_iota(jnp.int32, (Z, LANES), 1)
    right = (o % Z == b).astype(F32).astype(BF16)
    p = lax.broadcasted_iota(jnp.int32, (LANES, LANES), 0)
    q = lax.broadcasted_iota(jnp.int32, (LANES, LANES), 1)
    mask = (p % 8 if transposed else p // Z) == q // Z
    return [jnp.where(mask, mm(mm(left, part).astype(BF16), right), 0.0).astype(BF16) for part in split(vertical)]


def mix(matrix, data):
    high, low = split(data)
    return mm(matrix[0], high) + mm(matrix[0], low) + mm(matrix[1], high)


def finish(geo, *refs):
    Z, R, M, bases, frames = geo["Z"], geo["R"], geo["M"], geo["bases"], geo["frames"]
    it = iter(refs)
    take = lambda count: [next(it) for _ in range(count)]
    eastward, factors = take(2)
    joined = take(LEVELS)
    wide, gain = take(LEVELS), take(LEVELS)
    got_x, got_y, gain0, widths0, vertical, table, shifts = take(7)
    (out,) = take(1)
    got_low, got_high, ext, passed, north, result, spread, wf, gf, cf, north0, edge = take(12)
    e, n = lax.axis_index("east"), lax.axis_index("north")
    has_low, has_high = e > 0, e < geo["E"] - 1
    north_even = n % 2 == 0
    got_low[...] = jnp.where(north_even, got_y[...], got_x[...])
    got_high[...] = jnp.where(north_even, got_x[...], got_y[...])
    lane = lanes_of(Z)
    lane8 = lanes_of(8)
    per = LANES // H
    base = geo["coarse_tiles"] + R // per
    levels = range(1, LEVELS + 1)
    rows_of = [R >> l for l in levels]
    starts = lambda more: [sum(rows_of[:l]) + l * more for l in range(LEVELS + 1)]
    ext_at = starts(2 * H + 2)
    out_at = starts(2)
    width_at = starts(2 * H)
    for l in range(LEVELS):
        r, m, at = R >> (l + 1), M >> (l + 1), frames[l + 1]
        for source, target, j in ((wide[l], wf, l), (gain[l], gf, LEVELS + l)):
            for c in range(0, r + 2 * H, 8):
                t, row = base + c // Z, c % Z
                low_side = roll(got_low[t, row : row + 8, :], at - H - 1 - 16 * j)
                high_side = roll(got_high[t, row : row + 8, :], at + m - 16 * j)
                joint = jnp.where(lane8 < at, low_side, jnp.where(lane8 < at + m, source[pl.ds(c, 8), :], high_side))
                target[pl.ds(width_at[l] + c, 8), :] = jnp.where((lane8 >= at - H - 1) & (lane8 < at + m + H + 1), joint, 0.0)
        for i in range(r + 2 * H + 2):
            t, s = divmod(ext_at[l] + i, PER_TILE)
            own = roll(joined[l][i], at - 1 - bases[l])
            low_side = roll(got_low[t], at - H - 1 - SLOT * s)
            high_side = roll(got_high[t], at + m - 1 - SLOT * s)
            ext[ext_at[l] + i] = (
                jnp.where((lane >= at - 1) & (lane < at + m + 1), own, 0.0)
                + jnp.where((lane >= at - H - 1) & (lane < at + 1), low_side, 0.0)
                + jnp.where((lane >= at + m - 1) & (lane < at + m + H + 1), high_side, 0.0)
            )
    for k, a in enumerate(taps(wf[...])):
        cf[k] = a
    for l in range(LEVELS):
        r = R >> (l + 1)
        east_rows(ext, cf, passed, r + 2, 2, width_at[l] + H - 1, ext_at[l], out_at[l])

    def north_rows(source, target, rows, factor):
        data = source[pl.ds(rows[0], len(rows))].reshape(len(rows) * Z, LANES)
        pair = jnp.concatenate(split(data), axis=1)
        for k in range(1, H + 1, 2):
            moved = mm(pair, shifts[:, (k - 1) * LANES : (k + 1) * LANES])
            for i, x in enumerate(rows):
                here = moved[i * Z : (i + 1) * Z]
                before = factor(0, x) * source[x] if k == 1 else target[x]
                target[x] = before + factor(k, x) * here[:, :LANES] + factor(k + 1, x) * here[:, LANES:]

    total = out_at[-1]

    def coarse_factor(k, x):
        l = max(i for i in range(LEVELS) if out_at[i] <= x)
        return cf[k, pl.ds(width_at[l] + H - 1 + x - out_at[l], 1), :]

    half = -(-total // 2)
    north_rows(passed, north, range(0, half), coarse_factor)
    north_rows(passed, north, range(half, total), coarse_factor)
    for l in range(LEVELS - 1, -1, -1):
        r, m, at = R >> (l + 1), M >> (l + 1), frames[l + 1]
        groups = (r + 2 + 7) // 8
        matrix = kron(vertical[l + 1] * 4.0 ** (l + 1), False)
        for g in range(groups):
            have = min(8, r + 2 - 8 * g)
            data = north[out_at[l] + 8 * g : out_at[l] + 8 * g + have].reshape(have * Z, LANES)
            if have < 8:
                data = jnp.concatenate([data, jnp.zeros(((8 - have) * Z, LANES), F32)], axis=0)
            mixed = mix(matrix, data)
            for i in range(have):
                row = 8 * g + i
                result[row] = gf[pl.ds(width_at[l] + row + H - 1, 1), :] * mixed[i * Z : (i + 1) * Z]
        if l < LEVELS - 1:
            inside = ((lane >= at) | (n > 0)) & ((lane < at + m) | (n < geo["N"] - 1))
            for row in range(-1, r + 1):
                j = row // 2
                other = j + (1 if row % 2 else -1)
                summed = result[row + 1] + 0.75 * spread[j + 1] + 0.25 * spread[other + 1]
                keep = inside
                if row == -1:
                    keep = keep & has_low
                if row == r:
                    keep = keep & has_high
                result[row + 1] = jnp.where(keep, summed, 0.0)
        flat = result.reshape(result.shape[0] * Z, LANES)
        spread_flat = spread.reshape(spread.shape[0] * Z, LANES)
        spread_flat[pl.ds(0, (r + 2) * Z), :] = dot_exact(flat[pl.ds(0, (r + 2) * Z), :], table[l])
    slot = lane8 % (2 * H)
    width = jnp.zeros((H, LANES), F32)
    for s in range(H):
        rows = widths0[pl.ds(s, R // H, stride=H), :].astype(F32)
        width = jnp.where(lane8 // (2 * H) == s, roll(rows, 2 * H * s + H), width)
    edge_taps = [jnp.where((slot >= H - k) & (slot < H + k), a, 0.0) for k, a in enumerate(taps(width))]
    low_half = lane % (2 * H) < H
    for t in range(R // H):
        tile = geo["coarse_tiles"] + t // 2
        low_side, high_side = got_low[tile], got_high[tile]
        if t % 2:
            low_side = roll(low_side, -H)
        else:
            high_side = roll(high_side, H)
        halo = jnp.where(low_half, low_side, high_side)
        summed = jnp.zeros((Z, LANES), F32)
        for k in range(1, H + 1):
            summed = summed + edge_taps[k][t : t + 1] * jnp.where(low_half, roll(halo, -k), roll(halo, k))
        edge[t] = summed
    matrix = kron(vertical[0], True)
    widen = table[LEVELS][:, 0 : 6 * Z]
    factor0 = lambda k, x: factors[k, pl.ds(x, 1), :]
    for x0 in range(0, R, R // 2):
        north_rows(eastward, north0, range(x0, x0 + R // 2), factor0)
    at_edge = (lane < H) | (lane >= M - H)
    for b in range(R // 8):
        for i in range(8):
            x = 8 * b + i
            north0[x] = north0[x] + jnp.where(at_edge, roll(edge[b], M - H - 2 * H * i), 0.0)
        mixed = mix(matrix, north0[8 * b : 8 * b + 8].reshape(8 * Z, LANES))
        high, low = split(spread[4 * b : 4 * b + 6].reshape(6 * Z, LANES))
        added = mm(widen, high) + mm(widen, low)
        weight = gain0[pl.ds(8 * b, 8), :]
        for z in range(Z):
            out[z, pl.ds(8 * b, 8), :] = weight * mixed[z * 8 : z * 8 + 8] + added[z * 8 : z * 8 + 8]


def swap(x, axis, first, by=1):
    count = lax.axis_size(axis)
    route = []
    for i in range(count - by):
        if (i // by) % 2 == first:
            route += [(i, i + by), (i + by, i)]
    return lax.ppermute(x, axis, route)


def body(inc, w0, w1, w2, w3, g0, g1, g2, g3, vertical):
    Z, R, M = inc.shape
    bases, frames, down, up, shifts = tables(R, M)
    total_rows = sum((R >> l) + 2 * H + 2 for l in range(1, LEVELS + 1))
    geo = dict(
        Z=Z, R=R, M=M, bases=bases, frames=frames, E=lax.axis_size("east"), N=lax.axis_size("north"),
        coarse_tiles=-(-total_rows // PER_TILE),
    )
    shape = lambda *dims: jax.ShapeDtypeStruct(dims, F32)
    levels = range(1, LEVELS + 1)
    params = pltpu.CompilerParams(vmem_limit_bytes=48 * 1024 * 1024)
    east_tiles = H + SLOT + 1
    given = (inc, jnp.asarray(down), w1, w2, w3, g1, g2, g3)
    outs = pl.pallas_call(
        functools.partial(prepare, geo),
        out_shape=[shape(R, Z, M)] + [shape((R >> l) + 2, Z, M) for l in levels]
        + [shape(east_tiles, Z, M)] * 2 + [shape(2, Z, M)] * 2,
        in_specs=[pl.BlockSpec(memory_space=pltpu.HBM)] * len(given),
        scratch_shapes=[pltpu.VMEM((R, Z, M), F32)] + [pltpu.VMEM(x.shape, x.dtype) for x in given]
        + [pltpu.SemaphoreType.DMA((len(given),))],
        compiler_params=params,
    )(*[pltpu.with_memory_space_constraint(x, pltpu.HBM) for x in given])
    field, coarse, sends = outs[0], outs[1 : 1 + LEVELS], outs[1 + LEVELS :]
    got_b = swap(sends[1], "east", 1)
    got_a = swap(sends[0], "east", 0)
    got_c = swap(sends[2], "east", 0, 2)
    got_d = swap(sends[3], "east", 1, 2)
    wide_shapes = [shape((R >> l) + 2 * H, M) for l in levels]
    north_tiles = geo["coarse_tiles"] + R * H // LANES + wide_shapes[0].shape[0] // Z
    outs = pl.pallas_call(
        functools.partial(middle, geo),
        out_shape=[shape(R, Z, M), shape(H + 1, R, M)]
        + [shape((R >> l) + 2 * H + 2, Z, M) for l in levels]
        + [shape(north_tiles, Z, M)] * 2 + wide_shapes * 2,
        scratch_shapes=[pltpu.VMEM((R + 2 * H, Z, M), F32)],
        compiler_params=params,
    )(field, *coarse, got_a, got_b, got_c, got_d, w0, w1, w2, w3, g1, g2, g3)
    eastward, factors = outs[0], outs[1]
    joined, (send_x, send_y) = outs[2 : 2 + LEVELS], outs[2 + LEVELS : 4 + LEVELS]
    wide, gain = outs[4 + LEVELS : 4 + 2 * LEVELS], outs[4 + 2 * LEVELS :]
    got_x = swap(send_x, "north", 0)
    got_y = swap(send_y, "north", 1)
    rows1 = (R >> 1) + 2
    out_rows = sum((R >> l) + 2 for l in levels)
    width_rows = out_rows + LEVELS * (2 * H - 2)
    return pl.pallas_call(
        functools.partial(finish, geo),
        out_shape=shape(Z, R, M),
        scratch_shapes=[
            pltpu.VMEM(dims, F32)
            for dims in (
                (north_tiles, Z, M), (north_tiles, Z, M), (total_rows, Z, M), (out_rows, Z, M), (out_rows, Z, M),
                (rows1, Z, M), (rows1, Z, M), (width_rows, M), (width_rows, M), (H + 1, width_rows, M),
                (R, Z, M), (R // H, Z, M),
            )
        ],
        compiler_params=params,
    )(eastward, factors, *joined, *wide, *gain, got_x, got_y, g0, w0, vertical, jnp.asarray(up), jnp.asarray(shifts))


def solution(mesh):
    tile = P("east", "north")
    return jax.shard_map(
        body,
        mesh=mesh,
        in_specs=(P(None, "east", "north"), *([tile] * 8), P()),
        out_specs=P(None, "east", "north"),
        check_vma=False,
    )
```

```python
import functools

import jax
import jax.numpy as jnp
import numpy as np
from jax import lax
from jax.experimental import pallas as pl
from jax.experimental.pallas import tpu as pltpu
from jax.sharding import PartitionSpec as P

H = 8
LANES = 128
LEVELS = 3
F32 = jnp.float32
BF16 = jnp.bfloat16
SLOT = H + 2
PER_TILE = LANES // SLOT


def tables(rows, cols):
    bases, at = [], H
    for l in range(1, LEVELS + 1):
        bases.append(at)
        at += (cols >> l) + 2
    assert at <= LANES and cols == LANES
    down = np.zeros((4, cols, LANES), np.float32)
    for variant in range(4):
        current = np.eye(cols)
        low = 0
        for l in range(1, LEVELS + 1):
            m = cols >> l
            step = np.zeros((current.shape[1], m + 2))
            for j in range(-1, m + 1):
                for f, w in ((2 * j, 0.375), (2 * j + 1, 0.375), (2 * j - 1, 0.125), (2 * j + 2, 0.125)):
                    if 0 <= f - low < current.shape[1]:
                        step[f - low, j + 1] += w
            current = current @ step
            if variant & 1:
                current[:, 0] = 0
            if variant & 2:
                current[:, -1] = 0
            low = -1
            down[variant, :, bases[l - 1] : bases[l - 1] + m + 2] = current
    frames = [0]
    for l in range(1, LEVELS + 1):
        own = bases[l - 1] + 1
        frames.append(own if own + (cols >> l) + H < LANES else H + 1)
    up = np.zeros((LEVELS + 1, LANES, LANES), np.float32)
    for l in range(LEVELS):
        m = cols >> l
        for f in range(-1, m + 1) if l else range(m):
            j = f // 2
            out, at = f + frames[l], frames[l + 1]
            up[l, j + at, out] += 0.75
            up[l, j + (1 if f % 2 else -1) + at, out] += 0.25
    for z in range(16):
        for i in range(8):
            j = i // 2 + 1
            up[LEVELS, z * 8 + i, j * 16 + z] += 0.75
            up[LEVELS, z * 8 + i, (j + (1 if i % 2 else -1)) * 16 + z] += 0.25
    for t in (down, up):
        assert (t == t.astype(jnp.bfloat16).astype(np.float32)).all()
    shifts = np.concatenate([np.eye(LANES, k=k) + np.eye(LANES, k=-k) for k in range(1, H + 1)], axis=1)
    shifts = np.concatenate([shifts, shifts], axis=0)
    return bases, frames, down.astype(jnp.bfloat16), up.astype(jnp.bfloat16), shifts.astype(jnp.bfloat16)


def split(x):
    high = x.astype(BF16)
    return high, (x - high.astype(F32)).astype(BF16)


def mm(a, b):
    return jnp.dot(a, b, preferred_element_type=F32)


def dot_exact(x, weights):
    high, low = split(x)
    return mm(high, weights) + mm(low, weights)


def lanes_of(rows):
    return lax.broadcasted_iota(jnp.int32, (rows, LANES), 1)


def roll(x, shift):
    shift %= LANES
    return pltpu.roll(x, shift, 1) if shift else x


def taps(widths):
    grown = widths + 1.0
    inverse = 1.0 / (grown * grown)
    profile = [jnp.square(jnp.maximum(1.0 - float(k * k) * inverse, 0.0)) for k in range(1, H + 1)]
    total = profile[0]
    for p in profile[1:]:
        total = total + p
    scale = 1.0 / (1.0 + 2.0 * total)
    return [scale] + [p * scale for p in profile]


def prepare(geo, *refs):
    count = 2 * LEVELS + 2
    outside, (field, *rest) = refs[:count], refs[count:]
    coarse, (send_a, send_b, send_c, half, *inside) = rest[:LEVELS], rest[LEVELS:]
    sems = inside.pop()
    copies = [pltpu.make_async_copy(a, b, sems.at[i]) for i, (a, b) in enumerate(zip(outside, inside))]
    for copy in copies:
        copy.start()
    inc, table, *small = inside
    widths, gains = small[:LEVELS], small[LEVELS:]
    Z, R, M, bases = geo["Z"], geo["R"], geo["M"], geo["bases"]
    e, n = lax.axis_index("east"), lax.axis_index("north")
    has_low, has_high = e > 0, e < geo["E"] - 1
    even = e % 2 == 0
    flat = field.reshape(R * Z, M)
    for copy in copies:
        copy.wait()
    for z in range(Z):
        flat[pl.ds(z, R, stride=Z), :] = inc[z]
    variant = (n == 0).astype(jnp.int32) + 2 * (n == geo["N"] - 1).astype(jnp.int32)
    weights = table[variant]
    half_flat = half.reshape(R * Z, M)
    chunk = R * Z // 4
    for c in range(4):
        half_flat[pl.ds(c * chunk, chunk), :] = dot_exact(flat[pl.ds(c * chunk, chunk), :], weights)
    source, low, top = half, 0, R
    for l in range(1, LEVELS + 1):
        r, out = R >> l, coarse[l - 1]

        def get(i, source=source, low=low, top=top):
            return source[i - low] if low <= i < top else None

        for j in range(-1, r + 1):
            total = None
            for pair, w in (((2 * j, 2 * j + 1), 0.375), ((2 * j - 1, 2 * j + 2), 0.125)):
                terms = [t for t in (get(i) for i in pair) if t is not None]
                if terms:
                    part = w * functools.reduce(jnp.add, terms)
                    total = part if total is None else total + part
            if j == -1:
                total = jnp.where(has_low, total, 0.0)
            if j == r:
                total = jnp.where(has_high, total, 0.0)
            out[j + 1] = total
        source, low, top = out, -1, r + 1
    start = R - H
    send_a[0:H] = field[pl.ds(jnp.where(even, start, 0), H)]
    send_b[0:H] = field[pl.ds(jnp.where(even, 0, start), H)]
    lane = lanes_of(Z)
    for i in range(SLOT):
        def merged(picks):
            out = coarse[LEVELS - 1][picks[LEVELS - 1]]
            for l in range(LEVELS - 1, 0, -1):
                out = jnp.where(lane < bases[l], coarse[l - 1][picks[l - 1]], out)
            return out

        lower = merged([i] * LEVELS)
        upper = merged([(R >> l) - H + i for l in range(1, LEVELS + 1)])
        send_a[H + i] = jnp.where(even, upper, lower)
        send_b[H + i] = jnp.where(even, lower, upper)
    last = H + SLOT
    send_a[last] = jnp.zeros((Z, LANES), F32)
    send_b[last] = jnp.zeros((Z, LANES), F32)
    for j, ref in enumerate((*widths, *gains)):
        r, m = ref.shape
        lower = ref[pl.ds(0, 1), :].astype(F32)
        upper = ref[pl.ds(r - 1, 1), :].astype(F32)
        send_a[last, pl.ds(j, 1), pl.ds(0, m)] = jnp.where(even, upper, lower)
        send_b[last, pl.ds(j, 1), pl.ds(0, m)] = jnp.where(even, lower, upper)
    r = R >> LEVELS
    for i in range(2):
        send_c[i] = jnp.where(even, coarse[LEVELS - 1][r + i], coarse[LEVELS - 1][i])


def east_rows(source, factors, out, count, block, factor_at=0, source_at=0, out_at=0):
    def step(b, carry):
        x0 = b * block
        rows = [source[x0 + i + source_at] for i in range(block + 2 * H)]
        for i in range(block):
            def factor(k):
                return factors[k, pl.ds(x0 + i + factor_at, 1), :]

            total = factor(0) * rows[i + H]
            for k in range(1, H + 1):
                total = total + factor(k) * (rows[i + H + k] + rows[i + H - k])
            out[x0 + i + out_at] = total
        return carry

    lax.fori_loop(0, count // block, step, 0)


def interior(geo, field, widths0, factors, inner):
    for k, a in enumerate(taps(widths0[...].astype(F32))):
        factors[k] = a
    east_rows(field, factors, inner, geo["R"] - 2 * H, 4, H)


def middle(geo, *refs):
    Z, R, M, bases = geo["Z"], geo["R"], geo["M"], geo["bases"]
    it = iter(refs)
    take = lambda count: [next(it) for _ in range(count)]
    (field,) = take(1)
    coarse = take(LEVELS)
    got_a, got_b, got_c, got_d, factors, inner = take(6)
    widths, gains = take(LEVELS), take(LEVELS)
    (eastward,) = take(1)
    joined = take(LEVELS)
    send_x, send_y = take(2)
    wide, gain = take(LEVELS), take(LEVELS)
    below, above = take(2)
    e, n = lax.axis_index("east"), lax.axis_index("north")
    even = e % 2 == 0
    below[0:H] = jnp.where(even, got_b[0:H], got_a[0:H])
    below[H : 3 * H] = field[0 : 2 * H]
    above[0 : 2 * H] = field[R - 2 * H : R]
    above[2 * H : 3 * H] = jnp.where(even, got_a[0:H], got_b[0:H])
    east_rows(below, factors, eastward, H, 4)
    east_rows(above, factors, eastward, H, 4, R - H, 0, R - H)
    eastward[H : R - H] = inner[...]
    for l in range(1, LEVELS + 1):
        r, out, own = R >> l, joined[l - 1], coarse[l - 1]
        out[H : H + r + 2] = own[...]
        out[0:H] = jnp.zeros((H, Z, LANES), F32)
        out[H + r + 2 : 2 * H + r + 2] = jnp.zeros((H, Z, LANES), F32)
    for i in range(SLOT):
        a, b = got_a[H + i], got_b[H + i]
        lower, upper = jnp.where(even, b, a), jnp.where(even, a, b)
        for l in range(1, LEVELS + 1):
            r, out = R >> l, joined[l - 1]
            out[i] = out[i] + lower
            out[r + H + i] = out[r + H + i] + upper
    r, out = R >> LEVELS, joined[LEVELS - 1]
    for i in range(2):
        far = got_c[i]
        out[i] = out[i] + jnp.where(even, far, got_d[H + r + i])
        out[r + 2 * H + i] = out[r + 2 * H + i] + jnp.where(even, got_d[H + i], far)
    last = H + SLOT
    rows_a, rows_b = got_a[last], got_b[last]
    lower, upper = jnp.where(even, rows_b, rows_a), jnp.where(even, rows_a, rows_b)
    for j, (own, out) in enumerate(zip((*widths, *gains), (*wide, *gain))):
        r, m = own.shape
        out[...] = jnp.zeros(out.shape, F32)
        at = geo["frames"][j % LEVELS + 1]
        out[pl.ds(H, r), pl.ds(at, m)] = own[...].astype(F32)
        out[pl.ds(H - 1, 1), pl.ds(at, m)] = lower[j : j + 1, 0:m]
        out[pl.ds(H + r, 1), pl.ds(at, m)] = upper[j : j + 1, 0:m]
    north_even = n % 2 == 0
    lane = lanes_of(Z)

    def send(t, low_side, high_side):
        send_x[t] = jnp.where(north_even, high_side, low_side)
        send_y[t] = jnp.where(north_even, low_side, high_side)

    zero = jnp.zeros((Z, LANES), F32)
    todo = [(l, i) for l in range(LEVELS) for i in range(joined[l].shape[0])]
    for t in range(geo["coarse_tiles"]):
        low_side, high_side = zero, zero
        for s, (l, i) in enumerate(todo[t * PER_TILE : (t + 1) * PER_TILE]):
            row, m = joined[l][i], M >> (l + 1)
            here = (lane >= SLOT * s) & (lane < SLOT * (s + 1))
            low_side = jnp.where(here, roll(row, SLOT * s - bases[l]), low_side)
            high_side = jnp.where(here, roll(row, SLOT * s - bases[l] - m + H), high_side)
        send(t, low_side, high_side)
    per = LANES // H
    for t in range(R // per):
        low_side, high_side = zero, zero
        for s in range(per):
            row, at = eastward[t * per + s], 2 * H * (s % H) + H * (s // H)
            here = (lane >= at) & (lane < at + H)
            low_side = jnp.where(here, roll(row, at), low_side)
            high_side = jnp.where(here, roll(row, at - M + H), high_side)
        send(geo["coarse_tiles"] + t, low_side, high_side)
    low_side, high_side, q = zero, zero, 0
    for l in range(LEVELS):
        rows, m, at = wide[l].shape[0], M >> (l + 1), geo["frames"][l + 1]
        for c in range(0, rows, Z):
            have = min(rows - c, Z)
            width, weight = wide[l][pl.ds(c, have), :], gain[l][pl.ds(c, have), :]
            if have < Z:
                fill = jnp.zeros((Z - have, LANES), F32)
                width, weight = jnp.concatenate([width, fill], axis=0), jnp.concatenate([weight, fill], axis=0)
            begin = SLOT * q
            here, last_lane = (lane >= begin) & (lane < begin + H + 1), lane == begin + H + 1
            low_side = jnp.where(here, roll(width, begin - at), low_side)
            low_side = jnp.where(last_lane, roll(weight, begin + H + 1 - at), low_side)
            high_side = jnp.where(here, roll(width, begin - at - m + H + 1), high_side)
            high_side = jnp.where(last_lane, roll(weight, begin + H + 2 - at - m), high_side)
            q += 1
    send(geo["coarse_tiles"] + R // per, low_side, high_side)


def own_north(geo, eastward, factors, shifts, out):
    R = geo["R"]
    for x0 in range(0, R, R // 2):
        north_rows(eastward, out, range(x0, x0 + R // 2), lambda k, x: factors[k, pl.ds(x, 1), :], shifts)


def north_rows(source, target, rows, factor, shifts):
    Z = source.shape[1]
    data = source[pl.ds(rows[0], len(rows))].reshape(len(rows) * Z, LANES)
    pair = jnp.concatenate(split(data), axis=1)
    for k in range(1, H + 1, 2):
        moved = mm(pair, shifts[:, (k - 1) * LANES : (k + 1) * LANES])
        for i, x in enumerate(rows):
            here = moved[i * Z : (i + 1) * Z]
            before = factor(0, x) * source[x] if k == 1 else target[x]
            target[x] = before + factor(k, x) * here[:, :LANES] + factor(k + 1, x) * here[:, LANES:]


def kron(vertical, transposed):
    Z = 16
    i = lax.broadcasted_iota(jnp.int32, (LANES, Z), 0)
    a = lax.broadcasted_iota(jnp.int32, (LANES, Z), 1)
    left = ((i // 8 if transposed else i % Z) == a).astype(F32).astype(BF16)
    b = lax.broadcasted_iota(jnp.int32, (Z, LANES), 0)
    o = lax.broadcasted_iota(jnp.int32, (Z, LANES), 1)
    right = (o % Z == b).astype(F32).astype(BF16)
    p = lax.broadcasted_iota(jnp.int32, (LANES, LANES), 0)
    q = lax.broadcasted_iota(jnp.int32, (LANES, LANES), 1)
    mask = (p % 8 if transposed else p // Z) == q // Z
    return [jnp.where(mask, mm(mm(left, part).astype(BF16), right), 0.0).astype(BF16) for part in split(vertical)]


def mix(matrix, data):
    high, low = split(data)
    return mm(matrix[0], high) + mm(matrix[0], low) + mm(matrix[1], high)


def finish(geo, *refs):
    Z, R, M, bases, frames = geo["Z"], geo["R"], geo["M"], geo["bases"], geo["frames"]
    it = iter(refs)
    take = lambda count: [next(it) for _ in range(count)]
    (north0,) = take(1)
    joined = take(LEVELS)
    wide, gain = take(LEVELS), take(LEVELS)
    got_x, got_y, gain0, widths0, vertical, table, shifts = take(7)
    (out,) = take(1)
    got_low, got_high, ext, passed, north, result, spread, wf, gf, cf, edge = take(11)
    e, n = lax.axis_index("east"), lax.axis_index("north")
    has_low, has_high = e > 0, e < geo["E"] - 1
    north_even = n % 2 == 0
    got_low[...] = jnp.where(north_even, got_y[...], got_x[...])
    got_high[...] = jnp.where(north_even, got_x[...], got_y[...])
    lane = lanes_of(Z)
    lane8 = lanes_of(8)
    per = LANES // H
    base = geo["coarse_tiles"] + R // per
    levels = range(1, LEVELS + 1)
    rows_of = [R >> l for l in levels]
    starts = lambda more: [sum(rows_of[:l]) + l * more for l in range(LEVELS + 1)]
    ext_at = starts(2 * H + 2)
    out_at = starts(2)
    width_at = starts(2 * H)
    for l in range(LEVELS):
        r, m, at = R >> (l + 1), M >> (l + 1), frames[l + 1]
        for c in range(0, r + 2 * H, 8):
            row = c % Z
            begin = SLOT * (sum(-(-(R >> i) // Z) + 1 for i in range(1, l + 1)) + c // Z)
            lower, upper = got_low[base, row : row + 8, :], got_high[base, row : row + 8, :]
            width = jnp.where(
                lane8 < at,
                roll(lower, at - H - 1 - begin),
                jnp.where(lane8 < at + m, wide[l][pl.ds(c, 8), :], roll(upper, at + m - begin)),
            )
            wf[pl.ds(width_at[l] + c, 8), :] = jnp.where((lane8 >= at - H - 1) & (lane8 < at + m + H + 1), width, 0.0)
            weight = jnp.where(lane8 == at - 1, roll(lower, at - H - 2 - begin), gain[l][pl.ds(c, 8), :])
            gf[pl.ds(width_at[l] + c, 8), :] = jnp.where(lane8 == at + m, roll(upper, at + m - H - 1 - begin), weight)
        for i in range(r + 2 * H + 2):
            t, s = divmod(ext_at[l] + i, PER_TILE)
            own = roll(joined[l][i], at - 1 - bases[l])
            low_side = roll(got_low[t], at - H - 1 - SLOT * s)
            high_side = roll(got_high[t], at + m - 1 - SLOT * s)
            ext[ext_at[l] + i] = (
                jnp.where((lane >= at - 1) & (lane < at + m + 1), own, 0.0)
                + jnp.where((lane >= at - H - 1) & (lane < at + 1), low_side, 0.0)
                + jnp.where((lane >= at + m - 1) & (lane < at + m + H + 1), high_side, 0.0)
            )
    for k, a in enumerate(taps(wf[...])):
        cf[k] = a
    for l in range(LEVELS):
        r = R >> (l + 1)
        east_rows(ext, cf, passed, r + 2, 2, width_at[l] + H - 1, ext_at[l], out_at[l])

    total = out_at[-1]

    def coarse_factor(k, x):
        l = max(i for i in range(LEVELS) if out_at[i] <= x)
        return cf[k, pl.ds(width_at[l] + H - 1 + x - out_at[l], 1), :]

    half = -(-total // 2)
    north_rows(passed, north, range(0, half), coarse_factor, shifts)
    north_rows(passed, north, range(half, total), coarse_factor, shifts)
    for l in range(LEVELS - 1, -1, -1):
        r, m, at = R >> (l + 1), M >> (l + 1), frames[l + 1]
        groups = (r + 2 + 7) // 8
        matrix = kron(vertical[l + 1] * 4.0 ** (l + 1), False)
        for g in range(groups):
            have = min(8, r + 2 - 8 * g)
            data = north[out_at[l] + 8 * g : out_at[l] + 8 * g + have].reshape(have * Z, LANES)
            if have < 8:
                data = jnp.concatenate([data, jnp.zeros(((8 - have) * Z, LANES), F32)], axis=0)
            mixed = mix(matrix, data)
            for i in range(have):
                row = 8 * g + i
                result[row] = gf[pl.ds(width_at[l] + row + H - 1, 1), :] * mixed[i * Z : (i + 1) * Z]
        if l < LEVELS - 1:
            inside = ((lane >= at) | (n > 0)) & ((lane < at + m) | (n < geo["N"] - 1))
            for row in range(-1, r + 1):
                j = row // 2
                other = j + (1 if row % 2 else -1)
                summed = result[row + 1] + 0.75 * spread[j + 1] + 0.25 * spread[other + 1]
                keep = inside
                if row == -1:
                    keep = keep & has_low
                if row == r:
                    keep = keep & has_high
                result[row + 1] = jnp.where(keep, summed, 0.0)
        flat = result.reshape(result.shape[0] * Z, LANES)
        spread_flat = spread.reshape(spread.shape[0] * Z, LANES)
        spread_flat[pl.ds(0, (r + 2) * Z), :] = dot_exact(flat[pl.ds(0, (r + 2) * Z), :], table[l])
    slot = lane8 % (2 * H)
    width = jnp.zeros((H, LANES), F32)
    for s in range(H):
        rows = widths0[pl.ds(s, R // H, stride=H), :].astype(F32)
        width = jnp.where(lane8 // (2 * H) == s, roll(rows, 2 * H * s + H), width)
    edge_taps = [jnp.where((slot >= H - k) & (slot < H + k), a, 0.0) for k, a in enumerate(taps(width))]
    low_half = lane % (2 * H) < H
    for t in range(R // H):
        tile = geo["coarse_tiles"] + t // 2
        low_side, high_side = got_low[tile], got_high[tile]
        if t % 2:
            low_side = roll(low_side, -H)
        else:
            high_side = roll(high_side, H)
        halo = jnp.where(low_half, low_side, high_side)
        summed = jnp.zeros((Z, LANES), F32)
        for k in range(1, H + 1):
            summed = summed + edge_taps[k][t : t + 1] * jnp.where(low_half, roll(halo, -k), roll(halo, k))
        edge[t] = summed
    matrix = kron(vertical[0], True)
    widen = table[LEVELS][:, 0 : 6 * Z]
    at_edge = (lane < H) | (lane >= M - H)
    for b in range(R // 8):
        rows = [north0[8 * b + i] + jnp.where(at_edge, roll(edge[b], M - H - 2 * H * i), 0.0) for i in range(8)]
        mixed = mix(matrix, jnp.concatenate(rows, axis=0))
        high, low = split(spread[4 * b : 4 * b + 6].reshape(6 * Z, LANES))
        added = mm(widen, high) + mm(widen, low)
        weight = gain0[pl.ds(8 * b, 8), :]
        for z in range(Z):
            out[z, pl.ds(8 * b, 8), :] = weight * mixed[z * 8 : z * 8 + 8] + added[z * 8 : z * 8 + 8]


def swap(x, axis, first):
    route = [(i, i + 1) for i in range(first, lax.axis_size(axis) - 1, 2)]
    return lax.ppermute(x, axis, route + [(j, i) for i, j in route])


def far(x, axis):
    count = lax.axis_size(axis)
    return lax.ppermute(x, axis, [(i, i + 2) for i in range(0, count - 2, 2)] + [(i, i - 2) for i in range(3, count, 2)])


def body(inc, w0, w1, w2, w3, g0, g1, g2, g3, vertical):
    Z, R, M = inc.shape
    bases, frames, down, up, shifts = tables(R, M)
    total_rows = sum((R >> l) + 2 * H + 2 for l in range(1, LEVELS + 1))
    geo = dict(
        Z=Z, R=R, M=M, bases=bases, frames=frames, E=lax.axis_size("east"), N=lax.axis_size("north"),
        coarse_tiles=-(-total_rows // PER_TILE),
    )
    shape = lambda *dims: jax.ShapeDtypeStruct(dims, F32)
    levels = range(1, LEVELS + 1)
    params = pltpu.CompilerParams(vmem_limit_bytes=48 * 1024 * 1024)
    east_tiles = H + SLOT + 1
    given = (inc, jnp.asarray(down), w1, w2, w3, g1, g2, g3)
    outs = pl.pallas_call(
        functools.partial(prepare, geo),
        out_shape=[shape(R, Z, M)] + [shape((R >> l) + 2, Z, M) for l in levels]
        + [shape(east_tiles, Z, M)] * 2 + [shape(2, Z, M)],
        in_specs=[pl.BlockSpec(memory_space=pltpu.HBM)] * len(given),
        scratch_shapes=[pltpu.VMEM((R, Z, M), F32)] + [pltpu.VMEM(x.shape, x.dtype) for x in given]
        + [pltpu.SemaphoreType.DMA((len(given),))],
        compiler_params=params,
    )(*[pltpu.with_memory_space_constraint(x, pltpu.HBM) for x in given])
    field, coarse, sends = outs[0], outs[1 : 1 + LEVELS], outs[1 + LEVELS :]
    got_b = swap(sends[1], "east", 1)
    got_a = swap(sends[0], "east", 0)
    got_c = far(sends[2], "east")
    forward, got_c = lax.optimization_barrier((got_b, got_c))
    got_d = swap(forward, "east", 0)
    factors, inner = pl.pallas_call(
        functools.partial(interior, geo),
        out_shape=[shape(H + 1, R, M), shape(R - 2 * H, Z, M)],
        compiler_params=params,
    )(field, w0)
    wide_shapes = [shape((R >> l) + 2 * H, M) for l in levels]
    north_tiles = geo["coarse_tiles"] + R * H // LANES + 1
    outs = pl.pallas_call(
        functools.partial(middle, geo),
        out_shape=[shape(R, Z, M)] + [shape((R >> l) + 2 * H + 2, Z, M) for l in levels]
        + [shape(north_tiles, Z, M)] * 2 + wide_shapes * 2,
        scratch_shapes=[pltpu.VMEM((3 * H, Z, M), F32)] * 2,
        compiler_params=params,
    )(field, *coarse, got_a, got_b, got_c, got_d, factors, inner, w1, w2, w3, g1, g2, g3)
    eastward = outs[0]
    joined, (send_x, send_y) = outs[1 : 1 + LEVELS], outs[1 + LEVELS : 3 + LEVELS]
    wide, gain = outs[3 + LEVELS : 3 + 2 * LEVELS], outs[3 + 2 * LEVELS :]
    got_x = swap(send_x, "north", 0)
    got_y = swap(send_y, "north", 1)
    shifts = jnp.asarray(shifts)
    north0 = pl.pallas_call(
        functools.partial(own_north, geo), out_shape=shape(R, Z, M), compiler_params=params
    )(eastward, factors, shifts)
    rows1 = (R >> 1) + 2
    out_rows = sum((R >> l) + 2 for l in levels)
    width_rows = out_rows + LEVELS * (2 * H - 2)
    return pl.pallas_call(
        functools.partial(finish, geo),
        out_shape=shape(Z, R, M),
        scratch_shapes=[
            pltpu.VMEM(dims, F32)
            for dims in (
                (north_tiles, Z, M), (north_tiles, Z, M), (total_rows, Z, M), (out_rows, Z, M), (out_rows, Z, M),
                (rows1, Z, M), (rows1, Z, M), (width_rows, M), (width_rows, M), (H + 1, width_rows, M),
                (R // H, Z, M),
            )
        ],
        compiler_params=params,
    )(north0, *joined, *wide, *gain, got_x, got_y, g0, w0, vertical, jnp.asarray(up), shifts)


def solution(mesh):
    tile = P("east", "north")
    return jax.shard_map(
        body,
        mesh=mesh,
        in_specs=(P(None, "east", "north"), *([tile] * 8), P()),
        out_specs=P(None, "east", "north"),
        check_vma=False,
    )
```

```python
import functools

import jax
import jax.numpy as jnp
import numpy as np
from jax import lax
from jax.experimental import pallas as pl
from jax.experimental.pallas import tpu as pltpu
from jax.sharding import PartitionSpec as P

H = 8
LANES = 128
LEVELS = 3
F32 = jnp.float32
BF16 = jnp.bfloat16
SLOT = H + 2
PER_TILE = LANES // SLOT


def tables(rows, cols):
    bases, at = [], H
    for l in range(1, LEVELS + 1):
        bases.append(at)
        at += (cols >> l) + 2
    assert at <= LANES and cols == LANES
    down = np.zeros((4, cols, LANES), np.float32)
    for variant in range(4):
        current = np.eye(cols)
        low = 0
        for l in range(1, LEVELS + 1):
            m = cols >> l
            step = np.zeros((current.shape[1], m + 2))
            for j in range(-1, m + 1):
                for f, w in ((2 * j, 0.375), (2 * j + 1, 0.375), (2 * j - 1, 0.125), (2 * j + 2, 0.125)):
                    if 0 <= f - low < current.shape[1]:
                        step[f - low, j + 1] += w
            current = current @ step
            if variant & 1:
                current[:, 0] = 0
            if variant & 2:
                current[:, -1] = 0
            low = -1
            down[variant, :, bases[l - 1] : bases[l - 1] + m + 2] = current
    frames = [0]
    for l in range(1, LEVELS + 1):
        own = bases[l - 1] + 1
        frames.append(own if own + (cols >> l) + H < LANES else H + 1)
    up = np.zeros((LEVELS + 1, LANES, LANES), np.float32)
    for l in range(LEVELS):
        m = cols >> l
        for f in range(-1, m + 1) if l else range(m):
            j = f // 2
            out, at = f + frames[l], frames[l + 1]
            up[l, j + at, out] += 0.75
            up[l, j + (1 if f % 2 else -1) + at, out] += 0.25
    for z in range(16):
        for i in range(8):
            j = i // 2 + 1
            up[LEVELS, z * 8 + i, j * 16 + z] += 0.75
            up[LEVELS, z * 8 + i, (j + (1 if i % 2 else -1)) * 16 + z] += 0.25
    for t in (down, up):
        assert (t == t.astype(jnp.bfloat16).astype(np.float32)).all()
    shifts = np.concatenate([np.eye(LANES, k=k) + np.eye(LANES, k=-k) for k in range(1, H + 1)], axis=1)
    shifts = np.concatenate([shifts, shifts], axis=0)
    return bases, frames, down.astype(jnp.bfloat16), up.astype(jnp.bfloat16), shifts.astype(jnp.bfloat16)


def split(x):
    high = x.astype(BF16)
    return high, (x - high.astype(F32)).astype(BF16)


def mm(a, b):
    return jnp.dot(a, b, preferred_element_type=F32)


def dot_exact(x, weights):
    high, low = split(x)
    return mm(high, weights) + mm(low, weights)


def lanes_of(rows):
    return lax.broadcasted_iota(jnp.int32, (rows, LANES), 1)


def roll(x, shift):
    shift %= LANES
    return pltpu.roll(x, shift, 1) if shift else x


def taps(widths):
    grown = widths + 1.0
    inverse = 1.0 / (grown * grown)
    profile = [jnp.square(jnp.maximum(1.0 - float(k * k) * inverse, 0.0)) for k in range(1, H + 1)]
    total = profile[0]
    for p in profile[1:]:
        total = total + p
    scale = 1.0 / (1.0 + 2.0 * total)
    return [scale] + [p * scale for p in profile]


def prepare(geo, *refs):
    count = 2
    outside, (field, *rest) = refs[:count], refs[count:]
    coarse, (send_far, half, *inside) = rest[:LEVELS], rest[LEVELS:]
    sems = inside.pop()
    copies = [pltpu.make_async_copy(a, b, sems.at[i]) for i, (a, b) in enumerate(zip(outside, inside))]
    for copy in copies:
        copy.start()
    inc, table = inside
    Z, R, M, bases = geo["Z"], geo["R"], geo["M"], geo["bases"]
    e, n = lax.axis_index("east"), lax.axis_index("north")
    has_low, has_high = e > 0, e < geo["E"] - 1
    even = e % 2 == 0
    flat = field.reshape(R * Z, M)
    for copy in copies:
        copy.wait()
    for z in range(Z):
        flat[pl.ds(z, R, stride=Z), :] = inc[z]
    variant = (n == 0).astype(jnp.int32) + 2 * (n == geo["N"] - 1).astype(jnp.int32)
    weights = table[variant]
    half_flat = half.reshape(R * Z, M)
    chunk = R * Z // 4
    for c in range(4):
        half_flat[pl.ds(c * chunk, chunk), :] = dot_exact(flat[pl.ds(c * chunk, chunk), :], weights)
    source, low, top = half, 0, R
    for l in range(1, LEVELS + 1):
        r, out = R >> l, coarse[l - 1]

        def get(i, source=source, low=low, top=top):
            return source[i - low] if low <= i < top else None

        for j in range(-1, r + 1):
            total = None
            for pair, w in (((2 * j, 2 * j + 1), 0.375), ((2 * j - 1, 2 * j + 2), 0.125)):
                terms = [t for t in (get(i) for i in pair) if t is not None]
                if terms:
                    part = w * functools.reduce(jnp.add, terms)
                    total = part if total is None else total + part
            if j == -1:
                total = jnp.where(has_low, total, 0.0)
            if j == r:
                total = jnp.where(has_high, total, 0.0)
            out[j + 1] = total
        source, low, top = out, -1, r + 1
    r = R >> LEVELS
    for i in range(2):
        send_far[i] = jnp.where(even, coarse[LEVELS - 1][r + i], coarse[LEVELS - 1][i])


def gather(geo, field, *refs):
    coarse, got_far, widths, gains, send_a, send_b = refs[:LEVELS], refs[LEVELS], refs[LEVELS + 1 : 2 * LEVELS + 1], refs[2 * LEVELS + 1 : -2], refs[-2], refs[-1]
    Z, R, M, bases = geo["Z"], geo["R"], geo["M"], geo["bases"]
    even = lax.axis_index("east") % 2 == 0
    start = R - H
    send_a[0:H] = field[pl.ds(jnp.where(even, start, 0), H)]
    send_b[0:H] = field[pl.ds(jnp.where(even, 0, start), H)]
    lane = lanes_of(Z)
    for i in range(SLOT):
        def merged(picks):
            out = coarse[LEVELS - 1][picks[LEVELS - 1]]
            for l in range(LEVELS - 1, 0, -1):
                out = jnp.where(lane < bases[l], coarse[l - 1][picks[l - 1]], out)
            return out

        lower = merged([i] * LEVELS)
        upper = merged([(R >> l) - H + i for l in range(1, LEVELS + 1)])
        send_a[H + i] = jnp.where(even, upper, lower)
        send_b[H + i] = jnp.where(even, lower, upper)
    last = H + SLOT
    send_a[last] = jnp.zeros((Z, LANES), F32)
    send_b[last] = jnp.zeros((Z, LANES), F32)
    for j, ref in enumerate((*widths, *gains)):
        r, m = ref.shape
        lower = ref[pl.ds(0, 1), :].astype(F32)
        upper = ref[pl.ds(r - 1, 1), :].astype(F32)
        send_a[last, pl.ds(j, 1), pl.ds(0, m)] = jnp.where(even, upper, lower)
        send_b[last, pl.ds(j, 1), pl.ds(0, m)] = jnp.where(even, lower, upper)
    send_b[last + 1 : last + 3] = got_far[...]


def east_rows(source, factors, out, count, block, factor_at=0, source_at=0, out_at=0):
    def step(b, carry):
        x0 = b * block
        rows = [source[x0 + i + source_at] for i in range(block + 2 * H)]
        for i in range(block):
            def factor(k):
                return factors[k, pl.ds(x0 + i + factor_at, 1), :]

            total = factor(0) * rows[i + H]
            for k in range(1, H + 1):
                total = total + factor(k) * (rows[i + H + k] + rows[i + H - k])
            out[x0 + i + out_at] = total
        return carry

    lax.fori_loop(0, count // block, step, 0)


def interior(geo, field, widths0, factors, inner):
    for k, a in enumerate(taps(widths0[...].astype(F32))):
        factors[k] = a
    east_rows(field, factors, inner, geo["R"] - 2 * H, 4, H)


def middle(geo, *refs):
    Z, R, M, bases = geo["Z"], geo["R"], geo["M"], geo["bases"]
    it = iter(refs)
    take = lambda count: [next(it) for _ in range(count)]
    (field,) = take(1)
    coarse = take(LEVELS)
    got_a, got_b, got_d, factors, inner = take(5)
    widths, gains = take(LEVELS), take(LEVELS)
    (eastward,) = take(1)
    joined = take(LEVELS)
    send_x, send_y = take(2)
    wide, gain = take(LEVELS), take(LEVELS)
    below, above = take(2)
    e, n = lax.axis_index("east"), lax.axis_index("north")
    even = e % 2 == 0
    below[0:H] = jnp.where(even, got_b[0:H], got_a[0:H])
    below[H : 3 * H] = field[0 : 2 * H]
    above[0 : 2 * H] = field[R - 2 * H : R]
    above[2 * H : 3 * H] = jnp.where(even, got_a[0:H], got_b[0:H])
    east_rows(below, factors, eastward, H, 4)
    east_rows(above, factors, eastward, H, 4, R - H, 0, R - H)
    eastward[H : R - H] = inner[...]
    for l in range(1, LEVELS + 1):
        r, out, own = R >> l, joined[l - 1], coarse[l - 1]
        out[H : H + r + 2] = own[...]
        out[0:H] = jnp.zeros((H, Z, LANES), F32)
        out[H + r + 2 : 2 * H + r + 2] = jnp.zeros((H, Z, LANES), F32)
    for i in range(SLOT):
        a, b = got_a[H + i], got_b[H + i]
        lower, upper = jnp.where(even, b, a), jnp.where(even, a, b)
        for l in range(1, LEVELS + 1):
            r, out = R >> l, joined[l - 1]
            out[i] = out[i] + lower
            out[r + H + i] = out[r + H + i] + upper
    r, out = R >> LEVELS, joined[LEVELS - 1]
    for i in range(2):
        far = got_b[H + SLOT + 1 + i]
        out[i] = out[i] + jnp.where(even, far, got_d[H + r + i])
        out[r + 2 * H + i] = out[r + 2 * H + i] + jnp.where(even, got_d[H + i], far)
    last = H + SLOT
    rows_a, rows_b = got_a[last], got_b[last]
    lower, upper = jnp.where(even, rows_b, rows_a), jnp.where(even, rows_a, rows_b)
    for j, (own, out) in enumerate(zip((*widths, *gains), (*wide, *gain))):
        r, m = own.shape
        out[...] = jnp.zeros(out.shape, F32)
        at = geo["frames"][j % LEVELS + 1]
        out[pl.ds(H, r), pl.ds(at, m)] = own[...].astype(F32)
        out[pl.ds(H - 1, 1), pl.ds(at, m)] = lower[j : j + 1, 0:m]
        out[pl.ds(H + r, 1), pl.ds(at, m)] = upper[j : j + 1, 0:m]
    north_even = n % 2 == 0
    lane = lanes_of(Z)

    def send(t, low_side, high_side):
        send_x[t] = jnp.where(north_even, high_side, low_side)
        send_y[t] = jnp.where(north_even, low_side, high_side)

    zero = jnp.zeros((Z, LANES), F32)
    todo = [(l, i) for l in range(LEVELS) for i in range(joined[l].shape[0])]
    for t in range(geo["coarse_tiles"]):
        low_side, high_side = zero, zero
        for s, (l, i) in enumerate(todo[t * PER_TILE : (t + 1) * PER_TILE]):
            row, m = joined[l][i], M >> (l + 1)
            here = (lane >= SLOT * s) & (lane < SLOT * (s + 1))
            low_side = jnp.where(here, roll(row, SLOT * s - bases[l]), low_side)
            high_side = jnp.where(here, roll(row, SLOT * s - bases[l] - m + H), high_side)
        send(t, low_side, high_side)
    per = LANES // H
    for t in range(R // per):
        low_side, high_side = zero, zero
        for s in range(per):
            row, at = eastward[t * per + s], 2 * H * (H - 1 - s % H) + H * (s // H)
            here = (lane >= at) & (lane < at + H)
            low_side = jnp.where(here, roll(row, at), low_side)
            high_side = jnp.where(here, roll(row, at - M + H), high_side)
        send(geo["coarse_tiles"] + t, low_side, high_side)
    low_side, high_side, q = zero, zero, 0
    for l in range(LEVELS):
        rows, m, at = wide[l].shape[0], M >> (l + 1), geo["frames"][l + 1]
        for c in range(0, rows, Z):
            have = min(rows - c, Z)
            width, weight = wide[l][pl.ds(c, have), :], gain[l][pl.ds(c, have), :]
            if have < Z:
                fill = jnp.zeros((Z - have, LANES), F32)
                width, weight = jnp.concatenate([width, fill], axis=0), jnp.concatenate([weight, fill], axis=0)
            begin = SLOT * q
            here, last_lane = (lane >= begin) & (lane < begin + H + 1), lane == begin + H + 1
            low_side = jnp.where(here, roll(width, begin - at), low_side)
            low_side = jnp.where(last_lane, roll(weight, begin + H + 1 - at), low_side)
            high_side = jnp.where(here, roll(width, begin - at - m + H + 1), high_side)
            high_side = jnp.where(last_lane, roll(weight, begin + H + 2 - at - m), high_side)
            q += 1
    send(geo["coarse_tiles"] + R // per, low_side, high_side)


def own_north(geo, eastward, factors, shifts, widths0, vertical, mixed, matrices, edge_taps, north):
    R, Z = geo["R"], geo["Z"]
    for x0 in range(0, R, R // 2):
        north_rows(eastward, north, range(x0, x0 + R // 2), lambda k, x: factors[k, pl.ds(x, 1), :], shifts)
    matrix = kron(vertical[0], True)
    for b in range(R // 8):
        mixed[b] = mix(matrix, north[8 * b : 8 * b + 8].reshape(8 * Z, LANES))
    for l in range(LEVELS + 1):
        for i, part in enumerate(kron(vertical[l] * 4.0**l, False)):
            matrices[l, i] = part
    lane8 = lanes_of(8)
    slot = lane8 % (2 * H)
    width = jnp.zeros((H, LANES), F32)
    for s in range(H):
        rows = widths0[pl.ds(s, R // H, stride=H), :].astype(F32)
        at = H - 1 - s
        width = jnp.where(lane8 // (2 * H) == at, roll(rows, 2 * H * at + H), width)
    for k, a in enumerate(taps(width)):
        edge_taps[k] = jnp.where((slot >= H - k) & (slot < H + k), a, 0.0)


def north_rows(source, target, rows, factor, shifts):
    Z = source.shape[1]
    data = source[pl.ds(rows[0], len(rows))].reshape(len(rows) * Z, LANES)
    pair = jnp.concatenate(split(data), axis=1)
    for k in range(1, H + 1, 2):
        moved = mm(pair, shifts[:, (k - 1) * LANES : (k + 1) * LANES])
        for i, x in enumerate(rows):
            here = moved[i * Z : (i + 1) * Z]
            before = factor(0, x) * source[x] if k == 1 else target[x]
            target[x] = before + factor(k, x) * here[:, :LANES] + factor(k + 1, x) * here[:, LANES:]


def kron(vertical, transposed):
    Z = 16
    i = lax.broadcasted_iota(jnp.int32, (LANES, Z), 0)
    a = lax.broadcasted_iota(jnp.int32, (LANES, Z), 1)
    left = ((i // 8 if transposed else i % Z) == a).astype(F32).astype(BF16)
    b = lax.broadcasted_iota(jnp.int32, (Z, LANES), 0)
    o = lax.broadcasted_iota(jnp.int32, (Z, LANES), 1)
    right = (o % Z == b).astype(F32).astype(BF16)
    p = lax.broadcasted_iota(jnp.int32, (LANES, LANES), 0)
    q = lax.broadcasted_iota(jnp.int32, (LANES, LANES), 1)
    mask = (p % 8 if transposed else p // Z) == q // Z
    return [jnp.where(mask, mm(mm(left, part).astype(BF16), right), 0.0).astype(BF16) for part in split(vertical)]


def mix(matrix, data):
    high, low = split(data)
    return mm(matrix[0], high) + mm(matrix[0], low) + mm(matrix[1], high)


def finish(geo, *refs):
    Z, R, M, bases, frames = geo["Z"], geo["R"], geo["M"], geo["bases"], geo["frames"]
    it = iter(refs)
    take = lambda count: [next(it) for _ in range(count)]
    mixed0, matrices, edge_taps = take(3)
    joined = take(LEVELS)
    wide, gain = take(LEVELS), take(LEVELS)
    got_x, got_y, gain0, table, shifts = take(5)
    (out,) = take(1)
    got_low, got_high, ext, passed, north, result, spread, wf, gf, cf, edge = take(11)
    e, n = lax.axis_index("east"), lax.axis_index("north")
    has_low, has_high = e > 0, e < geo["E"] - 1
    north_even = n % 2 == 0
    got_low[...] = jnp.where(north_even, got_y[...], got_x[...])
    got_high[...] = jnp.where(north_even, got_x[...], got_y[...])
    lane = lanes_of(Z)
    lane8 = lanes_of(8)
    per = LANES // H
    base = geo["coarse_tiles"] + R // per
    levels = range(1, LEVELS + 1)
    rows_of = [R >> l for l in levels]
    starts = lambda more: [sum(rows_of[:l]) + l * more for l in range(LEVELS + 1)]
    ext_at = starts(2 * H + 2)
    out_at = starts(2)
    width_at = starts(2 * H)
    for l in range(LEVELS):
        r, m, at = R >> (l + 1), M >> (l + 1), frames[l + 1]
        for c in range(0, r + 2 * H, 8):
            row = c % Z
            begin = SLOT * (sum(-(-(R >> i) // Z) + 1 for i in range(1, l + 1)) + c // Z)
            lower, upper = got_low[base, row : row + 8, :], got_high[base, row : row + 8, :]
            width = jnp.where(
                lane8 < at,
                roll(lower, at - H - 1 - begin),
                jnp.where(lane8 < at + m, wide[l][pl.ds(c, 8), :], roll(upper, at + m - begin)),
            )
            wf[pl.ds(width_at[l] + c, 8), :] = jnp.where((lane8 >= at - H - 1) & (lane8 < at + m + H + 1), width, 0.0)
            weight = jnp.where(lane8 == at - 1, roll(lower, at - H - 2 - begin), gain[l][pl.ds(c, 8), :])
            gf[pl.ds(width_at[l] + c, 8), :] = jnp.where(lane8 == at + m, roll(upper, at + m - H - 1 - begin), weight)
        for i in range(r + 2 * H + 2):
            t, s = divmod(ext_at[l] + i, PER_TILE)
            own = roll(joined[l][i], at - 1 - bases[l])
            low_side = roll(got_low[t], at - H - 1 - SLOT * s)
            high_side = roll(got_high[t], at + m - 1 - SLOT * s)
            ext[ext_at[l] + i] = (
                jnp.where((lane >= at - 1) & (lane < at + m + 1), own, 0.0)
                + jnp.where((lane >= at - H - 1) & (lane < at + 1), low_side, 0.0)
                + jnp.where((lane >= at + m - 1) & (lane < at + m + H + 1), high_side, 0.0)
            )
    for k, a in enumerate(taps(wf[...])):
        cf[k] = a
    for l in range(LEVELS):
        r = R >> (l + 1)
        east_rows(ext, cf, passed, r + 2, 2, width_at[l] + H - 1, ext_at[l], out_at[l])

    total = out_at[-1]

    def coarse_factor(k, x):
        l = max(i for i in range(LEVELS) if out_at[i] <= x)
        return cf[k, pl.ds(width_at[l] + H - 1 + x - out_at[l], 1), :]

    half = -(-total // 2)
    north_rows(passed, north, range(0, half), coarse_factor, shifts)
    north_rows(passed, north, range(half, total), coarse_factor, shifts)
    for l in range(LEVELS - 1, -1, -1):
        r, m, at = R >> (l + 1), M >> (l + 1), frames[l + 1]
        groups = (r + 2 + 7) // 8
        matrix = [matrices[l + 1, 0], matrices[l + 1, 1]]
        for g in range(groups):
            have = min(8, r + 2 - 8 * g)
            data = north[out_at[l] + 8 * g : out_at[l] + 8 * g + have].reshape(have * Z, LANES)
            if have < 8:
                data = jnp.concatenate([data, jnp.zeros(((8 - have) * Z, LANES), F32)], axis=0)
            mixed = mix(matrix, data)
            for i in range(have):
                row = 8 * g + i
                result[row] = gf[pl.ds(width_at[l] + row + H - 1, 1), :] * mixed[i * Z : (i + 1) * Z]
        if l < LEVELS - 1:
            inside = ((lane >= at) | (n > 0)) & ((lane < at + m) | (n < geo["N"] - 1))
            for row in range(-1, r + 1):
                j = row // 2
                other = j + (1 if row % 2 else -1)
                summed = result[row + 1] + 0.75 * spread[j + 1] + 0.25 * spread[other + 1]
                keep = inside
                if row == -1:
                    keep = keep & has_low
                if row == r:
                    keep = keep & has_high
                result[row + 1] = jnp.where(keep, summed, 0.0)
        flat = result.reshape(result.shape[0] * Z, LANES)
        spread_flat = spread.reshape(spread.shape[0] * Z, LANES)
        spread_flat[pl.ds(0, (r + 2) * Z), :] = dot_exact(flat[pl.ds(0, (r + 2) * Z), :], table[l])
    low_half = lane % (2 * H) < H
    for t in range(R // H):
        tile = geo["coarse_tiles"] + t // 2
        low_side, high_side = got_low[tile], got_high[tile]
        if t % 2:
            low_side = roll(low_side, -H)
        else:
            high_side = roll(high_side, H)
        halo = jnp.where(low_half, low_side, high_side)
        summed = jnp.zeros((Z, LANES), F32)
        for k in range(1, H + 1):
            summed = summed + edge_taps[k, pl.ds(t, 1), :] * jnp.where(low_half, roll(halo, -k), roll(halo, k))
        edge[t] = summed
    edge_flat = edge.reshape(R // H * Z, LANES)
    edge_flat[...] = mix([matrices[0, 0], matrices[0, 1]], edge_flat[...])
    widen = table[LEVELS][:, 0 : 6 * Z]
    at_edge = (lane8 < H) | (lane8 >= M - H)
    for b in range(R // 8):
        high, low = split(spread[4 * b : 4 * b + 6].reshape(6 * Z, LANES))
        added = mm(widen, high) + mm(widen, low)
        weight = gain0[pl.ds(8 * b, 8), :]
        for z in range(Z):
            row = edge_flat[pl.ds(b * Z + z, 8, stride=0), :]
            moved = pltpu.roll(row, H, 1, stride=2 * H, stride_axis=0)
            here = mixed0[b, z * 8 : z * 8 + 8, :] + jnp.where(at_edge, moved, 0.0)
            out[z, pl.ds(8 * b, 8), :] = weight * here + added[z * 8 : z * 8 + 8]


def swap(x, axis, first):
    route = [(i, i + 1) for i in range(first, lax.axis_size(axis) - 1, 2)]
    return lax.ppermute(x, axis, route + [(j, i) for i, j in route])


def body(inc, w0, w1, w2, w3, g0, g1, g2, g3, vertical):
    Z, R, M = inc.shape
    bases, frames, down, up, shifts = tables(R, M)
    total_rows = sum((R >> l) + 2 * H + 2 for l in range(1, LEVELS + 1))
    geo = dict(
        Z=Z, R=R, M=M, bases=bases, frames=frames, E=lax.axis_size("east"), N=lax.axis_size("north"),
        coarse_tiles=-(-total_rows // PER_TILE),
    )
    shape = lambda *dims: jax.ShapeDtypeStruct(dims, F32)
    levels = range(1, LEVELS + 1)
    params = pltpu.CompilerParams(vmem_limit_bytes=48 * 1024 * 1024)
    east_tiles = H + SLOT + 1
    given = (inc, jnp.asarray(down))
    outs = pl.pallas_call(
        functools.partial(prepare, geo),
        out_shape=[shape(R, Z, M)] + [shape((R >> l) + 2, Z, M) for l in levels]
        + [shape(2, Z, M)],
        in_specs=[pl.BlockSpec(memory_space=pltpu.HBM)] * len(given),
        scratch_shapes=[pltpu.VMEM((R, Z, M), F32)] + [pltpu.VMEM(x.shape, x.dtype) for x in given]
        + [pltpu.SemaphoreType.DMA((len(given),))],
        compiler_params=params,
    )(*[pltpu.with_memory_space_constraint(x, pltpu.HBM) for x in given])
    field, coarse, send_far = outs[0], outs[1 : 1 + LEVELS], outs[1 + LEVELS]
    got_far = swap(send_far, "east", 0)
    send_a, send_b = pl.pallas_call(
        functools.partial(gather, geo),
        out_shape=[shape(east_tiles, Z, M), shape(east_tiles + 2, Z, M)],
        compiler_params=params,
    )(field, *coarse, got_far, w1, w2, w3, g1, g2, g3)
    got_b = swap(send_b, "east", 1)
    got_a = swap(send_a, "east", 0)
    factors, inner = pl.pallas_call(
        functools.partial(interior, geo),
        out_shape=[shape(H + 1, R, M), shape(R - 2 * H, Z, M)],
        compiler_params=params,
    )(field, w0)
    forward, inner, got_a = lax.optimization_barrier((got_b, inner, got_a))
    got_d = swap(forward, "east", 0)
    wide_shapes = [shape((R >> l) + 2 * H, M) for l in levels]
    north_tiles = geo["coarse_tiles"] + R * H // LANES + 1
    outs = pl.pallas_call(
        functools.partial(middle, geo),
        out_shape=[shape(R, Z, M)] + [shape((R >> l) + 2 * H + 2, Z, M) for l in levels]
        + [shape(north_tiles, Z, M)] * 2 + wide_shapes * 2,
        scratch_shapes=[pltpu.VMEM((3 * H, Z, M), F32)] * 2,
        compiler_params=params,
    )(field, *coarse, got_a, got_b, got_d, factors, inner, w1, w2, w3, g1, g2, g3)
    eastward = outs[0]
    joined, (send_x, send_y) = outs[1 : 1 + LEVELS], outs[1 + LEVELS : 3 + LEVELS]
    wide, gain = outs[3 + LEVELS : 3 + 2 * LEVELS], outs[3 + 2 * LEVELS :]
    got_x = swap(send_x, "north", 0)
    got_y = swap(send_y, "north", 1)
    shifts = jnp.asarray(shifts)
    assert R // H == 8 and 8 * Z == LANES
    window = pl.pallas_call(
        functools.partial(own_north, geo),
        out_shape=[
            shape(R // 8, LANES, LANES), jax.ShapeDtypeStruct((LEVELS + 1, 2, LANES, LANES), BF16), shape(H + 1, 8, LANES)
        ],
        scratch_shapes=[pltpu.VMEM((R, Z, M), F32)],
        compiler_params=params,
    )(eastward, factors, shifts, w0, vertical)
    rows1 = (R >> 1) + 2
    out_rows = sum((R >> l) + 2 for l in levels)
    width_rows = out_rows + LEVELS * (2 * H - 2)
    return pl.pallas_call(
        functools.partial(finish, geo),
        out_shape=shape(Z, R, M),
        scratch_shapes=[
            pltpu.VMEM(dims, F32)
            for dims in (
                (north_tiles, Z, M), (north_tiles, Z, M), (total_rows, Z, M), (out_rows, Z, M), (out_rows, Z, M),
                (rows1, Z, M), (rows1, Z, M), (width_rows, M), (width_rows, M), (H + 1, width_rows, M),
                (R // H, Z, M),
            )
        ],
        compiler_params=params,
    )(*window, *joined, *wide, *gain, got_x, got_y, g0, jnp.asarray(up), shifts)


def solution(mesh):
    tile = P("east", "north")
    return jax.shard_map(
        body,
        mesh=mesh,
        in_specs=(P(None, "east", "north"), *([tile] * 8), P()),
        out_specs=P(None, "east", "north"),
        check_vma=False,
    )
```

```python
import functools

import jax
import jax.numpy as jnp
import numpy as np
from jax import lax
from jax.experimental import pallas as pl
from jax.experimental.pallas import tpu as pltpu
from jax.sharding import PartitionSpec as P

H = 8
LANES = 128
LEVELS = 3
F32 = jnp.float32
BF16 = jnp.bfloat16
SLOT = H + 2
PER_TILE = LANES // SLOT


def tables(rows, cols):
    bases, at = [], H
    for l in range(1, LEVELS + 1):
        bases.append(at)
        at += (cols >> l) + 2
    assert at <= LANES and cols == LANES
    down = np.zeros((4, cols, LANES), np.float32)
    for variant in range(4):
        current = np.eye(cols)
        low = 0
        for l in range(1, LEVELS + 1):
            m = cols >> l
            step = np.zeros((current.shape[1], m + 2))
            for j in range(-1, m + 1):
                for f, w in ((2 * j, 0.375), (2 * j + 1, 0.375), (2 * j - 1, 0.125), (2 * j + 2, 0.125)):
                    if 0 <= f - low < current.shape[1]:
                        step[f - low, j + 1] += w
            current = current @ step
            if variant & 1:
                current[:, 0] = 0
            if variant & 2:
                current[:, -1] = 0
            low = -1
            down[variant, :, bases[l - 1] : bases[l - 1] + m + 2] = current
    frames = [0]
    for l in range(1, LEVELS + 1):
        own = bases[l - 1] + 1
        frames.append(own if own + (cols >> l) + H < LANES else H + 1)
    up = np.zeros((LEVELS + 1, LANES, LANES), np.float32)
    for l in range(LEVELS):
        m = cols >> l
        for f in range(-1, m + 1) if l else range(m):
            j = f // 2
            out, at = f + frames[l], frames[l + 1]
            up[l, j + at, out] += 0.75
            up[l, j + (1 if f % 2 else -1) + at, out] += 0.25
    for z in range(16):
        for i in range(8):
            j = i // 2 + 1
            up[LEVELS, z * 8 + i, j * 16 + z] += 0.75
            up[LEVELS, z * 8 + i, (j + (1 if i % 2 else -1)) * 16 + z] += 0.25
    for t in (down, up):
        assert (t == t.astype(jnp.bfloat16).astype(np.float32)).all()
    shifts = np.concatenate([np.eye(LANES, k=k) + np.eye(LANES, k=-k) for k in range(1, H + 1)], axis=1)
    shifts = np.concatenate([shifts, shifts], axis=0)
    return bases, frames, down.astype(jnp.bfloat16), up.astype(jnp.bfloat16), shifts.astype(jnp.bfloat16)


def place(geo, index):
    full = geo["coarse_tiles"] * PER_TILE
    if index < full:
        return divmod(index, PER_TILE)
    return geo["coarse_tiles"] + geo["R"] * H // LANES, geo["width_slots"] + index - full


def packed(geo, row, l, s):
    lane, m = lanes_of(row.shape[0]), geo["M"] >> (l + 1)
    here = (lane >= SLOT * s) & (lane < SLOT * (s + 1))
    at = SLOT * s - geo["bases"][l]
    return here, roll(row, at), roll(row, at - m + H)


def split(x):
    high = x.astype(BF16)
    return high, (x - high.astype(F32)).astype(BF16)


def mm(a, b):
    return jnp.dot(a, b, preferred_element_type=F32)


def dot_exact(x, weights):
    high, low = split(x)
    return mm(high, weights) + mm(low, weights)


def lanes_of(rows):
    return lax.broadcasted_iota(jnp.int32, (rows, LANES), 1)


def roll(x, shift):
    shift %= LANES
    return pltpu.roll(x, shift, 1) if shift else x


def taps(widths):
    grown = widths + 1.0
    inverse = 1.0 / (grown * grown)
    profile = [jnp.square(jnp.maximum(1.0 - float(k * k) * inverse, 0.0)) for k in range(1, H + 1)]
    total = profile[0]
    for p in profile[1:]:
        total = total + p
    scale = 1.0 / (1.0 + 2.0 * total)
    return [scale] + [p * scale for p in profile]


def prepare(geo, *refs):
    count = 2
    outside, (field, *rest) = refs[:count], refs[count:]
    coarse, (send_far, half, *inside) = rest[:LEVELS], rest[LEVELS:]
    sems = inside.pop()
    copies = [pltpu.make_async_copy(a, b, sems.at[i]) for i, (a, b) in enumerate(zip(outside, inside))]
    for copy in copies:
        copy.start()
    inc, table = inside
    Z, R, M, bases = geo["Z"], geo["R"], geo["M"], geo["bases"]
    e, n = lax.axis_index("east"), lax.axis_index("north")
    has_low, has_high = e > 0, e < geo["E"] - 1
    even = e % 2 == 0
    flat = field.reshape(R * Z, M)
    for copy in copies:
        copy.wait()
    for z in range(Z):
        flat[pl.ds(z, R, stride=Z), :] = inc[z]
    variant = (n == 0).astype(jnp.int32) + 2 * (n == geo["N"] - 1).astype(jnp.int32)
    weights = table[variant]
    half_flat = half.reshape(R * Z, M)
    chunk = R * Z // 4
    for c in range(4):
        half_flat[pl.ds(c * chunk, chunk), :] = dot_exact(flat[pl.ds(c * chunk, chunk), :], weights)
    source, low, top = half, 0, R
    for l in range(1, LEVELS + 1):
        r, out = R >> l, coarse[l - 1]

        def get(i, source=source, low=low, top=top):
            return source[i - low] if low <= i < top else None

        for j in range(-1, r + 1):
            total = None
            for pair, w in (((2 * j, 2 * j + 1), 0.375), ((2 * j - 1, 2 * j + 2), 0.125)):
                terms = [t for t in (get(i) for i in pair) if t is not None]
                if terms:
                    part = w * functools.reduce(jnp.add, terms)
                    total = part if total is None else total + part
            if j == -1:
                total = jnp.where(has_low, total, 0.0)
            if j == r:
                total = jnp.where(has_high, total, 0.0)
            out[j + 1] = total
        source, low, top = out, -1, r + 1
    r = R >> LEVELS
    for i in range(2):
        send_far[i] = jnp.where(even, coarse[LEVELS - 1][r + i], coarse[LEVELS - 1][i])


def gather(geo, field, *refs):
    coarse, got_far, widths, gains, send_a, send_b = refs[:LEVELS], refs[LEVELS], refs[LEVELS + 1 : 2 * LEVELS + 1], refs[2 * LEVELS + 1 : -2], refs[-2], refs[-1]
    Z, R, M, bases = geo["Z"], geo["R"], geo["M"], geo["bases"]
    even = lax.axis_index("east") % 2 == 0
    start = R - H
    send_a[0:H] = field[pl.ds(jnp.where(even, start, 0), H)]
    send_b[0:H] = field[pl.ds(jnp.where(even, 0, start), H)]
    lane = lanes_of(Z)
    for i in range(SLOT):
        def merged(picks):
            out = coarse[LEVELS - 1][picks[LEVELS - 1]]
            for l in range(LEVELS - 1, 0, -1):
                out = jnp.where(lane < bases[l], coarse[l - 1][picks[l - 1]], out)
            return out

        lower = merged([i] * LEVELS)
        upper = merged([(R >> l) - H + i for l in range(1, LEVELS + 1)])
        send_a[H + i] = jnp.where(even, upper, lower)
        send_b[H + i] = jnp.where(even, lower, upper)
    last = H + SLOT
    send_a[last] = jnp.zeros((Z, LANES), F32)
    send_b[last] = jnp.zeros((Z, LANES), F32)
    for j, ref in enumerate((*widths, *gains)):
        r, m = ref.shape
        lower = ref[pl.ds(0, 1), :].astype(F32)
        upper = ref[pl.ds(r - 1, 1), :].astype(F32)
        send_a[last, pl.ds(j, 1), pl.ds(0, m)] = jnp.where(even, upper, lower)
        send_b[last, pl.ds(j, 1), pl.ds(0, m)] = jnp.where(even, lower, upper)
    send_b[last + 1 : last + 3] = got_far[...]


def east_rows(source, factors, out, count, block, factor_at=0, source_at=0, out_at=0):
    def step(b, carry):
        east_block(source, factors, out, b * block, block, factor_at, source_at, out_at)
        return carry

    lax.fori_loop(0, count // block, step, 0)


def east_block(source, factors, out, x0, block, factor_at, source_at, out_at):
    rows = [source[x0 + i + source_at] for i in range(block + 2 * H)]
    for i in range(block):
        def factor(k):
            return factors[k, pl.ds(x0 + i + factor_at, 1), :]

        total = factor(0) * rows[i + H]
        for k in range(1, H + 1):
            total = total + factor(k) * (rows[i + H + k] + rows[i + H - k])
        out[x0 + i + out_at] = total


def interior(geo, field, widths0, factors, inner):
    for k, a in enumerate(taps(widths0[...].astype(F32))):
        factors[k] = a
    east_rows(field, factors, inner, geo["R"] - 2 * H, 4, H)


def middle(geo, *refs):
    Z, R, M, bases = geo["Z"], geo["R"], geo["M"], geo["bases"]
    it = iter(refs)
    take = lambda count: [next(it) for _ in range(count)]
    (field,) = take(1)
    coarse = take(LEVELS)
    got_a, got_b, factors, inner = take(4)
    widths, gains = take(LEVELS), take(LEVELS)
    (eastward,) = take(1)
    joined = take(LEVELS)
    send_x, send_y = take(2)
    wide, gain = take(LEVELS), take(LEVELS)
    below, above = take(2)
    e, n = lax.axis_index("east"), lax.axis_index("north")
    even = e % 2 == 0
    below[0:H] = jnp.where(even, got_b[0:H], got_a[0:H])
    below[H : 3 * H] = field[0 : 2 * H]
    above[0 : 2 * H] = field[R - 2 * H : R]
    above[2 * H : 3 * H] = jnp.where(even, got_a[0:H], got_b[0:H])
    east_rows(below, factors, eastward, H, 4)
    east_rows(above, factors, eastward, H, 4, R - H, 0, R - H)
    eastward[H : R - H] = inner[...]
    for l in range(1, LEVELS + 1):
        r, out, own = R >> l, joined[l - 1], coarse[l - 1]
        out[H : H + r + 2] = own[...]
        out[0:H] = jnp.zeros((H, Z, LANES), F32)
        out[H + r + 2 : 2 * H + r + 2] = jnp.zeros((H, Z, LANES), F32)
    for i in range(SLOT):
        a, b = got_a[H + i], got_b[H + i]
        lower, upper = jnp.where(even, b, a), jnp.where(even, a, b)
        for l in range(1, LEVELS + 1):
            r, out = R >> l, joined[l - 1]
            out[i] = out[i] + lower
            out[r + H + i] = out[r + H + i] + upper
    r, out = R >> LEVELS, joined[LEVELS - 1]
    for i in range(2):
        far = got_b[H + SLOT + 1 + i]
        out[i] = out[i] + jnp.where(even, far, 0.0)
        out[r + 2 * H + i] = out[r + 2 * H + i] + jnp.where(even, 0.0, far)
    last = H + SLOT
    rows_a, rows_b = got_a[last], got_b[last]
    lower, upper = jnp.where(even, rows_b, rows_a), jnp.where(even, rows_a, rows_b)
    for j, (own, out) in enumerate(zip((*widths, *gains), (*wide, *gain))):
        r, m = own.shape
        out[...] = jnp.zeros(out.shape, F32)
        at = geo["frames"][j % LEVELS + 1]
        out[pl.ds(H, r), pl.ds(at, m)] = own[...].astype(F32)
        out[pl.ds(H - 1, 1), pl.ds(at, m)] = lower[j : j + 1, 0:m]
        out[pl.ds(H + r, 1), pl.ds(at, m)] = upper[j : j + 1, 0:m]
    north_even = n % 2 == 0
    lane = lanes_of(Z)

    def send(t, low_side, high_side):
        send_x[t] = jnp.where(north_even, high_side, low_side)
        send_y[t] = jnp.where(north_even, low_side, high_side)

    zero = jnp.zeros((Z, LANES), F32)
    todo = [(l, i) for l in range(LEVELS) for i in range(joined[l].shape[0])]
    for t in range(geo["coarse_tiles"]):
        low_side, high_side = zero, zero
        for s, (l, i) in enumerate(todo[t * PER_TILE : (t + 1) * PER_TILE]):
            here, lower, upper = packed(geo, joined[l][i], l, s)
            low_side, high_side = jnp.where(here, lower, low_side), jnp.where(here, upper, high_side)
        send(t, low_side, high_side)
    per = LANES // H
    for t in range(R // per):
        low_side, high_side = zero, zero
        for s in range(per):
            row, at = eastward[t * per + s], 2 * H * (H - 1 - s % H) + H * (s // H)
            here = (lane >= at) & (lane < at + H)
            low_side = jnp.where(here, roll(row, at), low_side)
            high_side = jnp.where(here, roll(row, at - M + H), high_side)
        send(geo["coarse_tiles"] + t, low_side, high_side)
    low_side, high_side, q = zero, zero, 0
    for l in range(LEVELS):
        rows, m, at = wide[l].shape[0], M >> (l + 1), geo["frames"][l + 1]
        for c in range(0, rows, Z):
            have = min(rows - c, Z)
            width, weight = wide[l][pl.ds(c, have), :], gain[l][pl.ds(c, have), :]
            if have < Z:
                fill = jnp.zeros((Z - have, LANES), F32)
                width, weight = jnp.concatenate([width, fill], axis=0), jnp.concatenate([weight, fill], axis=0)
            begin = SLOT * q
            here, last_lane = (lane >= begin) & (lane < begin + H + 1), lane == begin + H + 1
            low_side = jnp.where(here, roll(width, begin - at), low_side)
            low_side = jnp.where(last_lane, roll(weight, begin + H + 1 - at), low_side)
            high_side = jnp.where(here, roll(width, begin - at - m + H + 1), high_side)
            high_side = jnp.where(last_lane, roll(weight, begin + H + 2 - at - m), high_side)
            q += 1
    for l, i in todo[geo["coarse_tiles"] * PER_TILE :]:
        here, lower, upper = packed(geo, joined[l][i], l, q)
        low_side, high_side = jnp.where(here, lower, low_side), jnp.where(here, upper, high_side)
        q += 1
    send(geo["coarse_tiles"] + R // per, low_side, high_side)


def forwarded(geo, got_d):
    even, r = lax.axis_index("east") % 2 == 0, geo["R"] >> LEVELS
    for i in range(2):
        yield i, jnp.where(even, 0.0, got_d[H + r + i])
        yield r + 2 * H + i, jnp.where(even, got_d[H + i], 0.0)


def patch(geo, before_x, before_y, got_d, send_x, send_y):
    north_even = lax.axis_index("north") % 2 == 0
    send_x[...] = before_x[...]
    send_y[...] = before_y[...]
    first = sum((geo["R"] >> l) + 2 * H + 2 for l in range(1, LEVELS))
    for i, row in forwarded(geo, got_d):
        t, s = place(geo, first + i)
        here, lower, upper = packed(geo, row, LEVELS - 1, s)
        send_x[t] = send_x[t] + jnp.where(here, jnp.where(north_even, upper, lower), 0.0)
        send_y[t] = send_y[t] + jnp.where(here, jnp.where(north_even, lower, upper), 0.0)


def own_north(geo, eastward, factors, shifts, widths0, vertical, mixed, matrices, edge_taps, north):
    R, Z = geo["R"], geo["Z"]
    for x0 in range(0, R, R // 2):
        north_rows(eastward, north, range(x0, x0 + R // 2), lambda k, x: factors[k, pl.ds(x, 1), :], shifts)
    matrix = kron(vertical[0], True)
    for b in range(R // 8):
        mixed[b] = mix(matrix, north[8 * b : 8 * b + 8].reshape(8 * Z, LANES))
    for l in range(LEVELS + 1):
        for i, part in enumerate(kron(vertical[l] * 4.0**l, False)):
            matrices[l, i] = part
    lane8 = lanes_of(8)
    slot = lane8 % (2 * H)
    width = jnp.zeros((H, LANES), F32)
    for s in range(H):
        rows = widths0[pl.ds(s, R // H, stride=H), :].astype(F32)
        at = H - 1 - s
        width = jnp.where(lane8 // (2 * H) == at, roll(rows, 2 * H * at + H), width)
    for k, a in enumerate(taps(width)):
        edge_taps[k] = jnp.where((slot >= H - k) & (slot < H + k), a, 0.0)


def north_rows(source, target, rows, factor, shifts):
    Z = source.shape[1]
    data = source[pl.ds(rows[0], len(rows))].reshape(len(rows) * Z, LANES)
    pair = jnp.concatenate(split(data), axis=1)
    for k in range(1, H + 1, 2):
        moved = mm(pair, shifts[:, (k - 1) * LANES : (k + 1) * LANES])
        for i, x in enumerate(rows):
            here = moved[i * Z : (i + 1) * Z]
            before = factor(0, x) * source[x] if k == 1 else target[x]
            target[x] = before + factor(k, x) * here[:, :LANES] + factor(k + 1, x) * here[:, LANES:]


def kron(vertical, transposed):
    Z = 16
    i = lax.broadcasted_iota(jnp.int32, (LANES, Z), 0)
    a = lax.broadcasted_iota(jnp.int32, (LANES, Z), 1)
    left = ((i // 8 if transposed else i % Z) == a).astype(F32).astype(BF16)
    b = lax.broadcasted_iota(jnp.int32, (Z, LANES), 0)
    o = lax.broadcasted_iota(jnp.int32, (Z, LANES), 1)
    right = (o % Z == b).astype(F32).astype(BF16)
    p = lax.broadcasted_iota(jnp.int32, (LANES, LANES), 0)
    q = lax.broadcasted_iota(jnp.int32, (LANES, LANES), 1)
    mask = (p % 8 if transposed else p // Z) == q // Z
    return [jnp.where(mask, mm(mm(left, part).astype(BF16), right), 0.0).astype(BF16) for part in split(vertical)]


def mix(matrix, data):
    high, low = split(data)
    return mm(matrix[0], high) + mm(matrix[0], low) + mm(matrix[1], high)


def finish(geo, *refs):
    Z, R, M, bases, frames = geo["Z"], geo["R"], geo["M"], geo["bases"], geo["frames"]
    it = iter(refs)
    take = lambda count: [next(it) for _ in range(count)]
    mixed0, matrices, edge_taps = take(3)
    joined = take(LEVELS)
    wide, gain = take(LEVELS), take(LEVELS)
    got_x, got_y, got_d, gain0, table, shifts = take(6)
    (out,) = take(1)
    got_low, got_high, ext, passed, north, result, spread, wf, gf, cf, edge = take(11)
    e, n = lax.axis_index("east"), lax.axis_index("north")
    has_low, has_high = e > 0, e < geo["E"] - 1
    north_even = n % 2 == 0
    got_low[...] = jnp.where(north_even, got_y[...], got_x[...])
    got_high[...] = jnp.where(north_even, got_x[...], got_y[...])
    lane = lanes_of(Z)
    lane8 = lanes_of(8)
    per = LANES // H
    base = geo["coarse_tiles"] + R // per
    levels = range(1, LEVELS + 1)
    rows_of = [R >> l for l in levels]
    wire_at = [sum(r + 2 * H + 2 for r in rows_of[:l]) for l in range(LEVELS)]
    groups = [[0], list(range(1, LEVELS))]
    group_of = [0] + [1] * (LEVELS - 1)
    used = [frames[l] + d for l in range(2, LEVELS + 1) for d in range(-H - 1, (M >> l) + H + 1)]
    assert len(set(used)) == len(used)
    begins = lambda more: [0 if g == 0 else rows_of[0] + more for g in group_of]
    ext_at, out_at, width_at = begins(2 * H + 2), begins(2), begins(2 * H)
    extra = dict(forwarded(geo, got_d))

    def widths_chunk(l, c):
        r, m, at = rows_of[l], M >> (l + 1), frames[l + 1]
        row = c % Z
        begin = SLOT * (sum(-(-(q + 2 * H) // Z) for q in rows_of[:l]) + c // Z)
        lower, upper = got_low[base, row : row + 8, :], got_high[base, row : row + 8, :]
        width = jnp.where(
            lane8 < at,
            roll(lower, at - H - 1 - begin),
            jnp.where(lane8 < at + m, wide[l][pl.ds(c, 8), :], roll(upper, at + m - begin)),
        )
        width = jnp.where((lane8 >= at - H - 1) & (lane8 < at + m + H + 1), width, 0.0)
        weight = jnp.where(lane8 == at - 1, roll(lower, at - H - 2 - begin), gain[l][pl.ds(c, 8), :])
        return width, jnp.where(lane8 == at + m, roll(upper, at + m - H - 1 - begin), weight)

    def source_row(l, i):
        m, at = M >> (l + 1), frames[l + 1]
        t, s = place(geo, wire_at[l] + i)
        own = joined[l][i]
        if l == LEVELS - 1 and i in extra:
            own = own + extra[i]
        own = roll(own, at - 1 - bases[l])
        low_side = roll(got_low[t], at - H - 1 - SLOT * s)
        high_side = roll(got_high[t], at + m - 1 - SLOT * s)
        return (
            jnp.where((lane >= at - 1) & (lane < at + m + 1), own, 0.0)
            + jnp.where((lane >= at - H - 1) & (lane < at + 1), low_side, 0.0)
            + jnp.where((lane >= at + m - 1) & (lane < at + m + H + 1), high_side, 0.0)
        )

    for g in groups:
        r = rows_of[g[0]]
        for c in range(0, r + 2 * H, 8):
            parts = [widths_chunk(l, c) for l in g if c < rows_of[l] + 2 * H]
            wf[pl.ds(width_at[g[0]] + c, 8), :] = functools.reduce(jnp.add, [p[0] for p in parts])
            gf[pl.ds(width_at[g[0]] + c, 8), :] = functools.reduce(jnp.add, [p[1] for p in parts])
    for k, a in enumerate(taps(wf[...])):
        cf[k] = a
    for g in groups:
        r = rows_of[g[0]]
        for i in range(r + 2 * H + 2):
            parts = [source_row(l, i) for l in g if i < rows_of[l] + 2 * H + 2]
            ext[ext_at[g[0]] + i] = functools.reduce(jnp.add, parts)
        for x in range(0, r + 2, 4):
            east_block(ext, cf, passed, x, min(4, r + 2 - x), width_at[g[0]] + H - 1, ext_at[g[0]], out_at[g[0]])

    total = rows_of[0] + rows_of[1] + 4

    def coarse_factor(k, x):
        l = 0 if x < out_at[1] else 1
        return cf[k, pl.ds(width_at[l] + H - 1 + x - out_at[l], 1), :]

    half = -(-total // 2)
    north_rows(passed, north, range(0, half), coarse_factor, shifts)
    north_rows(passed, north, range(half, total), coarse_factor, shifts)
    for l in range(LEVELS - 1, -1, -1):
        r, m, at = R >> (l + 1), M >> (l + 1), frames[l + 1]
        blocks = (r + 2 + 7) // 8
        matrix = [matrices[l + 1, 0], matrices[l + 1, 1]]
        for g in range(blocks):
            have = min(8, r + 2 - 8 * g)
            data = north[out_at[l] + 8 * g : out_at[l] + 8 * g + have].reshape(have * Z, LANES)
            if have < 8:
                data = jnp.concatenate([data, jnp.zeros(((8 - have) * Z, LANES), F32)], axis=0)
            mixed = mix(matrix, data)
            for i in range(have):
                row = 8 * g + i
                result[row] = gf[pl.ds(width_at[l] + row + H - 1, 1), :] * mixed[i * Z : (i + 1) * Z]
        if l < LEVELS - 1:
            inside = ((lane >= at) | (n > 0)) & ((lane < at + m) | (n < geo["N"] - 1))
            for row in range(-1, r + 1):
                j = row // 2
                other = j + (1 if row % 2 else -1)
                summed = result[row + 1] + 0.75 * spread[j + 1] + 0.25 * spread[other + 1]
                keep = inside
                if row == -1:
                    keep = keep & has_low
                if row == r:
                    keep = keep & has_high
                result[row + 1] = jnp.where(keep, summed, 0.0)
        flat = result.reshape(result.shape[0] * Z, LANES)
        spread_flat = spread.reshape(spread.shape[0] * Z, LANES)
        spread_flat[pl.ds(0, (r + 2) * Z), :] = dot_exact(flat[pl.ds(0, (r + 2) * Z), :], table[l])
    low_half = lane % (2 * H) < H
    for t in range(R // H):
        tile = geo["coarse_tiles"] + t // 2
        low_side, high_side = got_low[tile], got_high[tile]
        if t % 2:
            low_side = roll(low_side, -H)
        else:
            high_side = roll(high_side, H)
        halo = jnp.where(low_half, low_side, high_side)
        summed = jnp.zeros((Z, LANES), F32)
        for k in range(1, H + 1):
            summed = summed + edge_taps[k, pl.ds(t, 1), :] * jnp.where(low_half, roll(halo, -k), roll(halo, k))
        edge[t] = summed
    edge_flat = edge.reshape(R // H * Z, LANES)
    edge_flat[...] = mix([matrices[0, 0], matrices[0, 1]], edge_flat[...])
    widen = table[LEVELS][:, 0 : 6 * Z]
    at_edge = (lane8 < H) | (lane8 >= M - H)
    for b in range(R // 8):
        high, low = split(spread[4 * b : 4 * b + 6].reshape(6 * Z, LANES))
        added = mm(widen, high) + mm(widen, low)
        weight = gain0[pl.ds(8 * b, 8), :]
        for z in range(Z):
            row = edge_flat[pl.ds(b * Z + z, 8, stride=0), :]
            moved = pltpu.roll(row, H, 1, stride=2 * H, stride_axis=0)
            here = mixed0[b, z * 8 : z * 8 + 8, :] + jnp.where(at_edge, moved, 0.0)
            out[z, pl.ds(8 * b, 8), :] = weight * here + added[z * 8 : z * 8 + 8]


def swap(x, axis, first):
    route = [(i, i + 1) for i in range(first, lax.axis_size(axis) - 1, 2)]
    return lax.ppermute(x, axis, route + [(j, i) for i, j in route])


def body(inc, w0, w1, w2, w3, g0, g1, g2, g3, vertical):
    Z, R, M = inc.shape
    bases, frames, down, up, shifts = tables(R, M)
    total_rows = sum((R >> l) + 2 * H + 2 for l in range(1, LEVELS + 1))
    width_slots = sum(-(-((R >> l) + 2 * H) // Z) for l in range(1, LEVELS + 1))
    geo = dict(
        Z=Z, R=R, M=M, bases=bases, frames=frames, E=lax.axis_size("east"), N=lax.axis_size("north"),
        coarse_tiles=-(-(total_rows - PER_TILE + width_slots) // PER_TILE), width_slots=width_slots,
    )
    shape = lambda *dims: jax.ShapeDtypeStruct(dims, F32)
    levels = range(1, LEVELS + 1)
    params = pltpu.CompilerParams(vmem_limit_bytes=48 * 1024 * 1024)
    east_tiles = H + SLOT + 1
    given = (inc, jnp.asarray(down))
    outs = pl.pallas_call(
        functools.partial(prepare, geo),
        out_shape=[shape(R, Z, M)] + [shape((R >> l) + 2, Z, M) for l in levels]
        + [shape(2, Z, M)],
        in_specs=[pl.BlockSpec(memory_space=pltpu.HBM)] * len(given),
        scratch_shapes=[pltpu.VMEM((R, Z, M), F32)] + [pltpu.VMEM(x.shape, x.dtype) for x in given]
        + [pltpu.SemaphoreType.DMA((len(given),))],
        compiler_params=params,
    )(*[pltpu.with_memory_space_constraint(x, pltpu.HBM) for x in given])
    field, coarse, send_far = outs[0], outs[1 : 1 + LEVELS], outs[1 + LEVELS]
    got_far = swap(send_far, "east", 0)
    send_a, send_b = pl.pallas_call(
        functools.partial(gather, geo),
        out_shape=[shape(east_tiles, Z, M), shape(east_tiles + 2, Z, M)],
        compiler_params=params,
    )(field, *coarse, got_far, w1, w2, w3, g1, g2, g3)
    got_b = swap(send_b, "east", 1)
    got_a = swap(send_a, "east", 0)
    factors, inner = pl.pallas_call(
        functools.partial(interior, geo),
        out_shape=[shape(H + 1, R, M), shape(R - 2 * H, Z, M)],
        compiler_params=params,
    )(field, w0)
    forward, inner, got_a = lax.optimization_barrier((got_b, inner, got_a))
    got_d = swap(forward, "east", 0)
    wide_shapes = [shape((R >> l) + 2 * H, M) for l in levels]
    north_tiles = geo["coarse_tiles"] + R * H // LANES + 1
    outs = pl.pallas_call(
        functools.partial(middle, geo),
        out_shape=[shape(R, Z, M)] + [shape((R >> l) + 2 * H + 2, Z, M) for l in levels]
        + [shape(north_tiles, Z, M)] * 2 + wide_shapes * 2,
        scratch_shapes=[pltpu.VMEM((3 * H, Z, M), F32)] * 2,
        compiler_params=params,
    )(field, *coarse, got_a, got_b, factors, inner, w1, w2, w3, g1, g2, g3)
    eastward = outs[0]
    joined, (send_x, send_y) = outs[1 : 1 + LEVELS], outs[1 + LEVELS : 3 + LEVELS]
    wide, gain = outs[3 + LEVELS : 3 + 2 * LEVELS], outs[3 + 2 * LEVELS :]
    send_x, send_y = pl.pallas_call(
        functools.partial(patch, geo), out_shape=[shape(north_tiles, Z, M)] * 2, compiler_params=params
    )(send_x, send_y, got_d)
    got_x = swap(send_x, "north", 0)
    got_y = swap(send_y, "north", 1)
    shifts = jnp.asarray(shifts)
    assert R // H == 8 and 8 * Z == LANES
    window = pl.pallas_call(
        functools.partial(own_north, geo),
        out_shape=[
            shape(R // 8, LANES, LANES), jax.ShapeDtypeStruct((LEVELS + 1, 2, LANES, LANES), BF16), shape(H + 1, 8, LANES)
        ],
        scratch_shapes=[pltpu.VMEM((R, Z, M), F32)],
        compiler_params=params,
    )(eastward, factors, shifts, w0, vertical)
    rows1 = (R >> 1) + 2
    out_rows = (R >> 1) + (R >> 2) + 4
    ext_rows, width_rows = out_rows + 4 * H, out_rows + 4 * H - 4
    return pl.pallas_call(
        functools.partial(finish, geo),
        out_shape=shape(Z, R, M),
        scratch_shapes=[
            pltpu.VMEM(dims, F32)
            for dims in (
                (north_tiles, Z, M), (north_tiles, Z, M), (ext_rows, Z, M), (out_rows, Z, M), (out_rows, Z, M),
                (rows1, Z, M), (rows1, Z, M), (width_rows, M), (width_rows, M), (H + 1, width_rows, M),
                (R // H, Z, M),
            )
        ],
        compiler_params=params,
    )(*window, *joined, *wide, *gain, got_x, got_y, got_d, g0, jnp.asarray(up), shifts)


def solution(mesh):
    tile = P("east", "north")
    return jax.shard_map(
        body,
        mesh=mesh,
        in_specs=(P(None, "east", "north"), *([tile] * 8), P()),
        out_specs=P(None, "east", "north"),
        check_vma=False,
    )
```

```python
import functools

import jax
import jax.numpy as jnp
import numpy as np
from jax import lax
from jax.experimental import pallas as pl
from jax.experimental.pallas import tpu as pltpu
from jax.sharding import PartitionSpec as P

H = 8
LANES = 128
LEVELS = 3
F32 = jnp.float32
BF16 = jnp.bfloat16
SLOT = H + 2
PER_TILE = LANES // SLOT


def tables(rows, cols):
    bases, at = [], H
    for l in range(1, LEVELS + 1):
        bases.append(at)
        at += (cols >> l) + 2
    assert at <= LANES and cols == LANES
    down = np.zeros((4, cols, LANES), np.float32)
    for variant in range(4):
        current = np.eye(cols)
        low = 0
        for l in range(1, LEVELS + 1):
            m = cols >> l
            step = np.zeros((current.shape[1], m + 2))
            for j in range(-1, m + 1):
                for f, w in ((2 * j, 0.375), (2 * j + 1, 0.375), (2 * j - 1, 0.125), (2 * j + 2, 0.125)):
                    if 0 <= f - low < current.shape[1]:
                        step[f - low, j + 1] += w
            current = current @ step
            if variant & 1:
                current[:, 0] = 0
            if variant & 2:
                current[:, -1] = 0
            low = -1
            down[variant, :, bases[l - 1] : bases[l - 1] + m + 2] = current
    frames = [0]
    for l in range(1, LEVELS + 1):
        own = bases[l - 1] + 1
        frames.append(own if own + (cols >> l) + H < LANES else H + 1)
    up = np.zeros((LEVELS + 1, LANES, LANES), np.float32)
    for l in range(LEVELS):
        m = cols >> l
        for f in range(-1, m + 1) if l else range(m):
            j = f // 2
            out, at = f + frames[l], frames[l + 1]
            up[l, j + at, out] += 0.75
            up[l, j + (1 if f % 2 else -1) + at, out] += 0.25
    for z in range(16):
        for i in range(8):
            j = i // 2 + 1
            up[LEVELS, z * 8 + i, j * 16 + z] += 0.75
            up[LEVELS, z * 8 + i, (j + (1 if i % 2 else -1)) * 16 + z] += 0.25
    for t in (down, up):
        assert (t == t.astype(jnp.bfloat16).astype(np.float32)).all()
    shifts = np.concatenate([np.eye(LANES, k=k) + np.eye(LANES, k=-k) for k in range(1, H + 1)], axis=1)
    shifts = np.concatenate([shifts, shifts], axis=0)
    return bases, frames, down.astype(jnp.bfloat16), up.astype(jnp.bfloat16), shifts.astype(jnp.bfloat16)


def place(geo, index):
    full = geo["coarse_tiles"] * PER_TILE
    if index < full:
        return divmod(index, PER_TILE)
    return geo["coarse_tiles"] + geo["R"] * H // LANES, geo["width_slots"] + index - full


def packed(geo, row, l, s):
    lane, m = lanes_of(row.shape[0]), geo["M"] >> (l + 1)
    here = (lane >= SLOT * s) & (lane < SLOT * (s + 1))
    at = SLOT * s - geo["bases"][l]
    return here, roll(row, at), roll(row, at - m + H)


def split(x):
    high = x.astype(BF16)
    return high, (x - high.astype(F32)).astype(BF16)


def mm(a, b):
    return jnp.dot(a, b, preferred_element_type=F32)


def dot_exact(x, weights):
    high, low = split(x)
    return mm(high, weights) + mm(low, weights)


def lanes_of(rows):
    return lax.broadcasted_iota(jnp.int32, (rows, LANES), 1)


def roll(x, shift):
    shift %= LANES
    return pltpu.roll(x, shift, 1) if shift else x


def taps(widths):
    grown = widths + 1.0
    inverse = 1.0 / (grown * grown)
    profile = [jnp.square(jnp.maximum(1.0 - float(k * k) * inverse, 0.0)) for k in range(1, H + 1)]
    total = profile[0]
    for p in profile[1:]:
        total = total + p
    scale = 1.0 / (1.0 + 2.0 * total)
    return [scale] + [p * scale for p in profile]


def prepare(geo, *refs):
    count = 2
    outside, (field, *rest) = refs[:count], refs[count:]
    coarse, (send_far, half, *inside) = rest[:LEVELS], rest[LEVELS:]
    sems = inside.pop()
    copies = [pltpu.make_async_copy(a, b, sems.at[i]) for i, (a, b) in enumerate(zip(outside, inside))]
    for copy in copies:
        copy.start()
    inc, table = inside
    Z, R, M, bases = geo["Z"], geo["R"], geo["M"], geo["bases"]
    e, n = lax.axis_index("east"), lax.axis_index("north")
    has_low, has_high = e > 0, e < geo["E"] - 1
    even = e % 2 == 0
    flat = field.reshape(R * Z, M)
    for copy in copies:
        copy.wait()
    for z in range(Z):
        flat[pl.ds(z, R, stride=Z), :] = inc[z]
    variant = (n == 0).astype(jnp.int32) + 2 * (n == geo["N"] - 1).astype(jnp.int32)
    weights = table[variant]
    half_flat = half.reshape(R * Z, M)
    chunk = R * Z // 4
    for c in range(4):
        half_flat[pl.ds(c * chunk, chunk), :] = dot_exact(flat[pl.ds(c * chunk, chunk), :], weights)
    source, low, top = half, 0, R
    for l in range(1, LEVELS + 1):
        r, out = R >> l, coarse[l - 1]

        def get(i, source=source, low=low, top=top):
            return source[i - low] if low <= i < top else None

        for j in range(-1, r + 1):
            total = None
            for pair, w in (((2 * j, 2 * j + 1), 0.375), ((2 * j - 1, 2 * j + 2), 0.125)):
                terms = [t for t in (get(i) for i in pair) if t is not None]
                if terms:
                    part = w * functools.reduce(jnp.add, terms)
                    total = part if total is None else total + part
            if j == -1:
                total = jnp.where(has_low, total, 0.0)
            if j == r:
                total = jnp.where(has_high, total, 0.0)
            out[j + 1] = total
        source, low, top = out, -1, r + 1
    r = R >> LEVELS
    for i in range(2):
        send_far[i] = jnp.where(even, coarse[LEVELS - 1][r + i], coarse[LEVELS - 1][i])


def gather(geo, field, *refs):
    coarse, got_far, widths, gains, send_a, send_b = refs[:LEVELS], refs[LEVELS], refs[LEVELS + 1 : 2 * LEVELS + 1], refs[2 * LEVELS + 1 : -2], refs[-2], refs[-1]
    Z, R, M, bases = geo["Z"], geo["R"], geo["M"], geo["bases"]
    even = lax.axis_index("east") % 2 == 0
    start = R - H
    send_a[0:H] = field[pl.ds(jnp.where(even, start, 0), H)]
    send_b[0:H] = field[pl.ds(jnp.where(even, 0, start), H)]
    lane = lanes_of(Z)
    for i in range(SLOT):
        def merged(picks):
            out = coarse[LEVELS - 1][picks[LEVELS - 1]]
            for l in range(LEVELS - 1, 0, -1):
                out = jnp.where(lane < bases[l], coarse[l - 1][picks[l - 1]], out)
            return out

        lower = merged([i] * LEVELS)
        upper = merged([(R >> l) - H + i for l in range(1, LEVELS + 1)])
        send_a[H + i] = jnp.where(even, upper, lower)
        send_b[H + i] = jnp.where(even, lower, upper)
    last = H + SLOT
    send_a[last] = jnp.zeros((Z, LANES), F32)
    send_b[last] = jnp.zeros((Z, LANES), F32)
    for j, ref in enumerate((*widths, *gains)):
        r, m = ref.shape
        lower = ref[pl.ds(0, 1), :].astype(F32)
        upper = ref[pl.ds(r - 1, 1), :].astype(F32)
        send_a[last, pl.ds(j, 1), pl.ds(0, m)] = jnp.where(even, upper, lower)
        send_b[last, pl.ds(j, 1), pl.ds(0, m)] = jnp.where(even, lower, upper)
    send_b[last + 1 : last + 3] = got_far[...]


def east_rows(source, factors, out, count, block, factor_at=0, source_at=0, out_at=0):
    def step(b, carry):
        east_block(source, factors, out, b * block, block, factor_at, source_at, out_at)
        return carry

    lax.fori_loop(0, count // block, step, 0)


def east_block(source, factors, out, x0, block, factor_at, source_at, out_at):
    rows = [source[x0 + i + source_at] for i in range(block + 2 * H)]
    for i in range(block):
        def factor(k):
            return factors[k, pl.ds(x0 + i + factor_at, 1), :]

        total = factor(0) * rows[i + H]
        for k in range(1, H + 1):
            total = total + factor(k) * (rows[i + H + k] + rows[i + H - k])
        out[x0 + i + out_at] = total


def interior(geo, field, widths0, factors, inner):
    for k, a in enumerate(taps(widths0[...].astype(F32))):
        factors[k] = a
    east_rows(field, factors, inner, geo["R"] - 2 * H, 4, H)


def middle(geo, *refs):
    Z, R, M, bases = geo["Z"], geo["R"], geo["M"], geo["bases"]
    it = iter(refs)
    take = lambda count: [next(it) for _ in range(count)]
    (field,) = take(1)
    coarse = take(LEVELS)
    got_a, got_b, factors, inner = take(4)
    widths, gains = take(LEVELS), take(LEVELS)
    (eastward,) = take(1)
    joined = take(LEVELS)
    send_x, send_y = take(2)
    wide, gain = take(LEVELS), take(LEVELS)
    below, above = take(2)
    e, n = lax.axis_index("east"), lax.axis_index("north")
    even = e % 2 == 0
    below[0:H] = jnp.where(even, got_b[0:H], got_a[0:H])
    below[H : 3 * H] = field[0 : 2 * H]
    above[0 : 2 * H] = field[R - 2 * H : R]
    above[2 * H : 3 * H] = jnp.where(even, got_a[0:H], got_b[0:H])
    east_rows(below, factors, eastward, H, 4)
    east_rows(above, factors, eastward, H, 4, R - H, 0, R - H)
    eastward[H : R - H] = inner[...]
    for l in range(1, LEVELS + 1):
        r, out, own = R >> l, joined[l - 1], coarse[l - 1]
        out[H : H + r + 2] = own[...]
        out[0:H] = jnp.zeros((H, Z, LANES), F32)
        out[H + r + 2 : 2 * H + r + 2] = jnp.zeros((H, Z, LANES), F32)
    for i in range(SLOT):
        a, b = got_a[H + i], got_b[H + i]
        lower, upper = jnp.where(even, b, a), jnp.where(even, a, b)
        for l in range(1, LEVELS + 1):
            r, out = R >> l, joined[l - 1]
            out[i] = out[i] + lower
            out[r + H + i] = out[r + H + i] + upper
    r, out = R >> LEVELS, joined[LEVELS - 1]
    for i in range(2):
        far = got_b[H + SLOT + 1 + i]
        out[i] = out[i] + jnp.where(even, far, 0.0)
        out[r + 2 * H + i] = out[r + 2 * H + i] + jnp.where(even, 0.0, far)
    last = H + SLOT
    rows_a, rows_b = got_a[last], got_b[last]
    lower, upper = jnp.where(even, rows_b, rows_a), jnp.where(even, rows_a, rows_b)
    for j, (own, out) in enumerate(zip((*widths, *gains), (*wide, *gain))):
        r, m = own.shape
        out[...] = jnp.zeros(out.shape, F32)
        at = geo["frames"][j % LEVELS + 1]
        out[pl.ds(H, r), pl.ds(at, m)] = own[...].astype(F32)
        out[pl.ds(H - 1, 1), pl.ds(at, m)] = lower[j : j + 1, 0:m]
        out[pl.ds(H + r, 1), pl.ds(at, m)] = upper[j : j + 1, 0:m]
    north_even = n % 2 == 0
    lane = lanes_of(Z)

    def send(t, low_side, high_side):
        send_x[t] = jnp.where(north_even, high_side, low_side)
        send_y[t] = jnp.where(north_even, low_side, high_side)

    zero = jnp.zeros((Z, LANES), F32)
    todo = [(l, i) for l in range(LEVELS) for i in range(joined[l].shape[0])]
    for t in range(geo["coarse_tiles"]):
        low_side, high_side = zero, zero
        for s, (l, i) in enumerate(todo[t * PER_TILE : (t + 1) * PER_TILE]):
            here, lower, upper = packed(geo, joined[l][i], l, s)
            low_side, high_side = jnp.where(here, lower, low_side), jnp.where(here, upper, high_side)
        send(t, low_side, high_side)
    per = LANES // H
    for t in range(R // per):
        low_side, high_side = zero, zero
        for s in range(per):
            row, at = eastward[t * per + s], 2 * H * (H - 1 - s % H) + H * (s // H)
            here = (lane >= at) & (lane < at + H)
            low_side = jnp.where(here, roll(row, at), low_side)
            high_side = jnp.where(here, roll(row, at - M + H), high_side)
        send(geo["coarse_tiles"] + t, low_side, high_side)
    low_side, high_side, q = zero, zero, 0
    for l in range(LEVELS):
        rows, m, at = wide[l].shape[0], M >> (l + 1), geo["frames"][l + 1]
        for c in range(0, rows, Z):
            have = min(rows - c, Z)
            width, weight = wide[l][pl.ds(c, have), :], gain[l][pl.ds(c, have), :]
            if have < Z:
                fill = jnp.zeros((Z - have, LANES), F32)
                width, weight = jnp.concatenate([width, fill], axis=0), jnp.concatenate([weight, fill], axis=0)
            begin = SLOT * q
            here, last_lane = (lane >= begin) & (lane < begin + H + 1), lane == begin + H + 1
            low_side = jnp.where(here, roll(width, begin - at), low_side)
            low_side = jnp.where(last_lane, roll(weight, begin + H + 1 - at), low_side)
            high_side = jnp.where(here, roll(width, begin - at - m + H + 1), high_side)
            high_side = jnp.where(last_lane, roll(weight, begin + H + 2 - at - m), high_side)
            q += 1
    for l, i in todo[geo["coarse_tiles"] * PER_TILE :]:
        here, lower, upper = packed(geo, joined[l][i], l, q)
        low_side, high_side = jnp.where(here, lower, low_side), jnp.where(here, upper, high_side)
        q += 1
    send(geo["coarse_tiles"] + R // per, low_side, high_side)


def forwarded(geo, got_d):
    even, r = lax.axis_index("east") % 2 == 0, geo["R"] >> LEVELS
    for i in range(2):
        yield i, jnp.where(even, 0.0, got_d[H + r + i])
        yield r + 2 * H + i, jnp.where(even, got_d[H + i], 0.0)


def patch(geo, before_x, before_y, got_d, send_x, send_y):
    north_even = lax.axis_index("north") % 2 == 0
    send_x[...] = before_x[...]
    send_y[...] = before_y[...]
    first = sum((geo["R"] >> l) + 2 * H + 2 for l in range(1, LEVELS))
    for i, row in forwarded(geo, got_d):
        t, s = place(geo, first + i)
        here, lower, upper = packed(geo, row, LEVELS - 1, s)
        send_x[t] = send_x[t] + jnp.where(here, jnp.where(north_even, upper, lower), 0.0)
        send_y[t] = send_y[t] + jnp.where(here, jnp.where(north_even, lower, upper), 0.0)


def own_north(geo, eastward, factors, shifts, widths0, vertical, mixed, matrices, edge_taps, north):
    R, Z = geo["R"], geo["Z"]
    for x0 in range(0, R, R // 2):
        north_rows(eastward, north, range(x0, x0 + R // 2), lambda k, x: factors[k, pl.ds(x, 1), :], shifts)
    matrix = kron(vertical[0], True)
    for b in range(R // 8):
        mixed[b] = mix(matrix, north[8 * b : 8 * b + 8].reshape(8 * Z, LANES))
    for l in range(LEVELS + 1):
        for i, part in enumerate(kron(vertical[l] * 4.0**l, False)):
            matrices[l, i] = part
    lane8 = lanes_of(8)
    slot = lane8 % (2 * H)
    width = jnp.zeros((H, LANES), F32)
    for s in range(H):
        rows = widths0[pl.ds(s, R // H, stride=H), :].astype(F32)
        at = H - 1 - s
        width = jnp.where(lane8 // (2 * H) == at, roll(rows, 2 * H * at + H), width)
    for k, a in enumerate(taps(width)):
        edge_taps[k] = jnp.where((slot >= H - k) & (slot < H + k), a, 0.0)


def north_rows(source, target, rows, factor, shifts):
    Z = source.shape[1]
    data = source[pl.ds(rows[0], len(rows))].reshape(len(rows) * Z, LANES)
    pair = jnp.concatenate(split(data), axis=1)
    for k in range(1, H + 1, 2):
        moved = mm(pair, shifts[:, (k - 1) * LANES : (k + 1) * LANES])
        for i, x in enumerate(rows):
            here = moved[i * Z : (i + 1) * Z]
            before = factor(0, x) * source[x] if k == 1 else target[x]
            target[x] = before + factor(k, x) * here[:, :LANES] + factor(k + 1, x) * here[:, LANES:]


def kron(vertical, transposed):
    Z = 16
    i = lax.broadcasted_iota(jnp.int32, (LANES, Z), 0)
    a = lax.broadcasted_iota(jnp.int32, (LANES, Z), 1)
    left = ((i // 8 if transposed else i % Z) == a).astype(F32).astype(BF16)
    b = lax.broadcasted_iota(jnp.int32, (Z, LANES), 0)
    o = lax.broadcasted_iota(jnp.int32, (Z, LANES), 1)
    right = (o % Z == b).astype(F32).astype(BF16)
    p = lax.broadcasted_iota(jnp.int32, (LANES, LANES), 0)
    q = lax.broadcasted_iota(jnp.int32, (LANES, LANES), 1)
    mask = (p % 8 if transposed else p // Z) == q // Z
    return [jnp.where(mask, mm(mm(left, part).astype(BF16), right), 0.0).astype(BF16) for part in split(vertical)]


def mix(matrix, data):
    high, low = split(data)
    return mm(matrix[0], high) + mm(matrix[0], low) + mm(matrix[1], high)


def arrange(geo):
    rows_of = [geo["R"] >> l for l in range(1, LEVELS + 1)]
    groups = [[0], list(range(1, LEVELS))]
    wire_at = [sum(r + 2 * H + 2 for r in rows_of[:l]) for l in range(LEVELS)]
    begins = lambda more: [0] + [rows_of[0] + more] * (LEVELS - 1)
    frames, M = geo["frames"], geo["M"]
    used = [frames[l] + d for l in range(2, LEVELS + 1) for d in range(-H - 1, (M >> l) + H + 1)]
    assert len(set(used)) == len(used)
    return rows_of, groups, wire_at, begins


def side_rows(geo, got, high):
    frames, M, wire_at = geo["frames"], geo["M"], arrange(geo)[2]
    lane = lanes_of(geo["Z"])
    first, masks = [], []
    for l in range(LEVELS):
        m, at = M >> (l + 1), frames[l + 1]
        begin = jnp.where(high, at + m - 1, at - H - 1)
        first.append(begin)
        masks.append((lane >= begin) & (lane < begin + SLOT))

    def row(l, i):
        t, s = place(geo, wire_at[l] + i)
        return jnp.where(masks[l], pltpu.roll(got[t], (first[l] + LANES - SLOT * s) % LANES, 1), 0.0)

    return row


def side_edge(geo, got, high, edge_taps, t):
    Z = geo["Z"]
    lane = lanes_of(Z) % (2 * H)
    inside = (lane < H) != high
    shift = jnp.where(high, 0 if t % 2 else H, LANES - H if t % 2 else 0)
    halo = jnp.where(inside, pltpu.roll(got[geo["coarse_tiles"] + t // 2], shift, 1), 0.0)
    total = jnp.zeros((Z, LANES), F32)
    for k in range(1, H + 1):
        total = total + edge_taps[k, pl.ds(t, 1), :] * pltpu.roll(halo, jnp.where(high, LANES - k, k), 1)
    return jnp.where(inside, 0.0, total)


def near_side(geo, *refs):
    joined, (got_x, got_d, edge_taps, ext, edge) = refs[:LEVELS], refs[LEVELS:]
    Z, M, bases, frames = geo["Z"], geo["M"], geo["bases"], geo["frames"]
    high = lax.axis_index("north") % 2 == 0
    lane = lanes_of(Z)
    rows_of, groups, _, begins = arrange(geo)
    extra = dict(forwarded(geo, got_d))
    side = side_rows(geo, got_x, high)

    def source_row(l, i):
        m, at = M >> (l + 1), frames[l + 1]
        own = joined[l][i]
        if l == LEVELS - 1 and i in extra:
            own = own + extra[i]
        own = roll(own, at - 1 - bases[l])
        return jnp.where((lane >= at - 1) & (lane < at + m + 1), own, 0.0) + side(l, i)

    for g in groups:
        for i in range(rows_of[g[0]] + 2 * H + 2):
            parts = [source_row(l, i) for l in g if i < rows_of[l] + 2 * H + 2]
            ext[begins(2 * H + 2)[g[0]] + i] = functools.reduce(jnp.add, parts)
    for t in range(geo["R"] // H):
        edge[t] = side_edge(geo, got_x, high, edge_taps, t)


def finish(geo, *refs):
    Z, R, M, bases, frames = geo["Z"], geo["R"], geo["M"], geo["bases"], geo["frames"]
    it = iter(refs)
    take = lambda count: [next(it) for _ in range(count)]
    mixed0, matrices, edge_taps = take(3)
    near, near_edge = take(2)
    wide, gain = take(LEVELS), take(LEVELS)
    got_x, got_y, gain0, table, shifts = take(5)
    (result_hbm,) = take(1)
    ext, passed, north, result, spread, wf, gf, cf, edge, out, sems = take(11)
    e, n = lax.axis_index("east"), lax.axis_index("north")
    has_low, has_high = e > 0, e < geo["E"] - 1
    north_even = n % 2 == 0
    lane = lanes_of(Z)
    lane8 = lanes_of(8)
    per = LANES // H
    base = geo["coarse_tiles"] + R // per
    rows_of, groups, _, begins = arrange(geo)
    ext_at, out_at, width_at = begins(2 * H + 2), begins(2), begins(2 * H)
    tile_x, tile_y = got_x[base], got_y[base]
    tile_low, tile_high = jnp.where(north_even, tile_y, tile_x), jnp.where(north_even, tile_x, tile_y)
    side = side_rows(geo, got_y, jnp.logical_not(north_even))

    def widths_chunk(l, c):
        r, m, at = rows_of[l], M >> (l + 1), frames[l + 1]
        row = c % Z
        begin = SLOT * (sum(-(-(q + 2 * H) // Z) for q in rows_of[:l]) + c // Z)
        lower, upper = tile_low[row : row + 8], tile_high[row : row + 8]
        width = jnp.where(
            lane8 < at,
            roll(lower, at - H - 1 - begin),
            jnp.where(lane8 < at + m, wide[l][pl.ds(c, 8), :], roll(upper, at + m - begin)),
        )
        width = jnp.where((lane8 >= at - H - 1) & (lane8 < at + m + H + 1), width, 0.0)
        weight = jnp.where(lane8 == at - 1, roll(lower, at - H - 2 - begin), gain[l][pl.ds(c, 8), :])
        return width, jnp.where(lane8 == at + m, roll(upper, at + m - H - 1 - begin), weight)

    for g in groups:
        r = rows_of[g[0]]
        for c in range(0, r + 2 * H, 8):
            parts = [widths_chunk(l, c) for l in g if c < rows_of[l] + 2 * H]
            wf[pl.ds(width_at[g[0]] + c, 8), :] = functools.reduce(jnp.add, [p[0] for p in parts])
            gf[pl.ds(width_at[g[0]] + c, 8), :] = functools.reduce(jnp.add, [p[1] for p in parts])
    for k, a in enumerate(taps(wf[...])):
        cf[k] = a
    for g in groups:
        r = rows_of[g[0]]
        for i in range(r + 2 * H + 2):
            parts = [side(l, i) for l in g if i < rows_of[l] + 2 * H + 2]
            ext[ext_at[g[0]] + i] = functools.reduce(jnp.add, parts, near[ext_at[g[0]] + i])
        for x in range(0, r + 2, 4):
            east_block(ext, cf, passed, x, min(4, r + 2 - x), width_at[g[0]] + H - 1, ext_at[g[0]], out_at[g[0]])

    total = rows_of[0] + rows_of[1] + 4

    def coarse_factor(k, x):
        l = 0 if x < out_at[1] else 1
        return cf[k, pl.ds(width_at[l] + H - 1 + x - out_at[l], 1), :]

    half = -(-total // 2)
    north_rows(passed, north, range(0, half), coarse_factor, shifts)
    north_rows(passed, north, range(half, total), coarse_factor, shifts)
    for l in range(LEVELS - 1, -1, -1):
        r, m, at = R >> (l + 1), M >> (l + 1), frames[l + 1]
        blocks = (r + 2 + 7) // 8
        matrix = [matrices[l + 1, 0], matrices[l + 1, 1]]
        for g in range(blocks):
            have = min(8, r + 2 - 8 * g)
            data = north[out_at[l] + 8 * g : out_at[l] + 8 * g + have].reshape(have * Z, LANES)
            if have < 8:
                data = jnp.concatenate([data, jnp.zeros(((8 - have) * Z, LANES), F32)], axis=0)
            mixed = mix(matrix, data)
            for i in range(have):
                row = 8 * g + i
                result[row] = gf[pl.ds(width_at[l] + row + H - 1, 1), :] * mixed[i * Z : (i + 1) * Z]
        if l < LEVELS - 1:
            inside = ((lane >= at) | (n > 0)) & ((lane < at + m) | (n < geo["N"] - 1))
            for row in range(-1, r + 1):
                j = row // 2
                other = j + (1 if row % 2 else -1)
                summed = result[row + 1] + 0.75 * spread[j + 1] + 0.25 * spread[other + 1]
                keep = inside
                if row == -1:
                    keep = keep & has_low
                if row == r:
                    keep = keep & has_high
                result[row + 1] = jnp.where(keep, summed, 0.0)
        flat = result.reshape(result.shape[0] * Z, LANES)
        spread_flat = spread.reshape(spread.shape[0] * Z, LANES)
        spread_flat[pl.ds(0, (r + 2) * Z), :] = dot_exact(flat[pl.ds(0, (r + 2) * Z), :], table[l])
    for t in range(R // H):
        edge[t] = near_edge[t] + side_edge(geo, got_y, jnp.logical_not(north_even), edge_taps, t)
    edge_flat = edge.reshape(R // H * Z, LANES)
    edge_flat[...] = mix([matrices[0, 0], matrices[0, 1]], edge_flat[...])
    widen = table[LEVELS][:, 0 : 6 * Z]
    at_edge = (lane8 < H) | (lane8 >= M - H)
    copies = []
    for b in range(R // 8):
        high, low = split(spread[4 * b : 4 * b + 6].reshape(6 * Z, LANES))
        added = mm(widen, high) + mm(widen, low)
        weight = gain0[pl.ds(8 * b, 8), :]
        for z in range(Z):
            row = edge_flat[pl.ds(b * Z + z, 8, stride=0), :]
            moved = pltpu.roll(row, H, 1, stride=2 * H, stride_axis=0)
            here = mixed0[b, z * 8 : z * 8 + 8, :] + jnp.where(at_edge, moved, 0.0)
            out[z, pl.ds(8 * b, 8), :] = weight * here + added[z * 8 : z * 8 + 8]
        if b % 2:
            part = pl.ds(8 * (b - 1), 16)
            copies.append(pltpu.make_async_copy(out.at[:, part, :], result_hbm.at[:, part, :], sems.at[b // 2]))
            copies[-1].start()
    for copy in copies:
        copy.wait()


def swap(x, axis, first):
    route = [(i, i + 1) for i in range(first, lax.axis_size(axis) - 1, 2)]
    return lax.ppermute(x, axis, route + [(j, i) for i, j in route])


def body(inc, w0, w1, w2, w3, g0, g1, g2, g3, vertical):
    Z, R, M = inc.shape
    bases, frames, down, up, shifts = tables(R, M)
    total_rows = sum((R >> l) + 2 * H + 2 for l in range(1, LEVELS + 1))
    width_slots = sum(-(-((R >> l) + 2 * H) // Z) for l in range(1, LEVELS + 1))
    geo = dict(
        Z=Z, R=R, M=M, bases=bases, frames=frames, E=lax.axis_size("east"), N=lax.axis_size("north"),
        coarse_tiles=-(-(total_rows - PER_TILE + width_slots) // PER_TILE), width_slots=width_slots,
    )
    shape = lambda *dims: jax.ShapeDtypeStruct(dims, F32)
    levels = range(1, LEVELS + 1)
    params = pltpu.CompilerParams(vmem_limit_bytes=48 * 1024 * 1024)
    east_tiles = H + SLOT + 1
    given = (inc, jnp.asarray(down))
    outs = pl.pallas_call(
        functools.partial(prepare, geo),
        out_shape=[shape(R, Z, M)] + [shape((R >> l) + 2, Z, M) for l in levels]
        + [shape(2, Z, M)],
        in_specs=[pl.BlockSpec(memory_space=pltpu.HBM)] * len(given),
        scratch_shapes=[pltpu.VMEM((R, Z, M), F32)] + [pltpu.VMEM(x.shape, x.dtype) for x in given]
        + [pltpu.SemaphoreType.DMA((len(given),))],
        compiler_params=params,
    )(*[pltpu.with_memory_space_constraint(x, pltpu.HBM) for x in given])
    field, coarse, send_far = outs[0], outs[1 : 1 + LEVELS], outs[1 + LEVELS]
    got_far = swap(send_far, "east", 0)
    send_a, send_b = pl.pallas_call(
        functools.partial(gather, geo),
        out_shape=[shape(east_tiles, Z, M), shape(east_tiles + 2, Z, M)],
        compiler_params=params,
    )(field, *coarse, got_far, w1, w2, w3, g1, g2, g3)
    got_b = swap(send_b, "east", 1)
    got_a = swap(send_a, "east", 0)
    factors, inner = pl.pallas_call(
        functools.partial(interior, geo),
        out_shape=[shape(H + 1, R, M), shape(R - 2 * H, Z, M)],
        compiler_params=params,
    )(field, w0)
    forward, inner, got_a = lax.optimization_barrier((got_b, inner, got_a))
    got_d = swap(forward, "east", 0)
    wide_shapes = [shape((R >> l) + 2 * H, M) for l in levels]
    north_tiles = geo["coarse_tiles"] + R * H // LANES + 1
    outs = pl.pallas_call(
        functools.partial(middle, geo),
        out_shape=[shape(R, Z, M)] + [shape((R >> l) + 2 * H + 2, Z, M) for l in levels]
        + [shape(north_tiles, Z, M)] * 2 + wide_shapes * 2,
        scratch_shapes=[pltpu.VMEM((3 * H, Z, M), F32)] * 2,
        compiler_params=params,
    )(field, *coarse, got_a, got_b, factors, inner, w1, w2, w3, g1, g2, g3)
    eastward = outs[0]
    joined, (send_x, send_y) = outs[1 : 1 + LEVELS], outs[1 + LEVELS : 3 + LEVELS]
    wide, gain = outs[3 + LEVELS : 3 + 2 * LEVELS], outs[3 + 2 * LEVELS :]
    send_x, send_y = pl.pallas_call(
        functools.partial(patch, geo), out_shape=[shape(north_tiles, Z, M)] * 2, compiler_params=params
    )(send_x, send_y, got_d)
    got_x = swap(send_x, "north", 0)
    got_y = swap(send_y, "north", 1)
    shifts = jnp.asarray(shifts)
    assert R // H == 8 and 8 * Z == LANES
    window = pl.pallas_call(
        functools.partial(own_north, geo),
        out_shape=[
            shape(R // 8, LANES, LANES), jax.ShapeDtypeStruct((LEVELS + 1, 2, LANES, LANES), BF16), shape(H + 1, 8, LANES)
        ],
        scratch_shapes=[pltpu.VMEM((R, Z, M), F32)],
        compiler_params=params,
    )(eastward, factors, shifts, w0, vertical)
    rows1 = (R >> 1) + 2
    out_rows = (R >> 1) + (R >> 2) + 4
    ext_rows, width_rows = out_rows + 4 * H, out_rows + 4 * H - 4
    near = pl.pallas_call(
        functools.partial(near_side, geo), out_shape=[shape(ext_rows, Z, M), shape(R // H, Z, M)], compiler_params=params
    )(*joined, got_x, got_d, window[2])
    return pl.pallas_call(
        functools.partial(finish, geo),
        out_shape=shape(Z, R, M),
        out_specs=pl.BlockSpec(memory_space=pltpu.HBM),
        scratch_shapes=[
            pltpu.VMEM(dims, F32)
            for dims in (
                (ext_rows, Z, M), (out_rows, Z, M), (out_rows, Z, M),
                (rows1, Z, M), (rows1, Z, M), (width_rows, M), (width_rows, M), (H + 1, width_rows, M),
                (R // H, Z, M), (Z, R, M),
            )
        ] + [pltpu.SemaphoreType.DMA((R // 16,))],
        compiler_params=params,
    )(*window, *near, *wide, *gain, got_x, got_y, g0, jnp.asarray(up), shifts)


def solution(mesh):
    tile = P("east", "north")
    return jax.shard_map(
        body,
        mesh=mesh,
        in_specs=(P(None, "east", "north"), *([tile] * 8), P()),
        out_specs=P(None, "east", "north"),
        check_vma=False,
    )
```

```python
import functools

import jax
import jax.numpy as jnp
import numpy as np
from jax import lax
from jax.experimental import pallas as pl
from jax.experimental.pallas import tpu as pltpu
from jax.sharding import PartitionSpec as P

H = 8
LANES = 128
LEVELS = 3
F32 = jnp.float32
BF16 = jnp.bfloat16
SLOT = H + 2
PER_TILE = LANES // SLOT


def tables(rows, cols):
    bases, at = [], H
    for l in range(1, LEVELS + 1):
        bases.append(at)
        at += (cols >> l) + 2
    assert at <= LANES and cols == LANES
    down = np.zeros((4, cols, LANES), np.float32)
    for variant in range(4):
        current = np.eye(cols)
        low = 0
        for l in range(1, LEVELS + 1):
            m = cols >> l
            step = np.zeros((current.shape[1], m + 2))
            for j in range(-1, m + 1):
                for f, w in ((2 * j, 0.375), (2 * j + 1, 0.375), (2 * j - 1, 0.125), (2 * j + 2, 0.125)):
                    if 0 <= f - low < current.shape[1]:
                        step[f - low, j + 1] += w
            current = current @ step
            if variant & 1:
                current[:, 0] = 0
            if variant & 2:
                current[:, -1] = 0
            low = -1
            down[variant, :, bases[l - 1] : bases[l - 1] + m + 2] = current
    frames = [0]
    for l in range(1, LEVELS + 1):
        own = bases[l - 1] + 1
        frames.append(own if own + (cols >> l) + H < LANES else H + 1)
    up = np.zeros((LEVELS + 1, LANES, LANES), np.float32)
    for l in range(LEVELS):
        m = cols >> l
        for f in range(-1, m + 1) if l else range(m):
            j = f // 2
            out, at = f + frames[l], frames[l + 1]
            up[l, j + at, out] += 0.75
            up[l, j + (1 if f % 2 else -1) + at, out] += 0.25
    for z in range(16):
        for i in range(8):
            j = i // 2 + 1
            up[LEVELS, z * 8 + i, j * 16 + z] += 0.75
            up[LEVELS, z * 8 + i, (j + (1 if i % 2 else -1)) * 16 + z] += 0.25
    for t in (down, up):
        assert (t == t.astype(jnp.bfloat16).astype(np.float32)).all()
    shifts = np.concatenate([np.eye(LANES, k=k) + np.eye(LANES, k=-k) for k in range(1, H + 1)], axis=1)
    shifts = np.concatenate([shifts, shifts], axis=0)
    return bases, frames, down.astype(jnp.bfloat16), up.astype(jnp.bfloat16), shifts.astype(jnp.bfloat16)


def place(geo, index):
    full = geo["coarse_tiles"] * PER_TILE
    if index < full:
        return divmod(index, PER_TILE)
    return geo["coarse_tiles"] + geo["R"] * H // LANES, geo["width_slots"] + index - full


def packed(geo, row, l, s):
    lane, m = lanes_of(row.shape[0]), geo["M"] >> (l + 1)
    here = (lane >= SLOT * s) & (lane < SLOT * (s + 1))
    at = SLOT * s - geo["bases"][l]
    return here, roll(row, at), roll(row, at - m + H)


def split(x):
    high = x.astype(BF16)
    return high, (x - high.astype(F32)).astype(BF16)


def mm(a, b):
    return jnp.dot(a, b, preferred_element_type=F32)


def dot_exact(x, weights):
    high, low = split(x)
    return mm(high, weights) + mm(low, weights)


def lanes_of(rows):
    return lax.broadcasted_iota(jnp.int32, (rows, LANES), 1)


def roll(x, shift):
    shift %= LANES
    return pltpu.roll(x, shift, 1) if shift else x


def taps(widths):
    grown = widths + 1.0
    inverse = 1.0 / (grown * grown)
    profile = [jnp.square(jnp.maximum(1.0 - float(k * k) * inverse, 0.0)) for k in range(1, H + 1)]
    total = profile[0]
    for p in profile[1:]:
        total = total + p
    scale = 1.0 / (1.0 + 2.0 * total)
    return [scale] + [p * scale for p in profile]


def prepare(geo, *refs):
    count = 2
    outside, (field, *rest) = refs[:count], refs[count:]
    coarse, (send_far, half, *inside) = rest[:LEVELS], rest[LEVELS:]
    sems = inside.pop()
    copies = [pltpu.make_async_copy(a, b, sems.at[i]) for i, (a, b) in enumerate(zip(outside, inside))]
    for copy in copies:
        copy.start()
    inc, table = inside
    Z, R, M, bases = geo["Z"], geo["R"], geo["M"], geo["bases"]
    e, n = lax.axis_index("east"), lax.axis_index("north")
    has_low, has_high = e > 0, e < geo["E"] - 1
    even = e % 2 == 0
    flat = field.reshape(R * Z, M)
    for copy in copies:
        copy.wait()
    for z in range(Z):
        flat[pl.ds(z, R, stride=Z), :] = inc[z]
    variant = (n == 0).astype(jnp.int32) + 2 * (n == geo["N"] - 1).astype(jnp.int32)
    weights = table[variant]
    half_flat = half.reshape(R * Z, M)
    chunk = R * Z // 4
    for c in range(4):
        half_flat[pl.ds(c * chunk, chunk), :] = dot_exact(flat[pl.ds(c * chunk, chunk), :], weights)
    source, low, top = half, 0, R
    for l in range(1, LEVELS + 1):
        r, out = R >> l, coarse[l - 1]

        def get(i, source=source, low=low, top=top):
            return source[i - low] if low <= i < top else None

        for j in range(-1, r + 1):
            total = None
            for pair, w in (((2 * j, 2 * j + 1), 0.375), ((2 * j - 1, 2 * j + 2), 0.125)):
                terms = [t for t in (get(i) for i in pair) if t is not None]
                if terms:
                    part = w * functools.reduce(jnp.add, terms)
                    total = part if total is None else total + part
            if j == -1:
                total = jnp.where(has_low, total, 0.0)
            if j == r:
                total = jnp.where(has_high, total, 0.0)
            out[j + 1] = total
        source, low, top = out, -1, r + 1
    r = R >> LEVELS
    for i in range(2):
        send_far[i] = jnp.where(even, coarse[LEVELS - 1][r + i], coarse[LEVELS - 1][i])


def gather(geo, field, *refs):
    coarse, got_far, widths, gains, send_a, send_b = refs[:LEVELS], refs[LEVELS], refs[LEVELS + 1 : 2 * LEVELS + 1], refs[2 * LEVELS + 1 : -2], refs[-2], refs[-1]
    Z, R, M, bases = geo["Z"], geo["R"], geo["M"], geo["bases"]
    even = lax.axis_index("east") % 2 == 0
    start = R - H
    send_a[0:H] = field[pl.ds(jnp.where(even, start, 0), H)]
    send_b[0:H] = field[pl.ds(jnp.where(even, 0, start), H)]
    lane = lanes_of(Z)
    for i in range(SLOT):
        def merged(picks):
            out = coarse[LEVELS - 1][picks[LEVELS - 1]]
            for l in range(LEVELS - 1, 0, -1):
                out = jnp.where(lane < bases[l], coarse[l - 1][picks[l - 1]], out)
            return out

        lower = merged([i] * LEVELS)
        upper = merged([(R >> l) - H + i for l in range(1, LEVELS + 1)])
        send_a[H + i] = jnp.where(even, upper, lower)
        send_b[H + i] = jnp.where(even, lower, upper)
    last = H + SLOT
    send_a[last] = jnp.zeros((Z, LANES), F32)
    send_b[last] = jnp.zeros((Z, LANES), F32)
    for j, ref in enumerate((*widths, *gains)):
        r, m = ref.shape
        lower = ref[pl.ds(0, 1), :].astype(F32)
        upper = ref[pl.ds(r - 1, 1), :].astype(F32)
        send_a[last, pl.ds(j, 1), pl.ds(0, m)] = jnp.where(even, upper, lower)
        send_b[last, pl.ds(j, 1), pl.ds(0, m)] = jnp.where(even, lower, upper)
    send_b[last + 1 : last + 3] = got_far[...]


def east_rows(source, factors, out, count, block, factor_at=0, source_at=0, out_at=0):
    def step(b, carry):
        east_block(source, factors, out, b * block, block, factor_at, source_at, out_at)
        return carry

    lax.fori_loop(0, count // block, step, 0)


def east_block(source, factors, out, x0, block, factor_at, source_at, out_at):
    rows = [source[x0 + i + source_at] for i in range(block + 2 * H)]
    for i in range(block):
        def factor(k):
            return factors[k, pl.ds(x0 + i + factor_at, 1), :]

        total = factor(0) * rows[i + H]
        for k in range(1, H + 1):
            total = total + factor(k) * (rows[i + H + k] + rows[i + H - k])
        out[x0 + i + out_at] = total


def interior(geo, field, widths0, factors, inner):
    for k, a in enumerate(taps(widths0[...].astype(F32))):
        factors[k] = a
    east_rows(field, factors, inner, geo["R"] - 2 * H, 4, H)


def middle(geo, *refs):
    Z, R, M, bases = geo["Z"], geo["R"], geo["M"], geo["bases"]
    it = iter(refs)
    take = lambda count: [next(it) for _ in range(count)]
    (field,) = take(1)
    coarse = take(LEVELS)
    got_a, got_b, factors, inner = take(4)
    widths, gains = take(LEVELS), take(LEVELS)
    (eastward,) = take(1)
    joined = take(LEVELS)
    send_x, send_y = take(2)
    wide, gain = take(LEVELS), take(LEVELS)
    below, above = take(2)
    e, n = lax.axis_index("east"), lax.axis_index("north")
    even = e % 2 == 0
    below[0:H] = jnp.where(even, got_b[0:H], got_a[0:H])
    below[H : 3 * H] = field[0 : 2 * H]
    above[0 : 2 * H] = field[R - 2 * H : R]
    above[2 * H : 3 * H] = jnp.where(even, got_a[0:H], got_b[0:H])
    east_rows(below, factors, eastward, H, 4)
    east_rows(above, factors, eastward, H, 4, R - H, 0, R - H)
    eastward[H : R - H] = inner[...]
    for l in range(1, LEVELS + 1):
        r, out, own = R >> l, joined[l - 1], coarse[l - 1]
        out[H : H + r + 2] = own[...]
        out[0:H] = jnp.zeros((H, Z, LANES), F32)
        out[H + r + 2 : 2 * H + r + 2] = jnp.zeros((H, Z, LANES), F32)
    for i in range(SLOT):
        a, b = got_a[H + i], got_b[H + i]
        lower, upper = jnp.where(even, b, a), jnp.where(even, a, b)
        for l in range(1, LEVELS + 1):
            r, out = R >> l, joined[l - 1]
            out[i] = out[i] + lower
            out[r + H + i] = out[r + H + i] + upper
    r, out = R >> LEVELS, joined[LEVELS - 1]
    for i in range(2):
        far = got_b[H + SLOT + 1 + i]
        out[i] = out[i] + jnp.where(even, far, 0.0)
        out[r + 2 * H + i] = out[r + 2 * H + i] + jnp.where(even, 0.0, far)
    last = H + SLOT
    rows_a, rows_b = got_a[last], got_b[last]
    lower, upper = jnp.where(even, rows_b, rows_a), jnp.where(even, rows_a, rows_b)
    for j, (own, out) in enumerate(zip((*widths, *gains), (*wide, *gain))):
        r, m = own.shape
        out[...] = jnp.zeros(out.shape, F32)
        at = geo["frames"][j % LEVELS + 1]
        out[pl.ds(H, r), pl.ds(at, m)] = own[...].astype(F32)
        out[pl.ds(H - 1, 1), pl.ds(at, m)] = lower[j : j + 1, 0:m]
        out[pl.ds(H + r, 1), pl.ds(at, m)] = upper[j : j + 1, 0:m]
    north_even = n % 2 == 0
    lane = lanes_of(Z)

    def send(t, low_side, high_side):
        send_x[t] = jnp.where(north_even, high_side, low_side)
        send_y[t] = jnp.where(north_even, low_side, high_side)

    zero = jnp.zeros((Z, LANES), F32)
    todo = [(l, i) for l in range(LEVELS) for i in range(joined[l].shape[0])]
    for t in range(geo["coarse_tiles"]):
        low_side, high_side = zero, zero
        for s, (l, i) in enumerate(todo[t * PER_TILE : (t + 1) * PER_TILE]):
            here, lower, upper = packed(geo, joined[l][i], l, s)
            low_side, high_side = jnp.where(here, lower, low_side), jnp.where(here, upper, high_side)
        send(t, low_side, high_side)
    per = LANES // H
    for t in range(R // per):
        low_side, high_side = zero, zero
        for s in range(per):
            row, at = eastward[t * per + s], 2 * H * (H - 1 - s % H) + H * (s // H)
            here = (lane >= at) & (lane < at + H)
            low_side = jnp.where(here, roll(row, at), low_side)
            high_side = jnp.where(here, roll(row, at - M + H), high_side)
        send(geo["coarse_tiles"] + t, low_side, high_side)
    low_side, high_side, q = zero, zero, 0
    for l in range(LEVELS):
        rows, m, at = wide[l].shape[0], M >> (l + 1), geo["frames"][l + 1]
        for c in range(0, rows, Z):
            have = min(rows - c, Z)
            width, weight = wide[l][pl.ds(c, have), :], gain[l][pl.ds(c, have), :]
            if have < Z:
                fill = jnp.zeros((Z - have, LANES), F32)
                width, weight = jnp.concatenate([width, fill], axis=0), jnp.concatenate([weight, fill], axis=0)
            begin = SLOT * q
            here, last_lane = (lane >= begin) & (lane < begin + H + 1), lane == begin + H + 1
            low_side = jnp.where(here, roll(width, begin - at), low_side)
            low_side = jnp.where(last_lane, roll(weight, begin + H + 1 - at), low_side)
            high_side = jnp.where(here, roll(width, begin - at - m + H + 1), high_side)
            high_side = jnp.where(last_lane, roll(weight, begin + H + 2 - at - m), high_side)
            q += 1
    for l, i in todo[geo["coarse_tiles"] * PER_TILE :]:
        here, lower, upper = packed(geo, joined[l][i], l, q)
        low_side, high_side = jnp.where(here, lower, low_side), jnp.where(here, upper, high_side)
        q += 1
    send(geo["coarse_tiles"] + R // per, low_side, high_side)


def forwarded(geo, got_d):
    even, r = lax.axis_index("east") % 2 == 0, geo["R"] >> LEVELS
    for i in range(2):
        yield i, jnp.where(even, 0.0, got_d[H + r + i])
        yield r + 2 * H + i, jnp.where(even, got_d[H + i], 0.0)


def patch(geo, before_x, before_y, got_d, send_x, send_y):
    north_even = lax.axis_index("north") % 2 == 0
    send_x[...] = before_x[...]
    send_y[...] = before_y[...]
    first = sum((geo["R"] >> l) + 2 * H + 2 for l in range(1, LEVELS))
    for i, row in forwarded(geo, got_d):
        t, s = place(geo, first + i)
        here, lower, upper = packed(geo, row, LEVELS - 1, s)
        send_x[t] = send_x[t] + jnp.where(here, jnp.where(north_even, upper, lower), 0.0)
        send_y[t] = send_y[t] + jnp.where(here, jnp.where(north_even, lower, upper), 0.0)


def own_north(geo, eastward, factors, shifts, widths0, vertical, mixed, matrices, edge_taps, north):
    R, Z = geo["R"], geo["Z"]
    for x0 in range(0, R, R // 2):
        north_rows(eastward, north, range(x0, x0 + R // 2), lambda k, x: factors[k, pl.ds(x, 1), :], shifts)
    matrix = kron(vertical[0], True)
    for b in range(R // 8):
        mixed[b] = mix(matrix, north[8 * b : 8 * b + 8].reshape(8 * Z, LANES))
    for l in range(LEVELS + 1):
        for i, part in enumerate(kron(vertical[l] * 4.0**l, False)):
            matrices[l, i] = part
    lane8 = lanes_of(8)
    slot = lane8 % (2 * H)
    width = jnp.zeros((H, LANES), F32)
    for s in range(H):
        rows = widths0[pl.ds(s, R // H, stride=H), :].astype(F32)
        at = H - 1 - s
        width = jnp.where(lane8 // (2 * H) == at, roll(rows, 2 * H * at + H), width)
    for k, a in enumerate(taps(width)):
        edge_taps[k] = jnp.where((slot >= H - k) & (slot < H + k), a, 0.0)


def north_rows(source, target, rows, factor, shifts):
    Z = source.shape[1]
    data = source[pl.ds(rows[0], len(rows))].reshape(len(rows) * Z, LANES)
    pair = jnp.concatenate(split(data), axis=1)
    for k in range(1, H + 1, 2):
        moved = mm(pair, shifts[:, (k - 1) * LANES : (k + 1) * LANES])
        for i, x in enumerate(rows):
            here = moved[i * Z : (i + 1) * Z]
            before = factor(0, x) * source[x] if k == 1 else target[x]
            target[x] = before + factor(k, x) * here[:, :LANES] + factor(k + 1, x) * here[:, LANES:]


def kron(vertical, transposed):
    Z = 16
    i = lax.broadcasted_iota(jnp.int32, (LANES, Z), 0)
    a = lax.broadcasted_iota(jnp.int32, (LANES, Z), 1)
    left = ((i // 8 if transposed else i % Z) == a).astype(F32).astype(BF16)
    b = lax.broadcasted_iota(jnp.int32, (Z, LANES), 0)
    o = lax.broadcasted_iota(jnp.int32, (Z, LANES), 1)
    right = (o % Z == b).astype(F32).astype(BF16)
    p = lax.broadcasted_iota(jnp.int32, (LANES, LANES), 0)
    q = lax.broadcasted_iota(jnp.int32, (LANES, LANES), 1)
    mask = (p % 8 if transposed else p // Z) == q // Z
    return [jnp.where(mask, mm(mm(left, part).astype(BF16), right), 0.0).astype(BF16) for part in split(vertical)]


def mix(matrix, data):
    high, low = split(data)
    return mm(matrix[0], high) + mm(matrix[0], low) + mm(matrix[1], high)


def arrange(geo):
    rows_of = [geo["R"] >> l for l in range(1, LEVELS + 1)]
    groups = [[0], list(range(1, LEVELS))]
    wire_at = [sum(r + 2 * H + 2 for r in rows_of[:l]) for l in range(LEVELS)]
    begins = lambda more: [0] + [rows_of[0] + more] * (LEVELS - 1)
    frames, M = geo["frames"], geo["M"]
    used = [frames[l] + d for l in range(2, LEVELS + 1) for d in range(-H - 1, (M >> l) + H + 1)]
    assert len(set(used)) == len(used)
    return rows_of, groups, wire_at, begins


def side_rows(geo, got, high):
    frames, M, wire_at = geo["frames"], geo["M"], arrange(geo)[2]
    lane = lanes_of(geo["Z"])
    first, masks = [], []
    for l in range(LEVELS):
        m, at = M >> (l + 1), frames[l + 1]
        begin = jnp.where(high, at + m - 1, at - H - 1)
        first.append(begin)
        masks.append((lane >= begin) & (lane < begin + SLOT))

    def row(l, i):
        t, s = place(geo, wire_at[l] + i)
        return jnp.where(masks[l], pltpu.roll(got[t], (first[l] + LANES - SLOT * s) % LANES, 1), 0.0)

    return row


def side_edge(geo, got, high, edge_taps, t):
    Z = geo["Z"]
    lane = lanes_of(Z) % (2 * H)
    inside = (lane < H) != high
    shift = jnp.where(high, 0 if t % 2 else H, LANES - H if t % 2 else 0)
    halo = jnp.where(inside, pltpu.roll(got[geo["coarse_tiles"] + t // 2], shift, 1), 0.0)
    total = jnp.zeros((Z, LANES), F32)
    for k in range(1, H + 1):
        total = total + edge_taps[k, pl.ds(t, 1), :] * pltpu.roll(halo, jnp.where(high, LANES - k, k), 1)
    return jnp.where(inside, 0.0, total)


def near_side(geo, *refs):
    joined, (got_x, got_d, edge_taps, ext, edge) = refs[:LEVELS], refs[LEVELS:]
    Z, M, bases, frames = geo["Z"], geo["M"], geo["bases"], geo["frames"]
    high = lax.axis_index("north") % 2 == 0
    lane = lanes_of(Z)
    rows_of, groups, _, begins = arrange(geo)
    extra = dict(forwarded(geo, got_d))
    side = side_rows(geo, got_x, high)

    def source_row(l, i):
        m, at = M >> (l + 1), frames[l + 1]
        own = joined[l][i]
        if l == LEVELS - 1 and i in extra:
            own = own + extra[i]
        own = roll(own, at - 1 - bases[l])
        return jnp.where((lane >= at - 1) & (lane < at + m + 1), own, 0.0) + side(l, i)

    for g in groups:
        for i in range(rows_of[g[0]] + 2 * H + 2):
            parts = [source_row(l, i) for l in g if i < rows_of[l] + 2 * H + 2]
            ext[begins(2 * H + 2)[g[0]] + i] = functools.reduce(jnp.add, parts)
    for t in range(geo["R"] // H):
        edge[t] = side_edge(geo, got_x, high, edge_taps, t)


def finish(geo, *refs):
    Z, R, M, bases, frames = geo["Z"], geo["R"], geo["M"], geo["bases"], geo["frames"]
    it = iter(refs)
    take = lambda count: [next(it) for _ in range(count)]
    mixed0, matrices, edge_taps = take(3)
    near, near_edge = take(2)
    wide, gain = take(LEVELS), take(LEVELS)
    got_x, got_y, gain0, table, shifts = take(5)
    (result_hbm,) = take(1)
    ext, passed, north, result, spread, wf, gf, cf, edge, out, sems = take(11)
    e, n = lax.axis_index("east"), lax.axis_index("north")
    has_low, has_high = e > 0, e < geo["E"] - 1
    north_even = n % 2 == 0
    lane = lanes_of(Z)
    lane8 = lanes_of(8)
    per = LANES // H
    base = geo["coarse_tiles"] + R // per
    rows_of, groups, _, begins = arrange(geo)
    ext_at, out_at, width_at = begins(2 * H + 2), begins(2), begins(2 * H)
    tile_x, tile_y = got_x[base], got_y[base]
    tile_low, tile_high = jnp.where(north_even, tile_y, tile_x), jnp.where(north_even, tile_x, tile_y)
    side = side_rows(geo, got_y, jnp.logical_not(north_even))

    def widths_chunk(l, c):
        r, m, at = rows_of[l], M >> (l + 1), frames[l + 1]
        row = c % Z
        begin = SLOT * (sum(-(-(q + 2 * H) // Z) for q in rows_of[:l]) + c // Z)
        lower, upper = tile_low[row : row + 8], tile_high[row : row + 8]
        width = jnp.where(
            lane8 < at,
            roll(lower, at - H - 1 - begin),
            jnp.where(lane8 < at + m, wide[l][pl.ds(c, 8), :], roll(upper, at + m - begin)),
        )
        width = jnp.where((lane8 >= at - H - 1) & (lane8 < at + m + H + 1), width, 0.0)
        weight = jnp.where(lane8 == at - 1, roll(lower, at - H - 2 - begin), gain[l][pl.ds(c, 8), :])
        return width, jnp.where(lane8 == at + m, roll(upper, at + m - H - 1 - begin), weight)

    for g in groups:
        r = rows_of[g[0]]
        for c in range(0, r + 2 * H, 8):
            parts = [widths_chunk(l, c) for l in g if c < rows_of[l] + 2 * H]
            wf[pl.ds(width_at[g[0]] + c, 8), :] = functools.reduce(jnp.add, [p[0] for p in parts])
            gf[pl.ds(width_at[g[0]] + c, 8), :] = functools.reduce(jnp.add, [p[1] for p in parts])
    for k, a in enumerate(taps(wf[...])):
        cf[k] = a
    for g in groups:
        r = rows_of[g[0]]
        for i in range(r + 2 * H + 2):
            parts = [side(l, i) for l in g if i < rows_of[l] + 2 * H + 2]
            ext[ext_at[g[0]] + i] = functools.reduce(jnp.add, parts, near[ext_at[g[0]] + i])
        for x in range(0, r + 2, 4):
            east_block(ext, cf, passed, x, min(4, r + 2 - x), width_at[g[0]] + H - 1, ext_at[g[0]], out_at[g[0]])

    total = rows_of[0] + rows_of[1] + 4

    def coarse_factor(k, x):
        l = 0 if x < out_at[1] else 1
        return cf[k, pl.ds(width_at[l] + H - 1 + x - out_at[l], 1), :]

    half = -(-total // 2)
    north_rows(passed, north, range(0, half), coarse_factor, shifts)
    north_rows(passed, north, range(half, total), coarse_factor, shifts)
    for l in range(LEVELS - 1, -1, -1):
        r, m, at = R >> (l + 1), M >> (l + 1), frames[l + 1]
        blocks = (r + 2 + 7) // 8
        matrix = [matrices[l + 1, 0], matrices[l + 1, 1]]
        for g in range(blocks):
            have = min(8, r + 2 - 8 * g)
            data = north[out_at[l] + 8 * g : out_at[l] + 8 * g + have].reshape(have * Z, LANES)
            if have < 8:
                data = jnp.concatenate([data, jnp.zeros(((8 - have) * Z, LANES), F32)], axis=0)
            mixed = mix(matrix, data)
            for i in range(have):
                row = 8 * g + i
                result[row] = gf[pl.ds(width_at[l] + row + H - 1, 1), :] * mixed[i * Z : (i + 1) * Z]
        if l < LEVELS - 1:
            inside = ((lane >= at) | (n > 0)) & ((lane < at + m) | (n < geo["N"] - 1))
            for row in range(-1, r + 1):
                j = row // 2
                other = j + (1 if row % 2 else -1)
                summed = result[row + 1] + 0.75 * spread[j + 1] + 0.25 * spread[other + 1]
                keep = inside
                if row == -1:
                    keep = keep & has_low
                if row == r:
                    keep = keep & has_high
                result[row + 1] = jnp.where(keep, summed, 0.0)
        flat = result.reshape(result.shape[0] * Z, LANES)
        spread_flat = spread.reshape(spread.shape[0] * Z, LANES)
        spread_flat[pl.ds(0, (r + 2) * Z), :] = dot_exact(flat[pl.ds(0, (r + 2) * Z), :], table[l])
    for t in range(R // H):
        edge[t] = near_edge[t] + side_edge(geo, got_y, jnp.logical_not(north_even), edge_taps, t)
    edge_flat = edge.reshape(edge.shape[0] * Z, LANES)
    used = pl.ds(0, R // H * Z)
    edge_flat[used, :] = mix([matrices[0, 0], matrices[0, 1]], edge_flat[used, :])
    widen = table[LEVELS][:, 0 : 6 * Z]
    at_edge = (lane8 < H) | (lane8 >= M - H)
    copies = []
    for b in range(R // 8):
        high, low = split(spread[4 * b : 4 * b + 6].reshape(6 * Z, LANES))
        added = mm(widen, high) + mm(widen, low)
        weight = gain0[pl.ds(8 * b, 8), :]
        for z in range(Z):
            row = edge_flat[pl.ds(b * Z + z, 8, stride=0), :]
            moved = pltpu.roll(row, H, 1, stride=2 * H, stride_axis=0)
            here = mixed0[b, z * 8 : z * 8 + 8, :] + jnp.where(at_edge, moved, 0.0)
            out[z, pl.ds(8 * b, 8), :] = weight * here + added[z * 8 : z * 8 + 8]
        if b % 2:
            part = pl.ds(8 * (b - 1), 16)
            copies.append(pltpu.make_async_copy(out.at[:, part, :], result_hbm.at[:, part, :], sems.at[b // 2]))
            copies[-1].start()
    for copy in copies:
        copy.wait()


def swap(x, axis, first):
    route = [(i, i + 1) for i in range(first, lax.axis_size(axis) - 1, 2)]
    return lax.ppermute(x, axis, route + [(j, i) for i, j in route])


def body(inc, w0, w1, w2, w3, g0, g1, g2, g3, vertical):
    Z, R, M = inc.shape
    bases, frames, down, up, shifts = tables(R, M)
    total_rows = sum((R >> l) + 2 * H + 2 for l in range(1, LEVELS + 1))
    width_slots = sum(-(-((R >> l) + 2 * H) // Z) for l in range(1, LEVELS + 1))
    geo = dict(
        Z=Z, R=R, M=M, bases=bases, frames=frames, E=lax.axis_size("east"), N=lax.axis_size("north"),
        coarse_tiles=-(-(total_rows - PER_TILE + width_slots) // PER_TILE), width_slots=width_slots,
    )
    shape = lambda *dims: jax.ShapeDtypeStruct(dims, F32)
    levels = range(1, LEVELS + 1)
    params = pltpu.CompilerParams(vmem_limit_bytes=48 * 1024 * 1024)
    east_tiles = H + SLOT + 1
    given = (inc, jnp.asarray(down))
    outs = pl.pallas_call(
        functools.partial(prepare, geo),
        out_shape=[shape(R, Z, M)] + [shape((R >> l) + 2, Z, M) for l in levels]
        + [shape(2, Z, M)],
        in_specs=[pl.BlockSpec(memory_space=pltpu.HBM)] * len(given),
        scratch_shapes=[pltpu.VMEM((R, Z, M), F32)] + [pltpu.VMEM(x.shape, x.dtype) for x in given]
        + [pltpu.SemaphoreType.DMA((len(given),))],
        compiler_params=params,
    )(*[pltpu.with_memory_space_constraint(x, pltpu.HBM) for x in given])
    field, coarse, send_far = outs[0], outs[1 : 1 + LEVELS], outs[1 + LEVELS]
    got_far = swap(send_far, "east", 0)
    send_a, send_b = pl.pallas_call(
        functools.partial(gather, geo),
        out_shape=[shape(east_tiles, Z, M), shape(east_tiles + 2, Z, M)],
        compiler_params=params,
    )(field, *coarse, got_far, w1, w2, w3, g1, g2, g3)
    got_b = swap(send_b, "east", 1)
    got_a = swap(send_a, "east", 0)
    factors, inner = pl.pallas_call(
        functools.partial(interior, geo),
        out_shape=[shape(H + 1, R, M), shape(R - 2 * H, Z, M)],
        compiler_params=params,
    )(field, w0)
    forward, inner, got_a = lax.optimization_barrier((got_b, inner, got_a))
    got_d = swap(forward, "east", 0)
    wide_shapes = [shape((R >> l) + 2 * H, M) for l in levels]
    north_tiles = geo["coarse_tiles"] + R * H // LANES + 1
    outs = pl.pallas_call(
        functools.partial(middle, geo),
        out_shape=[shape(R, Z, M)] + [shape((R >> l) + 2 * H + 2, Z, M) for l in levels]
        + [shape(north_tiles, Z, M)] * 2 + wide_shapes * 2,
        scratch_shapes=[pltpu.VMEM((3 * H, Z, M), F32)] * 2,
        compiler_params=params,
    )(field, *coarse, got_a, got_b, factors, inner, w1, w2, w3, g1, g2, g3)
    eastward = outs[0]
    joined, (send_x, send_y) = outs[1 : 1 + LEVELS], outs[1 + LEVELS : 3 + LEVELS]
    wide, gain = outs[3 + LEVELS : 3 + 2 * LEVELS], outs[3 + 2 * LEVELS :]
    send_x, send_y = pl.pallas_call(
        functools.partial(patch, geo), out_shape=[shape(north_tiles, Z, M)] * 2, compiler_params=params
    )(send_x, send_y, got_d)
    got_x = swap(send_x, "north", 0)
    got_y = swap(send_y, "north", 1)
    shifts = jnp.asarray(shifts)
    assert R // H == 8 and 8 * Z == LANES
    window = pl.pallas_call(
        functools.partial(own_north, geo),
        out_shape=[
            shape(R // 8, LANES, LANES), jax.ShapeDtypeStruct((LEVELS + 1, 2, LANES, LANES), BF16), shape(H + 1, 8, LANES)
        ],
        scratch_shapes=[pltpu.VMEM((R, Z, M), F32)],
        compiler_params=params,
    )(eastward, factors, shifts, w0, vertical)
    rows1 = (R >> 1) + 2
    out_rows = (R >> 1) + (R >> 2) + 4
    ext_rows, width_rows = out_rows + 4 * H, out_rows + 4 * H - 4
    near = pl.pallas_call(
        functools.partial(near_side, geo), out_shape=[shape(ext_rows, Z, M), shape(R // H, Z, M)], compiler_params=params
    )(*joined, got_x, got_d, window[2])
    return pl.pallas_call(
        functools.partial(finish, geo),
        out_shape=shape(Z, R, M),
        out_specs=pl.BlockSpec(memory_space=pltpu.HBM),
        scratch_shapes=[
            pltpu.VMEM(dims, F32)
            for dims in (
                (ext_rows, Z, M), (out_rows, Z, M), (out_rows, Z, M),
                (rows1, Z, M), (rows1, Z, M), (width_rows, M), (width_rows, M), (H + 1, width_rows, M),
                (R // H + 1, Z, M), (Z, R, M),
            )
        ] + [pltpu.SemaphoreType.DMA((R // 16,))],
        compiler_params=params,
    )(*window, *near, *wide, *gain, got_x, got_y, g0, jnp.asarray(up), shifts)


def solution(mesh):
    tile = P("east", "north")
    return jax.shard_map(
        body,
        mesh=mesh,
        in_specs=(P(None, "east", "north"), *([tile] * 8), P()),
        out_specs=P(None, "east", "north"),
        check_vma=False,
    )
```
